128 devices in a mesh: row: 8 (over z, x_hi), col: 16 (over x_lo, y, core).
Axes of the slice: x: 4 (x_hi: 2, x_lo: 2; x = x_hi * 2 + x_lo), y: 4, z: 4, core: 2. Of those that a mesh axis runs over, the one named last changes fastest.
Arguments:
- tile_blocks: bfloat16 [8, 16, 384, 128, 128], P('row', 'col'), may hold values from -0.109375 to 0.109375
- tile_rows: int32 [8, 16, 384], P('row', 'col'), may hold values from 0 to 127, as said below
- tile_cols: int32 [8, 16, 384], P('row', 'col'), may hold values from 0 to 63, as said below
- tile_count: int32 [8, 16], P('row', 'col'), may hold values from 48 to 384, as said below
- vectors: float32 [16, 131072], P(None, ('row', 'col')), may hold values from -8 to 8
- hvectors: float32 [16, 131072], P(None, ('row', 'col')), may hold values from -20 to 20
- previous: float32 [16, 131072], P(None, ('row', 'col')), may hold values from -6 to 6
- hprevious: float32 [16, 131072], P(None, ('row', 'col')), may hold values from -6 to 6
Outputs:
- orthonormal: float32 [48, 131072], P(None, ('row', 'col'))
- orthonormal_image: float32 [48, 131072], P(None, ('row', 'col'))
- projected: float32 [48, 48], replicated
The draws below stay inside these ranges and needn't reach their ends.
Inputs may be any that keep to these rules, and one draw needn't show every extreme that they name: `tile_rows`: both ends occur in every draw. `tile_cols`: both ends occur in every draw. `tile_count`: one process cell holds exactly 384 live slots in every draw; every other cell holds between 48 and 192.
All inputs are finite; a program needn't handle non-finite values.
Results may differ from the reference program's by a relative error of at most 0.0003.
Values sent between devices are 32-bit elements; how exact they have to be, the bound alone decides.
No kernel may reach another device: no remote copies, remote signals or barrier semaphores. Data moves between devices by JAX's collectives and lax.ppermute only.
A program may use at most 64 MiB of HBM per device.

```python
import math
import jax
import jax.numpy as jnp
from jax import lax

TILE = 128
K = 16
TILES_DEV = 384
GRID_ROWS = 8
GRID_COLS = 16
NROWS = 131072
BLOCKS_DEV = 8
ROW_BLOCKS = 128
COL_BLOCKS = 64
N_ROW = 8
N_COL = 16


def vector_pair(key):
    base_key = jax.random.fold_in(key, 23)
    first_key, ritz_key, random_key = jax.random.split(base_key, 3)
    vectors = jax.random.normal(first_key, (K, NROWS), jnp.float32)
    random_part = 0.7 * jax.random.normal(random_key, (K, NROWS), jnp.float32)
    ritz_scale = jax.random.uniform(ritz_key, (K, 1), jnp.float32, -1.5, 1.5)
    return (vectors, ritz_scale * vectors + random_part)


def draw_vectors(key, part):
    return vector_pair(key)[0]


def draw_hvectors(key, part):
    return vector_pair(key)[1]


def draw_tile_rows(key, part):
    values = jax.random.randint(jax.random.fold_in(key, 11), (GRID_ROWS, GRID_COLS, TILES_DEV), 0, ROW_BLOCKS, jnp.int32)
    return values.at[0, 0, 0].set(ROW_BLOCKS - 1).at[0, 0, 1].set(0)


def draw_tile_cols(key, part):
    values = jax.random.randint(jax.random.fold_in(key, 13), (GRID_ROWS, GRID_COLS, TILES_DEV), 0, COL_BLOCKS, jnp.int32)
    return values.at[0, 0, 0].set(COL_BLOCKS - 1).at[0, 0, 1].set(0)


def draw_tile_count(key, part):
    count_key, pick_key = jax.random.split(jax.random.fold_in(key, 17))
    cell_total = GRID_ROWS * GRID_COLS
    counts = jax.random.randint(count_key, (cell_total,), max(1, TILES_DEV // 8), TILES_DEV // 2 + 1, jnp.int32)
    chosen = jax.random.randint(pick_key, (), 0, cell_total, jnp.int32)
    counts = jnp.where(jnp.arange(cell_total, dtype=jnp.int32) == chosen, TILES_DEV, counts)
    return counts.reshape(GRID_ROWS, GRID_COLS)


def levels(key, extent, cuts, least, high):
    def one(dim, shards_of):
        steps = jax.random.uniform(jax.random.fold_in(jax.random.fold_in(key, 6), dim), (shards_of,), jnp.float32, least / len(cuts), high / len(cuts))
        return jnp.repeat(jnp.exp(steps), extent[dim] // shards_of).reshape((-1,) + (1,) * (len(extent) - dim - 1))

    gain = one(*cuts[0])
    for cut in cuts[1:]:
        gain = gain * one(*cut)
    return gain


def gaussian(rng, shape, deviation, most, shards=(), held_as=jnp.bfloat16):
    array = deviation * jax.random.normal(rng, shape, jnp.float32)
    if shards:
        array = array * levels(rng, shape, shards, -0.22, 0.18)
    return jnp.clip(array, -most, most).astype(held_as)


def setup_inputs(seed: int = 0) -> dict:
    seeds = jax.random.split(jax.random.key(seed), 9)
    return {
        "tile_blocks": gaussian(seeds[0], (GRID_ROWS, GRID_COLS, TILES_DEV, TILE, TILE), (TILE * max(1, TILES_DEV * N_ROW * N_COL * TILE // (2 * NROWS))) ** -0.5, 0.109375, ((0, 8), (1, 16))),
        "tile_rows": draw_tile_rows(jax.random.fold_in(seeds[8], 71), 0),
        "tile_cols": draw_tile_cols(jax.random.fold_in(seeds[8], 71), 0),
        "tile_count": draw_tile_count(jax.random.fold_in(seeds[8], 71), 0),
        "vectors": draw_vectors(jax.random.fold_in(seeds[8], 71), 0),
        "hvectors": draw_hvectors(jax.random.fold_in(seeds[8], 71), 0),
        "previous": gaussian(seeds[6], (K, NROWS), 1.0, 6.0, ((1, 128),), jnp.float32),
        "hprevious": gaussian(seeds[7], (K, NROWS), 1.0, 6.0, ((1, 128),), jnp.float32),
    }


EPSILON = 1e-06
HIGHEST_PRECISION = lax.Precision.HIGHEST

def dense_product(first, second):
    return jnp.dot(first.astype(jnp.float32), second.astype(jnp.float32), preferred_element_type=jnp.float32, precision=HIGHEST_PRECISION)

def reference(tile_blocks, tile_rows, tile_cols, tile_count, vectors, hvectors, previous, hprevious):
    members = vectors.shape[0]
    rayleigh_top = lax.optimization_barrier(jnp.sum(vectors * hvectors, axis=1))
    rayleigh_bottom = lax.optimization_barrier(jnp.sum(vectors * vectors, axis=1))
    ritz_values = rayleigh_top / (rayleigh_bottom + EPSILON)
    residual = hvectors - ritz_values[:, None] * vectors
    residual_blocks = residual.reshape(members, NROWS // TILE, TILE)
    cell_count = GRID_ROWS * GRID_COLS
    cell_index = jnp.arange(cell_count, dtype=jnp.int32)
    grid_row = cell_index // GRID_COLS
    grid_col = cell_index % GRID_COLS
    slot_index = jnp.arange(TILES_DEV, dtype=jnp.int32)

    def one_cell(totals, cell_item):
        tile_stack, row_ids, col_ids, live_count, row_cell, col_cell = cell_item
        global_rows = row_cell * ROW_BLOCKS + row_ids
        global_cols = (col_ids // BLOCKS_DEV * GRID_COLS + col_cell) * BLOCKS_DEV + col_ids % BLOCKS_DEV
        live_part = (slot_index < live_count)[None, :, None]
        dense_tiles = tile_stack.astype(jnp.float32)
        col_inputs = jnp.take(residual_blocks, global_cols, axis=1)
        row_inputs = jnp.take(residual_blocks, global_rows, axis=1)
        forward = jnp.einsum('tij,mtj->mti', dense_tiles, col_inputs, precision=HIGHEST_PRECISION)
        backward = jnp.einsum('tij,mti->mtj', dense_tiles, row_inputs, precision=HIGHEST_PRECISION)
        totals = totals.at[:, global_rows, :].add(jnp.where(live_part, forward, 0.0))
        totals = totals.at[:, global_cols, :].add(jnp.where(live_part, backward, 0.0))
        return (totals, None)
    initial = jnp.zeros((members, NROWS // TILE, TILE), jnp.float32)
    cell_items = (tile_blocks.reshape(cell_count, TILES_DEV, TILE, TILE), tile_rows.reshape(cell_count, TILES_DEV), tile_cols.reshape(cell_count, TILES_DEV), tile_count.reshape(cell_count), grid_row, grid_col)
    totals, unused = lax.scan(one_cell, initial, cell_items)
    residual_image = totals.reshape(members, NROWS)
    basis_rows = jnp.concatenate([vectors, residual, previous], axis=0)
    image_rows = jnp.concatenate([hvectors, residual_image, hprevious], axis=0)
    gram_matrix = dense_product(basis_rows, basis_rows.T)
    mixed_matrix = dense_product(basis_rows, image_rows.T)
    factor = jnp.linalg.cholesky(gram_matrix)
    row_scale = math.sqrt(NROWS)
    orthonormal = row_scale * lax.linalg.triangular_solve(factor, basis_rows, left_side=True, lower=True)
    orthonormal_image = row_scale * lax.linalg.triangular_solve(factor, image_rows, left_side=True, lower=True)
    half_done = lax.linalg.triangular_solve(factor, mixed_matrix, left_side=True, lower=True)
    projected = lax.linalg.triangular_solve(factor, half_done, left_side=False, lower=True, transpose_a=True)
    return (orthonormal, orthonormal_image, projected)
```

```python
import functools
import math

import jax
import jax.numpy as jnp
from jax import lax
from jax.experimental import pallas as pl
from jax.experimental.pallas import tpu as pltpu
from jax.sharding import PartitionSpec as P

EPSILON = 1e-06
HIGHEST_PRECISION = lax.Precision.HIGHEST
LANES = 128
VMEM_BYTES = 48 << 20
NT = (((1,), (1,)), ((), ()))
NN = (((1,), (0,)), ((), ()))


def exact_dot(first, second, dims):
    return lax.dot_general(
        first, second, dims, precision=HIGHEST_PRECISION, preferred_element_type=jnp.float32
    )


def call(kernel, out_shapes, name):
    return pl.pallas_call(
        kernel,
        out_shape=[jax.ShapeDtypeStruct(shape, jnp.float32) for shape in out_shapes],
        compiler_params=pltpu.CompilerParams(vmem_limit_bytes=VMEM_BYTES),
        name=name,
    )


def block(array, index):
    return array[:, index * LANES : (index + 1) * LANES]


def rayleigh_kernel(vectors_ref, hvectors_ref, slots_ref):
    vectors = vectors_ref[...]
    hvectors = hvectors_ref[...]
    members = vectors.shape[0]
    top = jnp.sum(vectors * hvectors, axis=1, keepdims=True)
    bottom = jnp.sum(vectors * vectors, axis=1, keepdims=True)
    lane = lax.broadcasted_iota(jnp.int32, (members, LANES), 1)
    line = lax.broadcasted_iota(jnp.int32, (members, LANES), 0)
    spread = jnp.where(lane == line, top, 0.0) + jnp.where(lane == line + members, bottom, 0.0)
    sums = jnp.sum(spread, axis=0, keepdims=True)
    slots_ref[...] = jnp.broadcast_to(sums, slots_ref.shape)


def residual_kernel(
    sums_ref, vectors_ref, hvectors_ref, previous_ref, hprevious_ref, residual_ref, slots_ref
):
    vectors = vectors_ref[...]
    hvectors = hvectors_ref[...]
    previous = previous_ref[...]
    hprevious = hprevious_ref[...]
    members = vectors.shape[0]
    sums = jnp.sum(sums_ref[...], axis=0, keepdims=True)
    lane = lax.broadcasted_iota(jnp.int32, (members, LANES), 1)
    line = lax.broadcasted_iota(jnp.int32, (members, LANES), 0)
    top = jnp.sum(jnp.where(lane == line, sums, 0.0), axis=1, keepdims=True)
    bottom = jnp.sum(jnp.where(lane == line + members, sums, 0.0), axis=1, keepdims=True)
    residual = hvectors - (top / (bottom + EPSILON)) * vectors
    residual_ref[...] = residual
    blocks = vectors.shape[1] // LANES
    for index in range(blocks):
        part = block(residual, index)
        for slot in range(slots_ref.shape[0]):
            slots_ref[slot, index] = part
    basis = jnp.concatenate([vectors, residual, previous], axis=0)
    gram = exact_dot(basis, basis, NT)
    early = exact_dot(jnp.concatenate([hvectors, hprevious], axis=0), basis, NT)
    pad = jnp.zeros((members, LANES - 3 * members), jnp.float32)
    extra = [
        gram[:members],
        gram[members : 2 * members],
        gram[2 * members :],
        early[:members],
        early[members:],
    ]
    for index, part in enumerate(pack_rows(extra, pad)):
        for slot in range(slots_ref.shape[0]):
            slots_ref[slot, blocks + index] = part


def pack_rows(parts, pad):
    members = pad.shape[0]
    first, second, third, fourth, fifth = parts
    pieces = [fifth[:, i * members : (i + 1) * members] for i in range(3)]
    zero = jnp.zeros((members, members), jnp.float32)
    return [
        jnp.concatenate([first, second, pieces[0], pieces[1]], axis=1),
        jnp.concatenate([third, fourth, pieces[2], zero], axis=1),
    ]


def unpack_rows(one, two, members):
    wide = 3 * members
    fifth = jnp.concatenate([one[:, 2 * wide :], two[:, 2 * wide : 2 * wide + members]], axis=1)
    return [one[:, :wide], one[:, wide : 2 * wide], two[:, :wide], two[:, wide : 2 * wide], fifth]


def relay_kernel(received_ref, residual_ref, slots_ref):
    residual = residual_ref[...]
    blocks = residual.shape[1] // LANES
    for index in range(blocks):
        part = block(residual, index)
        for slot in range(slots_ref.shape[0]):
            slots_ref[slot, index] = part
    for index in range(blocks, slots_ref.shape[1]):
        part = received_ref[0, index]
        for peer in range(1, received_ref.shape[0]):
            part = part + received_ref[peer, index]
        for slot in range(slots_ref.shape[0]):
            slots_ref[slot, index] = part


def factor_kernel(received_ref, inverse_ref, early_ref):
    extras = []
    for index in range(received_ref.shape[1] - 2, received_ref.shape[1]):
        part = received_ref[0, index]
        for peer in range(1, received_ref.shape[0]):
            part = part + received_ref[peer, index]
        extras.append(part)
    members = extras[0].shape[0]
    order = 3 * members
    first, second, third, fourth, fifth = unpack_rows(*extras, members)
    early_ref[...] = jnp.concatenate([fourth, fifth], axis=0)
    gram = jnp.concatenate([first, second, third], axis=0)
    line = lax.broadcasted_iota(jnp.int32, (order, order), 0)
    lane = lax.broadcasted_iota(jnp.int32, (order, order), 1)
    work = jnp.concatenate([gram, jnp.where(line == lane, 1.0, 0.0)], axis=1)
    rows = lax.broadcasted_iota(jnp.int32, (order, 1), 0)
    for step in range(order):
        pivot = work[step : step + 1, step : step + 1]
        scale = lax.rsqrt(pivot)
        scale = scale * (1.5 - 0.5 * pivot * scale * scale)
        lead = work[step : step + 1, :] * scale
        column = work[:, step : step + 1] * scale
        work = jnp.where(rows == step, lead, jnp.where(rows > step, work - column * lead, work))
    inverse_ref[...] = work[:, order:]


def orthonormal_kernel(inverse_ref, first_ref, second_ref, third_ref, out_ref, *, row_scale):
    rows = jnp.concatenate([first_ref[...], second_ref[...], third_ref[...]], axis=0)
    out_ref[...] = exact_dot(inverse_ref[...] * row_scale, rows, NN)


def image_kernel(
    row_parts_ref, col_parts_ref, vectors_ref, residual_ref, previous_ref, image_ref, slots_ref
):
    for index in range(row_parts_ref.shape[1]):
        part = row_parts_ref[0, index]
        for peer in range(1, row_parts_ref.shape[0]):
            part = part + row_parts_ref[peer, index]
        other = col_parts_ref[0, index]
        for peer in range(1, col_parts_ref.shape[0]):
            other = other + col_parts_ref[peer, index]
        image_ref[:, index * LANES : (index + 1) * LANES] = part + other
    basis = jnp.concatenate([vectors_ref[...], residual_ref[...], previous_ref[...]], axis=0)
    late = exact_dot(image_ref[...], basis, NT)
    half = late.shape[0] // 2
    pad = jnp.zeros((half, LANES // 2 - late.shape[1]), jnp.float32)
    packed = jnp.concatenate([late[:half], pad, late[half:], pad], axis=1)
    slots_ref[...] = jnp.broadcast_to(packed[None], slots_ref.shape)


def projected_kernel(received_ref, inverse_ref, early_ref, projected_ref):
    packed = jnp.sum(received_ref[...], axis=0)
    early = early_ref[...]
    members = early.shape[0] // 2
    wide = early.shape[1]
    half = LANES // 2
    late = jnp.concatenate([packed[:, :wide], packed[:, half : half + wide]], axis=0)
    mixed_t = jnp.concatenate([early[:members], late, early[members:]], axis=0)
    inverse = inverse_ref[...]
    half_done = exact_dot(inverse, mixed_t, NT)
    projected_ref[...] = exact_dot(half_done, inverse, NT)


def tile_kernel(
    count_ref, source_ref, target_ref, tiles_ref, x_ref, out_ref, split_ref, *, transpose, unroll
):
    step = pl.program_id(0)
    batch, _, _ = tiles_ref.shape
    live = count_ref[0, 0]
    start = step * batch
    members = x_ref.shape[2]

    @pl.when(step == 0)
    def _():
        out_ref[...] = jnp.zeros_like(out_ref)
        per_peer = split_ref.shape[0] // x_ref.shape[0]

        def split(peer, carry):
            for index in range(per_peer):
                value = x_ref[peer, index]
                high = value.astype(jnp.bfloat16)
                low = (value - high.astype(jnp.float32)).astype(jnp.bfloat16)
                split_ref[peer * per_peer + index] = jnp.concatenate([high, low], axis=0)
            return carry

        lax.fori_loop(0, x_ref.shape[0], split, 0)

    @pl.when(start < live)
    def _():
        def group(counter, carry):
            base = counter * unroll
            products = []
            for offset in range(unroll):
                slot = start + base + offset
                product = lax.dot_general(
                    split_ref[source_ref[0, 0, slot]],
                    tiles_ref[base + offset],
                    NT if transpose else NN,
                    preferred_element_type=jnp.float32,
                )
                product = product[:members] + product[members:]
                products.append(jnp.where(slot < live, product, 0.0))
            for offset in range(unroll):
                target = target_ref[0, 0, start + base + offset]
                out_ref[target] = out_ref[target] + products[offset]
            return carry

        groups = jnp.minimum((live - start + unroll - 1) // unroll, batch // unroll)
        lax.fori_loop(0, groups, group, 0)


def tile_products(count, source, target, tiles, received, sources, targets, transpose):
    slots = tiles.shape[0]
    batch = math.gcd(slots, 96)
    unroll = math.gcd(batch, 24)
    members = received.shape[2]
    return pl.pallas_call(
        functools.partial(tile_kernel, transpose=transpose, unroll=unroll),
        out_shape=jax.ShapeDtypeStruct((targets, members, LANES), jnp.float32),
        grid_spec=pltpu.PrefetchScalarGridSpec(
            num_scalar_prefetch=3,
            grid=(slots // batch,),
            in_specs=[
                pl.BlockSpec(
                    (batch,) + tiles.shape[1:],
                    lambda i, count, source, target: (
                        jnp.minimum(i, (count[0, 0] - 1) // batch),
                        0,
                        0,
                    ),
                ),
                pl.BlockSpec(
                    received.shape,
                    lambda i, count, source, target: (0, 0, 0, 0),
                    pipeline_mode=pl.Buffered(1),
                ),
            ],
            out_specs=pl.BlockSpec(
                (targets, members, LANES),
                lambda i, count, source, target: (0, 0, 0),
                pipeline_mode=pl.Buffered(1),
            ),
            scratch_shapes=[pltpu.VMEM((sources, 2 * members, LANES), jnp.bfloat16)],
        ),
        compiler_params=pltpu.CompilerParams(vmem_limit_bytes=VMEM_BYTES),
        name="forward_tiles" if transpose else "backward_tiles",
    )(count, source, target, tiles, received)


def exchange(slots, axes):
    return lax.all_to_all(slots, axes, 0, 0, tiled=True)


def on_device(
    tile_blocks, tile_rows, tile_cols, tile_count, vectors, hvectors, previous, hprevious
):
    n_row = lax.axis_size("row")
    n_col = lax.axis_size("col")
    everyone = ("row", "col")
    members, piece = vectors.shape
    blocks = piece // LANES
    order = 3 * members
    row_scale = math.sqrt(piece * n_row * n_col)
    tiles = tile_blocks[0, 0]

    (sums,) = call(rayleigh_kernel, [(n_row * n_col, LANES)], "rayleigh")(vectors, hvectors)
    sums = exchange(sums, everyone)
    slot = (blocks + 2, members, LANES)
    residual, slots = call(residual_kernel, [(members, piece), (n_row,) + slot], "residual")(
        sums, vectors, hvectors, previous, hprevious
    )
    col_range = exchange(slots, "row")
    (slots,) = call(relay_kernel, [(n_col,) + slot], "relay")(col_range, residual)
    row_range = exchange(slots, "col")
    row_totals = tile_products(
        tile_count, tile_cols, tile_rows, tiles, col_range, n_row * blocks, n_col * blocks, True
    )
    row_parts = exchange(row_totals.reshape(n_col, blocks, members, LANES), "col")
    col_totals = tile_products(
        tile_count, tile_rows, tile_cols, tiles, row_range, n_col * blocks, n_row * blocks, False
    )
    col_parts = exchange(col_totals.reshape(n_row, blocks, members, LANES), "row")
    inverse, early = call(factor_kernel, [(order, order), (2 * members, order)], "factor")(row_range)
    scaled = functools.partial(orthonormal_kernel, row_scale=row_scale)
    (orthonormal,) = call(scaled, [(order, piece)], "orthonormal")(
        inverse, vectors, residual, previous
    )
    image, slots = call(
        image_kernel, [(members, piece), (n_row * n_col, members // 2, LANES)], "image"
    )(row_parts, col_parts, vectors, residual, previous)
    late = exchange(slots, everyone)
    (orthonormal_image,) = call(scaled, [(order, piece)], "orthonormal_image")(
        inverse, hvectors, image, hprevious
    )
    (projected,) = call(projected_kernel, [(order, order)], "projected")(late, inverse, early)
    return (orthonormal, orthonormal_image, projected)


def solution(mesh):
    in_specs = (
        P("row", "col", None, None, None),
        P("row", "col", None),
        P("row", "col", None),
        P("row", "col"),
        P(None, ("row", "col")),
        P(None, ("row", "col")),
        P(None, ("row", "col")),
        P(None, ("row", "col")),
    )
    out_specs = (P(None, ("row", "col")), P(None, ("row", "col")), P())
    return jax.shard_map(
        on_device, mesh=mesh, in_specs=in_specs, out_specs=out_specs, check_vma=False
    )
```

```python
import functools
import math

import jax
import jax.numpy as jnp
from jax import lax
from jax.experimental import pallas as pl
from jax.experimental.pallas import tpu as pltpu
from jax.sharding import PartitionSpec as P

EPSILON = 1e-06
HIGHEST_PRECISION = lax.Precision.HIGHEST
LANES = 128
VMEM_BYTES = 48 << 20
NT = (((1,), (1,)), ((), ()))
NN = (((1,), (0,)), ((), ()))


def exact_dot(first, second, dims):
    return lax.dot_general(
        first, second, dims, precision=HIGHEST_PRECISION, preferred_element_type=jnp.float32
    )


def call(kernel, out_shapes, name):
    return pl.pallas_call(
        kernel,
        out_shape=[jax.ShapeDtypeStruct(shape, jnp.float32) for shape in out_shapes],
        compiler_params=pltpu.CompilerParams(vmem_limit_bytes=VMEM_BYTES),
        name=name,
    )


def block(array, index):
    return array[:, index * LANES : (index + 1) * LANES]


def here():
    row = lax.axis_index("row")
    col = lax.axis_index("col")
    return (lax.rem(row, 2), col // (lax.axis_size("col") // 2), lax.rem(col, 2))


def stage_kernel(
    rows_ref, vectors_hbm, hvectors_hbm, previous_hbm, slots_ref, stack_ref, rows_out_ref, arrived
):
    copies = [
        pltpu.make_async_copy(source, stack_ref.at[index], arrived.at[index])
        for index, source in enumerate((vectors_hbm, hvectors_hbm, previous_hbm))
    ]
    for copy in copies:
        copy.start()
    rows = rows_ref[...]
    core = lax.rem(lax.axis_index("col"), 2)
    lines = lax.axis_size("col") // 4
    blocks = stack_ref.shape[2] // LANES
    index, peer = rows % blocks, rows // blocks
    other = jnp.where(peer % 2 == core, 0, 1)
    line = (peer // 2) % lines
    half = peer // (2 * lines)
    rows_out_ref[...] = ((other * lines + line) * 2 + half) * blocks + index
    for copy in copies[:2]:
        copy.wait()
    vectors = stack_ref[0]
    hvectors = stack_ref[1]
    members = vectors.shape[0]
    top = jnp.sum(vectors * hvectors, axis=1, keepdims=True)
    bottom = jnp.sum(vectors * vectors, axis=1, keepdims=True)
    lane = lax.broadcasted_iota(jnp.int32, (members, LANES), 1)
    line = lax.broadcasted_iota(jnp.int32, (members, LANES), 0)
    spread = jnp.where(lane == line, top, 0.0) + jnp.where(lane == line + members, bottom, 0.0)
    sums = jnp.sum(spread, axis=0, keepdims=True)
    slots_ref[...] = jnp.broadcast_to(sums, slots_ref.shape)
    copies[2].wait()


def residual_kernel(
    sums_ref, stack_ref, lo_ref, hi_ref, hprevious_ref, residuals_ref, y_slots_ref, z_slots_ref
):
    x_hi, x_lo, _ = here()
    members = stack_ref.shape[1]
    sums = jnp.sum(sums_ref[...], axis=0, keepdims=True)
    lane = lax.broadcasted_iota(jnp.int32, (members, LANES), 1)
    line = lax.broadcasted_iota(jnp.int32, (members, LANES), 0)
    top = jnp.sum(jnp.where(lane == line, sums, 0.0), axis=1, keepdims=True)
    bottom = jnp.sum(jnp.where(lane == line + members, sums, 0.0), axis=1, keepdims=True)
    ritz_values = top / (bottom + EPSILON)
    residual = stack_ref[1] - ritz_values * stack_ref[0]
    lo_residual = lo_ref[1] - ritz_values * lo_ref[0]
    hi_residual = hi_ref[1] - ritz_values * hi_ref[0]
    residuals_ref[0] = residual
    residuals_ref[1] = lo_residual
    residuals_ref[2] = hi_residual
    blocks = residual.shape[1] // LANES
    for index in range(blocks):
        mine = block(residual, index)
        for slot in range(y_slots_ref.shape[0]):
            y_slots_ref[slot, x_lo * blocks + index] = mine
            y_slots_ref[slot, (1 - x_lo) * blocks + index] = block(lo_residual, index)
        for slot in range(z_slots_ref.shape[0]):
            z_slots_ref[slot, x_hi * blocks + index] = mine
            z_slots_ref[slot, (1 - x_hi) * blocks + index] = block(hi_residual, index)
    hvectors = stack_ref[1]
    basis = jnp.concatenate([stack_ref[0], residual, stack_ref[2]], axis=0)
    gram = exact_dot(basis, basis, NT)
    early = exact_dot(jnp.concatenate([hvectors, hprevious_ref[...]], axis=0), basis, NT)
    extra = [
        gram[:members],
        gram[members : 2 * members],
        gram[2 * members :],
        early[:members],
        early[members:],
    ]
    for index, part in enumerate(pack_rows(extra)):
        for slot in range(y_slots_ref.shape[0]):
            y_slots_ref[slot, 2 * blocks + index] = part


def pack_rows(parts):
    first, second, third, fourth, fifth = parts
    members = first.shape[0]
    pieces = [fifth[:, i * members : (i + 1) * members] for i in range(3)]
    zero = jnp.zeros((members, members), jnp.float32)
    return [
        jnp.concatenate([first, second, pieces[0], pieces[1]], axis=1),
        jnp.concatenate([third, fourth, pieces[2], zero], axis=1),
    ]


def unpack_rows(one, two):
    members = one.shape[0]
    wide = 3 * members
    fifth = jnp.concatenate([one[:, 2 * wide :], two[:, 2 * wide : 2 * wide + members]], axis=1)
    return [one[:, :wide], one[:, wide : 2 * wide], two[:, :wide], two[:, wide : 2 * wide], fifth]


def factor_kernel(sums_ref, far_ref, inverse_ref, early_ref):
    extras = [sums_ref[index] + far_ref[index] for index in range(2)]
    members = extras[0].shape[0]
    order = 3 * members
    first, second, third, fourth, fifth = unpack_rows(*extras)
    early_ref[...] = jnp.concatenate([fourth, fifth], axis=0)
    gram = jnp.concatenate([first, second, third], axis=0)
    line = lax.broadcasted_iota(jnp.int32, (order, order), 0)
    lane = lax.broadcasted_iota(jnp.int32, (order, order), 1)
    work = jnp.concatenate([gram, jnp.where(line == lane, 1.0, 0.0)], axis=1)
    rows = lax.broadcasted_iota(jnp.int32, (order, 1), 0)
    for step in range(order):
        pivot = work[step : step + 1, step : step + 1]
        scale = lax.rsqrt(pivot)
        scale = scale * (1.5 - 0.5 * pivot * scale * scale)
        lead = work[step : step + 1, :] * scale
        column = work[:, step : step + 1] * scale
        work = jnp.where(rows == step, lead, jnp.where(rows > step, work - column * lead, work))
    inverse_ref[...] = work[:, order:]


def orthonormal_kernel(inverse_ref, stack_ref, residuals_ref, out_ref, *, row_scale):
    rows = jnp.concatenate([stack_ref[0], residuals_ref[0], stack_ref[2]], axis=0)
    out_ref[...] = exact_dot(inverse_ref[...] * row_scale, rows, NN)


def orthonormal_image_kernel(
    inverse_ref, stack_ref, image_ref, lo_ref, hi_ref, hprevious_ref, out_ref, *, row_scale
):
    image = image_ref[...] + lo_ref[...] + hi_ref[...]
    rows = jnp.concatenate([stack_ref[1], image, hprevious_ref[...]], axis=0)
    out_ref[...] = exact_dot(inverse_ref[...] * row_scale, rows, NN)


def sum_peers(parts_ref, index):
    part = parts_ref[0, index]
    for peer in range(1, parts_ref.shape[0]):
        part = part + parts_ref[peer, index]
    return part


def image_kernel(
    y_parts_ref,
    z_parts_ref,
    stack_ref,
    lo_ref,
    hi_ref,
    residuals_ref,
    image_ref,
    to_lo_ref,
    to_hi_ref,
    slots_ref,
):
    x_hi, x_lo, _ = here()
    blocks = image_ref.shape[1] // LANES
    for index in range(blocks):
        lanes = slice(index * LANES, (index + 1) * LANES)
        image_ref[:, lanes] = sum_peers(y_parts_ref, x_lo * blocks + index) + sum_peers(
            z_parts_ref, x_hi * blocks + index
        )
        to_lo_ref[:, lanes] = sum_peers(y_parts_ref, (1 - x_lo) * blocks + index)
        to_hi_ref[:, lanes] = sum_peers(z_parts_ref, (1 - x_hi) * blocks + index)
    late = None
    for rows, parts, place in ((image_ref, stack_ref, 0), (to_lo_ref, lo_ref, 1), (to_hi_ref, hi_ref, 2)):
        basis = jnp.concatenate([parts[0], residuals_ref[place], parts[2]], axis=0)
        product = exact_dot(rows[...], basis, NT)
        late = product if late is None else late + product
    half = late.shape[0] // 2
    pad = jnp.zeros((half, LANES // 2 - late.shape[1]), jnp.float32)
    packed = jnp.concatenate([late[:half], pad, late[half:], pad], axis=1)
    slots_ref[...] = jnp.broadcast_to(packed[None], slots_ref.shape)


def projected_kernel(received_ref, inverse_ref, early_ref, projected_ref):
    packed = jnp.sum(received_ref[...], axis=0)
    early = early_ref[...]
    members = early.shape[0] // 2
    wide = early.shape[1]
    half = LANES // 2
    late = jnp.concatenate([packed[:, :wide], packed[:, half : half + wide]], axis=0)
    mixed_t = jnp.concatenate([early[:members], late, early[members:]], axis=0)
    inverse = inverse_ref[...]
    half_done = exact_dot(inverse, mixed_t, NT)
    projected_ref[...] = exact_dot(half_done, inverse, NT)


def split_blocks(x_ref, split_ref, start, per_peer):
    def split(peer, carry):
        for index in range(per_peer):
            value = x_ref[peer, index]
            high = value.astype(jnp.bfloat16)
            low = (value - high.astype(jnp.float32)).astype(jnp.bfloat16)
            split_ref[start + peer * per_peer + index] = jnp.concatenate([high, low], axis=0)
        return carry

    lax.fori_loop(0, x_ref.shape[0], split, 0)


def tile_groups(count_ref, tiles_ref, split_ref, out_ref, source_of, target_of, dims, unroll):
    batch = tiles_ref.shape[0]
    live = count_ref[0, 0]
    start = pl.program_id(0) * batch
    members = split_ref.shape[1] // 2

    @pl.when(start < live)
    def _():
        def group(counter, carry):
            base = counter * unroll
            products = []
            for offset in range(unroll):
                slot = start + base + offset
                product = lax.dot_general(
                    split_ref[source_of(slot)],
                    tiles_ref[base + offset],
                    dims,
                    preferred_element_type=jnp.float32,
                )
                product = product[:members] + product[members:]
                products.append(jnp.where(slot < live, product, 0.0))
            for offset in range(unroll):
                target = target_of(start + base + offset)
                out_ref[target] = out_ref[target] + products[offset]
            return carry

        groups = jnp.minimum((live - start + unroll - 1) // unroll, batch // unroll)
        lax.fori_loop(0, groups, group, 0)


def backward_kernel(
    count_ref, rows_ref, cols_ref, tiles_ref, own_ref, other_ref, out_ref, split_ref, *, unroll
):
    peers, width = own_ref.shape[:2]
    per_peer = split_ref.shape[0] // (2 * peers)

    @pl.when(pl.program_id(0) == 0)
    def _():
        out_ref[...] = jnp.zeros_like(out_ref)
        split_blocks(own_ref, split_ref, 0, per_peer)
        split_blocks(other_ref, split_ref, peers * per_peer, per_peer)
        for index in range(per_peer, width):
            part = sum_peers(own_ref, index) + sum_peers(other_ref, index)
            for start in range(0, out_ref.shape[0], width):
                out_ref[start + index] = part

    tile_groups(
        count_ref,
        tiles_ref,
        split_ref,
        out_ref,
        lambda slot: rows_ref[0, 0, slot],
        lambda slot: cols_ref[0, 0, slot] + (width - per_peer) * (cols_ref[0, 0, slot] // per_peer),
        NN,
        unroll,
    )


def forward_kernel(
    count_ref,
    rows_ref,
    cols_ref,
    tiles_ref,
    x_ref,
    own_ref,
    other_ref,
    split_ref,
    totals_ref,
    *,
    unroll,
):
    peers, width = x_ref.shape[:2]

    @pl.when(pl.program_id(0) == 0)
    def _():
        totals_ref[...] = jnp.zeros_like(totals_ref)
        split_blocks(x_ref, split_ref, 0, width)

    tile_groups(
        count_ref,
        tiles_ref,
        split_ref,
        totals_ref,
        lambda slot: cols_ref[0, 0, slot],
        lambda slot: rows_ref[0, 0, slot],
        NT,
        unroll,
    )

    @pl.when(pl.program_id(0) == pl.num_programs(0) - 1)
    def _():
        half = totals_ref.shape[0] // 2
        own_ref[...] = totals_ref[:half]
        other_ref[...] = totals_ref[half:]


def tile_call(kernel, count, rows, cols, tiles, arrays, out_shapes, scratch, name):
    slots = tiles.shape[0]
    batch = math.gcd(slots, 96)
    unroll = math.gcd(batch, 24)

    def whole(shape):
        return pl.BlockSpec(
            shape, lambda i, count, rows, cols: (0,) * len(shape), pipeline_mode=pl.Buffered(1)
        )

    def tile_index(i, count, rows, cols):
        return (jnp.minimum(i, (count[0, 0] - 1) // batch), 0, 0)

    return pl.pallas_call(
        functools.partial(kernel, unroll=unroll),
        out_shape=[jax.ShapeDtypeStruct(shape, jnp.float32) for shape in out_shapes],
        grid_spec=pltpu.PrefetchScalarGridSpec(
            num_scalar_prefetch=3,
            grid=(slots // batch,),
            in_specs=[pl.BlockSpec((batch,) + tiles.shape[1:], tile_index)]
            + [whole(array.shape) for array in arrays],
            out_specs=[whole(shape) for shape in out_shapes],
            scratch_shapes=scratch,
        ),
        compiler_params=pltpu.CompilerParams(vmem_limit_bytes=VMEM_BYTES),
        name=name,
    )(count, rows, cols, tiles, *arrays)


def exchange(slots, axes, groups=None):
    return lax.all_to_all(slots, axes, 0, 0, axis_index_groups=groups, tiled=True)


def swap(array, axis, distance):
    return lax.ppermute(array, axis, [(i, i ^ distance) for i in range(lax.axis_size(axis))])


def on_device(
    tile_blocks, tile_rows, tile_cols, tile_count, vectors, hvectors, previous, hprevious
):
    n_row = lax.axis_size("row")
    n_col = lax.axis_size("col")
    everyone = ("row", "col")
    y_lines = n_col // 4
    z_lines = n_row // 2
    y_groups = [[x * n_col // 2 + y * 2 + core for y in range(y_lines)] for x in (0, 1) for core in (0, 1)]
    z_groups = [[z * 2 + x for z in range(z_lines)] for x in (0, 1)]
    members, piece = vectors.shape
    blocks = piece // LANES
    order = 3 * members
    row_scale = math.sqrt(piece * n_row * n_col)
    tiles = tile_blocks[0, 0]
    f32 = jnp.float32

    any_spec = pl.BlockSpec(memory_space=pl.ANY)
    vmem_spec = pl.BlockSpec(memory_space=pltpu.VMEM)
    sums, stack, rows = pl.pallas_call(
        stage_kernel,
        out_shape=[
            jax.ShapeDtypeStruct((n_row * n_col, LANES), f32),
            jax.ShapeDtypeStruct((3, members, piece), f32),
            jax.ShapeDtypeStruct(tile_rows.shape, jnp.int32),
        ],
        in_specs=[vmem_spec, any_spec, any_spec, any_spec],
        out_specs=[vmem_spec] * 3,
        scratch_shapes=[pltpu.SemaphoreType.DMA((3,))],
        name="stage",
    )(tile_rows, vectors, hvectors, previous)
    lo_stack = swap(stack, "col", n_col // 2)
    hi_stack = swap(stack, "row", 1)
    sums = exchange(sums, everyone)
    pair = 2 * blocks
    residuals, y_slots, z_slots = call(
        residual_kernel,
        [
            (3, members, piece),
            (y_lines, pair + 2, members, LANES),
            (z_lines, pair, members, LANES),
        ],
        "residual",
    )(sums, stack, lo_stack, hi_stack, hprevious)
    own_range = exchange(y_slots, "col", y_groups)
    other_range = swap(own_range, "col", 1)
    col_range = exchange(z_slots, "row", z_groups)
    (col_totals,) = tile_call(
        backward_kernel,
        tile_count,
        rows,
        tile_cols,
        tiles,
        (own_range, other_range),
        [(z_lines * (pair + 2), members, LANES)],
        [pltpu.VMEM((2 * y_lines * pair, 2 * members, LANES), jnp.bfloat16)],
        "backward_tiles",
    )
    z_parts = exchange(col_totals.reshape(z_lines, pair + 2, members, LANES), "row", z_groups)
    half = (y_lines * pair, members, LANES)
    own_totals, other_totals = tile_call(
        forward_kernel,
        tile_count,
        rows,
        tile_cols,
        tiles,
        (col_range,),
        [half, half],
        [
            pltpu.VMEM((z_lines * pair, 2 * members, LANES), jnp.bfloat16),
            pltpu.VMEM((2 * y_lines * pair, members, LANES), f32),
        ],
        "forward_tiles",
    )
    totals = own_totals + swap(other_totals, "col", 1)
    y_parts = exchange(totals.reshape(y_lines, pair, members, LANES), "col", y_groups)
    gram_sums = jnp.sum(z_parts[:, pair:], axis=0)
    gram_sums = gram_sums + swap(gram_sums, "col", n_col // 2)
    gram_far = swap(gram_sums, "row", 1)
    image, to_lo, to_hi, slots = call(
        image_kernel,
        [(members, piece)] * 3 + [(n_row * n_col, members // 2, LANES)],
        "image",
    )(y_parts, z_parts, stack, lo_stack, hi_stack, residuals)
    late = exchange(slots, everyone)
    from_lo = swap(to_lo, "col", n_col // 2)
    from_hi = swap(to_hi, "row", 1)
    inverse, early = call(factor_kernel, [(order, order), (2 * members, order)], "factor")(
        gram_sums, gram_far
    )
    (orthonormal,) = call(
        functools.partial(orthonormal_kernel, row_scale=row_scale), [(order, piece)], "orthonormal"
    )(inverse, stack, residuals)
    (orthonormal_image,) = call(
        functools.partial(orthonormal_image_kernel, row_scale=row_scale),
        [(order, piece)],
        "orthonormal_image",
    )(inverse, stack, image, from_lo, from_hi, hprevious)
    (projected,) = call(projected_kernel, [(order, order)], "projected")(late, inverse, early)
    return (orthonormal, orthonormal_image, projected)


def solution(mesh):
    in_specs = (
        P("row", "col", None, None, None),
        P("row", "col", None),
        P("row", "col", None),
        P("row", "col"),
        P(None, ("row", "col")),
        P(None, ("row", "col")),
        P(None, ("row", "col")),
        P(None, ("row", "col")),
    )
    out_specs = (P(None, ("row", "col")), P(None, ("row", "col")), P())
    return jax.shard_map(
        on_device, mesh=mesh, in_specs=in_specs, out_specs=out_specs, check_vma=False
    )
```

```python
import functools
import math

import jax
import jax.numpy as jnp
from jax import lax
from jax.experimental import pallas as pl
from jax.experimental.pallas import tpu as pltpu
from jax.sharding import PartitionSpec as P

EPSILON = 1e-06
HIGHEST_PRECISION = lax.Precision.HIGHEST
LANES = 128
VMEM_BYTES = 48 << 20
STAGE_BYTES = 60 << 20
NT = (((1,), (1,)), ((), ()))
NN = (((1,), (0,)), ((), ()))


def exact_dot(first, second, dims):
    return lax.dot_general(
        first, second, dims, precision=HIGHEST_PRECISION, preferred_element_type=jnp.float32
    )


def call(kernel, out_shapes, name):
    return pl.pallas_call(
        kernel,
        out_shape=[jax.ShapeDtypeStruct(shape, jnp.float32) for shape in out_shapes],
        compiler_params=pltpu.CompilerParams(vmem_limit_bytes=VMEM_BYTES),
        name=name,
    )


def block(array, index):
    return array[:, index * LANES : (index + 1) * LANES]


def stage_kernel(vectors_hbm, hvectors_hbm, slots_ref, stack_ref, arrived):
    copies = [
        pltpu.make_async_copy(source, stack_ref.at[index], arrived.at[index])
        for index, source in enumerate((vectors_hbm, hvectors_hbm))
    ]
    for copy in copies:
        copy.start()
    for copy in copies:
        copy.wait()
    vectors = stack_ref[0]
    hvectors = stack_ref[1]
    members = vectors.shape[0]
    top = jnp.sum(vectors * hvectors, axis=1, keepdims=True)
    bottom = jnp.sum(vectors * vectors, axis=1, keepdims=True)
    lane = lax.broadcasted_iota(jnp.int32, (members, LANES), 1)
    line = lax.broadcasted_iota(jnp.int32, (members, LANES), 0)
    spread = jnp.where(lane == line, top, 0.0) + jnp.where(lane == line + members, bottom, 0.0)
    sums = jnp.sum(spread, axis=0, keepdims=True)
    slots_ref[...] = jnp.broadcast_to(sums, slots_ref.shape)


def prepare_kernel(
    rows_ref,
    stack_hbm,
    previous_hbm,
    hprevious_hbm,
    rows_out_ref,
    stack_ref,
    previous_ref,
    hprevious_ref,
    arrived,
):
    copies = [
        pltpu.make_async_copy(source, target, arrived.at[index])
        for index, (source, target) in enumerate(
            (
                (stack_hbm, stack_ref),
                (previous_hbm, previous_ref),
                (hprevious_hbm, hprevious_ref),
            )
        )
    ]
    for copy in copies:
        copy.start()
    rows = rows_ref[...]
    core = lax.rem(lax.axis_index("col"), 2)
    chips = lax.axis_size("col") // 2
    blocks = previous_ref.shape[1] // LANES
    index, peer = rows % blocks, rows // blocks
    other = jnp.where(peer % 2 == core, 0, 1)
    rows_out_ref[...] = (other * chips + peer // 2) * blocks + index
    for copy in copies:
        copy.wait()


def residual_kernel(
    sums_ref,
    stack_ref,
    previous_ref,
    hprevious_ref,
    far_hbm,
    residuals_ref,
    col_slots_ref,
    row_slots_ref,
    far_ref,
    arrived,
):
    fetch = pltpu.make_async_copy(far_hbm, far_ref, arrived)
    fetch.start()
    x_hi = lax.rem(lax.axis_index("row"), 2)
    members = stack_ref.shape[1]
    sums = jnp.sum(sums_ref[...], axis=0, keepdims=True)
    lane = lax.broadcasted_iota(jnp.int32, (members, LANES), 1)
    line = lax.broadcasted_iota(jnp.int32, (members, LANES), 0)
    top = jnp.sum(jnp.where(lane == line, sums, 0.0), axis=1, keepdims=True)
    bottom = jnp.sum(jnp.where(lane == line + members, sums, 0.0), axis=1, keepdims=True)
    ritz_values = top / (bottom + EPSILON)
    hvectors = stack_ref[1]
    residual = hvectors - ritz_values * stack_ref[0]
    residuals_ref[0] = residual
    blocks = residual.shape[1] // LANES
    for index in range(blocks):
        mine = block(residual, index)
        for slot in range(col_slots_ref.shape[0]):
            col_slots_ref[slot, index] = mine
        for slot in range(row_slots_ref.shape[0]):
            row_slots_ref[slot, x_hi * blocks + index] = mine
    basis = jnp.concatenate([stack_ref[0], residual, previous_ref[...]], axis=0)
    gram = exact_dot(basis, basis, NT)
    early = exact_dot(jnp.concatenate([hvectors, hprevious_ref[...]], axis=0), basis, NT)
    extra = [
        gram[:members],
        gram[members : 2 * members],
        gram[2 * members :],
        early[:members],
        early[members:],
    ]
    for index, part in enumerate(pack_rows(extra)):
        for slot in range(col_slots_ref.shape[0]):
            col_slots_ref[slot, blocks + index] = part
    fetch.wait()
    far_residual = far_ref[1] - ritz_values * far_ref[0]
    residuals_ref[1] = far_residual
    for index in range(blocks):
        for slot in range(row_slots_ref.shape[0]):
            row_slots_ref[slot, (1 - x_hi) * blocks + index] = block(far_residual, index)


def pack_rows(parts):
    first, second, third, fourth, fifth = parts
    members = first.shape[0]
    pieces = [fifth[:, i * members : (i + 1) * members] for i in range(3)]
    zero = jnp.zeros((members, members), jnp.float32)
    return [
        jnp.concatenate([first, second, pieces[0], pieces[1]], axis=1),
        jnp.concatenate([third, fourth, pieces[2], zero], axis=1),
    ]


def unpack_rows(one, two):
    members = one.shape[0]
    wide = 3 * members
    fifth = jnp.concatenate([one[:, 2 * wide :], two[:, 2 * wide : 2 * wide + members]], axis=1)
    return [one[:, :wide], one[:, wide : 2 * wide], two[:, :wide], two[:, wide : 2 * wide], fifth]


def factor_kernel(sums_ref, far_ref, inverse_ref, early_ref):
    extras = [sums_ref[index] + far_ref[index] for index in range(2)]
    members = extras[0].shape[0]
    order = 3 * members
    first, second, third, fourth, fifth = unpack_rows(*extras)
    early_ref[...] = jnp.concatenate([fourth, fifth], axis=0)
    gram = jnp.concatenate([first, second, third], axis=0)
    line = lax.broadcasted_iota(jnp.int32, (order, order), 0)
    lane = lax.broadcasted_iota(jnp.int32, (order, order), 1)
    work = jnp.concatenate([gram, jnp.where(line == lane, 1.0, 0.0)], axis=1)
    rows = lax.broadcasted_iota(jnp.int32, (order, 1), 0)
    for step in range(order):
        pivot = work[step : step + 1, step : step + 1]
        scale = lax.rsqrt(pivot)
        scale = scale * (1.5 - 0.5 * pivot * scale * scale)
        lead = work[step : step + 1, :] * scale
        column = work[:, step : step + 1] * scale
        work = jnp.where(rows == step, lead, jnp.where(rows > step, work - column * lead, work))
    inverse_ref[...] = work[:, order:]


def orthonormal_kernel(
    inverse_ref, stack_ref, residuals_ref, previous_ref, out_ref, *, row_scale
):
    rows = jnp.concatenate([stack_ref[0], residuals_ref[0], previous_ref[...]], axis=0)
    out_ref[...] = exact_dot(inverse_ref[...] * row_scale, rows, NN)


def orthonormal_image_kernel(
    inverse_ref, stack_ref, image_ref, far_ref, hprevious_ref, out_ref, *, row_scale
):
    image = image_ref[...] + far_ref[...]
    rows = jnp.concatenate([stack_ref[1], image, hprevious_ref[...]], axis=0)
    out_ref[...] = exact_dot(inverse_ref[...] * row_scale, rows, NN)


def sum_peers(parts_ref, index):
    part = parts_ref[0, index]
    for peer in range(1, parts_ref.shape[0]):
        part = part + parts_ref[peer, index]
    return part


def image_kernel(
    col_parts_ref,
    row_parts_ref,
    stack_ref,
    previous_ref,
    far_ref,
    far_previous_ref,
    residuals_ref,
    image_ref,
    to_far_ref,
    slots_ref,
):
    x_hi = lax.rem(lax.axis_index("row"), 2)
    blocks = image_ref.shape[1] // LANES
    for index in range(blocks):
        lanes = slice(index * LANES, (index + 1) * LANES)
        image_ref[:, lanes] = sum_peers(col_parts_ref, index) + sum_peers(
            row_parts_ref, x_hi * blocks + index
        )
        to_far_ref[:, lanes] = sum_peers(row_parts_ref, (1 - x_hi) * blocks + index)
    basis = jnp.concatenate([stack_ref[0], residuals_ref[0], previous_ref[...]], axis=0)
    late = exact_dot(image_ref[...], basis, NT)
    basis = jnp.concatenate([far_ref[0], residuals_ref[1], far_previous_ref[...]], axis=0)
    late = late + exact_dot(to_far_ref[...], basis, NT)
    half = late.shape[0] // 2
    pad = jnp.zeros((half, LANES // 2 - late.shape[1]), jnp.float32)
    packed = jnp.concatenate([late[:half], pad, late[half:], pad], axis=1)
    slots_ref[...] = jnp.broadcast_to(packed[None], slots_ref.shape)


def projected_kernel(received_ref, inverse_ref, early_ref, projected_ref):
    packed = jnp.sum(received_ref[...], axis=0)
    early = early_ref[...]
    members = early.shape[0] // 2
    wide = early.shape[1]
    half = LANES // 2
    late = jnp.concatenate([packed[:, :wide], packed[:, half : half + wide]], axis=0)
    mixed_t = jnp.concatenate([early[:members], late, early[members:]], axis=0)
    inverse = inverse_ref[...]
    half_done = exact_dot(inverse, mixed_t, NT)
    projected_ref[...] = exact_dot(half_done, inverse, NT)


def split_blocks(x_ref, split_ref, start, per_peer):
    def split(peer, carry):
        for index in range(per_peer):
            value = x_ref[peer, index]
            high = value.astype(jnp.bfloat16)
            low = (value - high.astype(jnp.float32)).astype(jnp.bfloat16)
            split_ref[start + peer * per_peer + index] = jnp.concatenate([high, low], axis=0)
        return carry

    lax.fori_loop(0, x_ref.shape[0], split, 0)


def tile_groups(count_ref, tiles_ref, split_ref, out_ref, source_of, target_of, dims, unroll):
    batch = tiles_ref.shape[0]
    live = count_ref[0, 0]
    start = pl.program_id(0) * batch
    members = split_ref.shape[1] // 2

    @pl.when(start < live)
    def _():
        def group(counter, carry):
            base = counter * unroll
            products = []
            for offset in range(unroll):
                slot = start + base + offset
                product = lax.dot_general(
                    split_ref[source_of(slot)],
                    tiles_ref[base + offset],
                    dims,
                    preferred_element_type=jnp.float32,
                )
                product = product[:members] + product[members:]
                products.append(jnp.where(slot < live, product, 0.0))
            for offset in range(unroll):
                target = target_of(start + base + offset)
                out_ref[target] = out_ref[target] + products[offset]
            return carry

        groups = jnp.minimum((live - start + unroll - 1) // unroll, batch // unroll)
        lax.fori_loop(0, groups, group, 0)


def backward_kernel(
    count_ref, rows_ref, cols_ref, tiles_ref, own_ref, other_ref, out_ref, split_ref, *, unroll
):
    peers, width = own_ref.shape[:2]
    per_peer = split_ref.shape[0] // (2 * peers)
    extra = width - per_peer
    pair = 2 * per_peer

    @pl.when(pl.program_id(0) == 0)
    def _():
        out_ref[...] = jnp.zeros_like(out_ref)
        split_blocks(own_ref, split_ref, 0, per_peer)
        split_blocks(other_ref, split_ref, peers * per_peer, per_peer)
        for index in range(extra):
            part = sum_peers(own_ref, per_peer + index) + sum_peers(other_ref, per_peer + index)
            for start in range(pair, out_ref.shape[0], pair + extra):
                out_ref[start + index] = part

    tile_groups(
        count_ref,
        tiles_ref,
        split_ref,
        out_ref,
        lambda slot: rows_ref[0, 0, slot],
        lambda slot: cols_ref[0, 0, slot] + extra * (cols_ref[0, 0, slot] // pair),
        NN,
        unroll,
    )


def forward_kernel(
    count_ref,
    rows_ref,
    cols_ref,
    tiles_ref,
    x_ref,
    own_ref,
    other_ref,
    split_ref,
    totals_ref,
    *,
    unroll,
):
    peers, width = x_ref.shape[:2]

    @pl.when(pl.program_id(0) == 0)
    def _():
        totals_ref[...] = jnp.zeros_like(totals_ref)
        split_blocks(x_ref, split_ref, 0, width)

    tile_groups(
        count_ref,
        tiles_ref,
        split_ref,
        totals_ref,
        lambda slot: cols_ref[0, 0, slot],
        lambda slot: rows_ref[0, 0, slot],
        NT,
        unroll,
    )

    @pl.when(pl.program_id(0) == pl.num_programs(0) - 1)
    def _():
        half = totals_ref.shape[0] // 2
        own_ref[...] = totals_ref[:half]
        other_ref[...] = totals_ref[half:]


def tile_call(kernel, count, rows, cols, tiles, arrays, out_shapes, scratch, name):
    slots = tiles.shape[0]
    batch = math.gcd(slots, 96)
    unroll = math.gcd(batch, 24)

    def whole(shape):
        return pl.BlockSpec(
            shape, lambda i, count, rows, cols: (0,) * len(shape), pipeline_mode=pl.Buffered(1)
        )

    def tile_index(i, count, rows, cols):
        return (jnp.minimum(i, (count[0, 0] - 1) // batch), 0, 0)

    return pl.pallas_call(
        functools.partial(kernel, unroll=unroll),
        out_shape=[jax.ShapeDtypeStruct(shape, jnp.float32) for shape in out_shapes],
        grid_spec=pltpu.PrefetchScalarGridSpec(
            num_scalar_prefetch=3,
            grid=(slots // batch,),
            in_specs=[pl.BlockSpec((batch,) + tiles.shape[1:], tile_index)]
            + [whole(array.shape) for array in arrays],
            out_specs=[whole(shape) for shape in out_shapes],
            scratch_shapes=scratch,
        ),
        compiler_params=pltpu.CompilerParams(vmem_limit_bytes=VMEM_BYTES),
        name=name,
    )(count, rows, cols, tiles, *arrays)


def exchange(slots, axes, groups=None):
    return lax.all_to_all(slots, axes, 0, 0, axis_index_groups=groups, tiled=True)


def swap(array, axis, distance):
    return lax.ppermute(array, axis, [(i, i ^ distance) for i in range(lax.axis_size(axis))])


def on_device(
    tile_blocks, tile_rows, tile_cols, tile_count, vectors, hvectors, previous, hprevious
):
    n_row = lax.axis_size("row")
    n_col = lax.axis_size("col")
    everyone = ("row", "col")
    chips = n_col // 2
    lines = n_row // 2
    core_groups = [[2 * chip + core for chip in range(chips)] for core in (0, 1)]
    z_groups = [[2 * line + x for line in range(lines)] for x in (0, 1)]
    members, piece = vectors.shape
    blocks = piece // LANES
    pair = 2 * blocks
    order = 3 * members
    row_scale = math.sqrt(piece * n_row * n_col)
    tiles = tile_blocks[0, 0]
    f32 = jnp.float32

    hbm_spec = pl.BlockSpec(memory_space=pl.ANY)
    vmem_spec = pl.BlockSpec(memory_space=pltpu.VMEM)
    params = pltpu.CompilerParams(vmem_limit_bytes=VMEM_BYTES)
    sums, stack = pl.pallas_call(
        stage_kernel,
        out_shape=[
            jax.ShapeDtypeStruct((n_row * n_col, LANES), f32),
            jax.ShapeDtypeStruct((2, members, piece), f32),
        ],
        in_specs=[hbm_spec, hbm_spec],
        out_specs=[vmem_spec] * 2,
        scratch_shapes=[pltpu.SemaphoreType.DMA((2,))],
        compiler_params=pltpu.CompilerParams(vmem_limit_bytes=STAGE_BYTES),
        name="stage",
    )(vectors, hvectors)
    far_stack = swap(stack, "row", 1)
    rows, stack, previous, hprevious = pl.pallas_call(
        prepare_kernel,
        out_shape=[
            jax.ShapeDtypeStruct(tile_rows.shape, jnp.int32),
            jax.ShapeDtypeStruct(stack.shape, f32),
            jax.ShapeDtypeStruct(previous.shape, f32),
            jax.ShapeDtypeStruct(hprevious.shape, f32),
        ],
        in_specs=[vmem_spec, hbm_spec, hbm_spec, hbm_spec],
        out_specs=[vmem_spec] * 4,
        scratch_shapes=[pltpu.SemaphoreType.DMA((3,))],
        compiler_params=params,
        name="prepare",
    )(tile_rows, stack, previous, hprevious)
    sums = exchange(sums, everyone)
    sums, rows, stack, previous, hprevious = lax.optimization_barrier(
        (sums, rows, stack, previous, hprevious)
    )
    far_previous = swap(previous, "row", 1)
    residuals, col_slots, row_slots, far_stack = pl.pallas_call(
        residual_kernel,
        out_shape=[
            jax.ShapeDtypeStruct(shape, f32)
            for shape in (
                (2, members, piece),
                (chips, blocks + 2, members, LANES),
                (lines, pair, members, LANES),
                (2, members, piece),
            )
        ],
        in_specs=[vmem_spec] * 4 + [hbm_spec],
        out_specs=[vmem_spec] * 4,
        scratch_shapes=[pltpu.SemaphoreType.DMA(())],
        compiler_params=params,
        name="residual",
    )(sums, stack, previous, hprevious, far_stack)
    own_range = exchange(col_slots, "col", core_groups)
    own_range, row_slots = lax.optimization_barrier((own_range, row_slots))
    other_range = swap(own_range, "col", 1)
    col_range = exchange(row_slots, "row", z_groups)
    (col_totals,) = tile_call(
        backward_kernel,
        tile_count,
        rows,
        tile_cols,
        tiles,
        (own_range, other_range),
        [(lines * (pair + 2), members, LANES)],
        [pltpu.VMEM((n_col * blocks, 2 * members, LANES), jnp.bfloat16)],
        "backward_tiles",
    )
    col_totals, col_range = lax.optimization_barrier((col_totals, col_range))
    row_parts = exchange(col_totals.reshape(lines, pair + 2, members, LANES), "row", z_groups)
    half = (chips * blocks, members, LANES)
    own_totals, other_totals = tile_call(
        forward_kernel,
        tile_count,
        rows,
        tile_cols,
        tiles,
        (col_range,),
        [half, half],
        [
            pltpu.VMEM((lines * pair, 2 * members, LANES), jnp.bfloat16),
            pltpu.VMEM((n_col * blocks, members, LANES), f32),
        ],
        "forward_tiles",
    )
    row_parts, own_totals, other_totals = lax.optimization_barrier(
        (row_parts, own_totals, other_totals)
    )
    totals = own_totals + swap(other_totals, "col", 1)
    col_parts = exchange(totals.reshape(chips, blocks, members, LANES), "col", core_groups)
    gram_sums = jnp.sum(row_parts[:, pair:], axis=0)
    gram_far = swap(gram_sums, "row", 1)
    inverse, early = call(factor_kernel, [(order, order), (2 * members, order)], "factor")(
        gram_sums, gram_far
    )
    (orthonormal,) = call(
        functools.partial(orthonormal_kernel, row_scale=row_scale), [(order, piece)], "orthonormal"
    )(inverse, stack, residuals, previous)
    col_parts, inverse, orthonormal = lax.optimization_barrier((col_parts, inverse, orthonormal))
    image, to_far, slots = call(
        image_kernel,
        [(members, piece)] * 2 + [(n_row * n_col, members // 2, LANES)],
        "image",
    )(col_parts, row_parts, stack, previous, far_stack, far_previous, residuals)
    late = exchange(slots, everyone)
    from_far = swap(to_far, "row", 1)
    (orthonormal_image,) = call(
        functools.partial(orthonormal_image_kernel, row_scale=row_scale),
        [(order, piece)],
        "orthonormal_image",
    )(inverse, stack, image, from_far, hprevious)
    (projected,) = call(projected_kernel, [(order, order)], "projected")(late, inverse, early)
    return (orthonormal, orthonormal_image, projected)


def solution(mesh):
    in_specs = (
        P("row", "col", None, None, None),
        P("row", "col", None),
        P("row", "col", None),
        P("row", "col"),
        P(None, ("row", "col")),
        P(None, ("row", "col")),
        P(None, ("row", "col")),
        P(None, ("row", "col")),
    )
    out_specs = (P(None, ("row", "col")), P(None, ("row", "col")), P())
    return jax.shard_map(
        on_device, mesh=mesh, in_specs=in_specs, out_specs=out_specs, check_vma=False
    )
```

```python
import functools
import math

import jax
import jax.numpy as jnp
from jax import lax
from jax.experimental import pallas as pl
from jax.experimental.pallas import tpu as pltpu
from jax.sharding import PartitionSpec as P

EPSILON = 1e-06
HIGHEST_PRECISION = lax.Precision.HIGHEST
LANES = 128
VMEM_BYTES = 32 << 20
FULL_VMEM_BYTES = 60 << 20
NT = (((1,), (1,)), ((), ()))
NN = (((1,), (0,)), ((), ()))


def exact_dot(first, second, dims):
    return lax.dot_general(
        first, second, dims, precision=HIGHEST_PRECISION, preferred_element_type=jnp.float32
    )


def call(kernel, out_shapes, name):
    return pl.pallas_call(
        kernel,
        out_shape=[jax.ShapeDtypeStruct(shape, jnp.float32) for shape in out_shapes],
        compiler_params=pltpu.CompilerParams(vmem_limit_bytes=VMEM_BYTES),
        name=name,
    )


def block(array, index):
    return array[:, index * LANES : (index + 1) * LANES]


def stage_kernel(vectors_hbm, hvectors_hbm, slots_ref, stack_ref, arrived):
    copies = [
        pltpu.make_async_copy(source, stack_ref.at[index], arrived.at[index])
        for index, source in enumerate((vectors_hbm, hvectors_hbm))
    ]
    for copy in copies:
        copy.start()
    for copy in copies:
        copy.wait()
    vectors = stack_ref[0]
    hvectors = stack_ref[1]
    members = vectors.shape[0]
    top = jnp.sum(vectors * hvectors, axis=1, keepdims=True)
    bottom = jnp.sum(vectors * vectors, axis=1, keepdims=True)
    lane = lax.broadcasted_iota(jnp.int32, (members, LANES), 1)
    line = lax.broadcasted_iota(jnp.int32, (members, LANES), 0)
    spread = jnp.where(lane == line, top, 0.0) + jnp.where(lane == line + members, bottom, 0.0)
    sums = jnp.sum(spread, axis=0, keepdims=True)
    slots_ref[...] = jnp.broadcast_to(sums, slots_ref.shape)


def prepare_kernel(
    rows_ref,
    vectors_hbm,
    previous_hbm,
    hvectors_hbm,
    hprevious_hbm,
    rows_out_ref,
    basis_ref,
    images_ref,
    arrived,
):
    copies = [
        pltpu.make_async_copy(source, target.at[place], arrived.at[index])
        for index, (source, target, place) in enumerate(
            (
                (vectors_hbm, basis_ref, 0),
                (previous_hbm, basis_ref, 1),
                (hvectors_hbm, images_ref, 0),
                (hprevious_hbm, images_ref, 1),
            )
        )
    ]
    for copy in copies:
        copy.start()
    rows = rows_ref[...]
    core = lax.rem(lax.axis_index("col"), 2)
    chips = lax.axis_size("col") // 2
    blocks = basis_ref.shape[2] // LANES
    index, peer = rows % blocks, rows // blocks
    other = jnp.where(peer % 2 == core, 0, 1)
    rows_out_ref[...] = (other * chips + peer // 2) * blocks + index
    for copy in copies:
        copy.wait()


def residual_kernel(sums_ref, basis_ref, images_ref, residual_ref, slots_ref):
    members = basis_ref.shape[1]
    sums = jnp.sum(sums_ref[...], axis=0, keepdims=True)
    lane = lax.broadcasted_iota(jnp.int32, (members, LANES), 1)
    line = lax.broadcasted_iota(jnp.int32, (members, LANES), 0)
    top = jnp.sum(jnp.where(lane == line, sums, 0.0), axis=1, keepdims=True)
    bottom = jnp.sum(jnp.where(lane == line + members, sums, 0.0), axis=1, keepdims=True)
    residual = images_ref[0] - (top / (bottom + EPSILON)) * basis_ref[0]
    residual_ref[...] = residual
    blocks = residual.shape[1] // LANES
    for index in range(blocks):
        for slot in range(slots_ref.shape[0]):
            slots_ref[slot, index] = block(residual, index)
    basis = jnp.concatenate([basis_ref[0], residual, basis_ref[1]], axis=0)
    gram = exact_dot(basis, basis, NT)
    early = exact_dot(jnp.concatenate([images_ref[0], images_ref[1]], axis=0), basis, NT)
    extra = [
        gram[:members],
        gram[members : 2 * members],
        gram[2 * members :],
        early[:members],
        early[members:],
    ]
    for index, part in enumerate(pack_rows(extra)):
        for slot in range(slots_ref.shape[0]):
            slots_ref[slot, blocks + index] = part


def pair_kernel(residual_ref, far_ref, slots_ref):
    x_hi = lax.rem(lax.axis_index("row"), 2)
    blocks = residual_ref.shape[1] // LANES
    for place, rows in ((x_hi, residual_ref[...]), (1 - x_hi, far_ref[...])):
        for index in range(blocks):
            for slot in range(slots_ref.shape[0]):
                slots_ref[slot, place * blocks + index] = block(rows, index)


def pack_rows(parts):
    first, second, third, fourth, fifth = parts
    members = first.shape[0]
    pieces = [fifth[:, i * members : (i + 1) * members] for i in range(3)]
    zero = jnp.zeros((members, members), jnp.float32)
    return [
        jnp.concatenate([first, second, pieces[0], pieces[1]], axis=1),
        jnp.concatenate([third, fourth, pieces[2], zero], axis=1),
    ]


def unpack_rows(one, two):
    members = one.shape[0]
    wide = 3 * members
    fifth = jnp.concatenate([one[:, 2 * wide :], two[:, 2 * wide : 2 * wide + members]], axis=1)
    return [one[:, :wide], one[:, wide : 2 * wide], two[:, :wide], two[:, wide : 2 * wide], fifth]


def factor_kernel(sums_ref, far_ref, inverse_ref, early_ref):
    extras = [sums_ref[index] + far_ref[index] for index in range(2)]
    members = extras[0].shape[0]
    order = 3 * members
    first, second, third, fourth, fifth = unpack_rows(*extras)
    early_ref[...] = jnp.concatenate([fourth, fifth], axis=0)
    gram = jnp.concatenate([first, second, third], axis=0)
    line = lax.broadcasted_iota(jnp.int32, (order, order), 0)
    lane = lax.broadcasted_iota(jnp.int32, (order, order), 1)
    work = jnp.concatenate([gram, jnp.where(line == lane, 1.0, 0.0)], axis=1)
    rows = lax.broadcasted_iota(jnp.int32, (order, 1), 0)
    for step in range(order):
        pivot = work[step : step + 1, step : step + 1]
        scale = lax.rsqrt(pivot)
        scale = scale * (1.5 - 0.5 * pivot * scale * scale)
        lead = work[step : step + 1, :] * scale
        column = work[:, step : step + 1] * scale
        work = jnp.where(rows == step, lead, jnp.where(rows > step, work - column * lead, work))
    inverse_ref[...] = work[:, order:]


def orthonormal_kernel(inverse_ref, basis_ref, residual_ref, out_ref, *, row_scale):
    rows = jnp.concatenate([basis_ref[0], residual_ref[...], basis_ref[1]], axis=0)
    out_ref[...] = exact_dot(inverse_ref[...] * row_scale, rows, NN)


def orthonormal_image_kernel(
    inverse_ref, images_ref, image_ref, far_ref, out_ref, *, row_scale
):
    image = image_ref[...] + far_ref[...]
    rows = jnp.concatenate([images_ref[0], image, images_ref[1]], axis=0)
    out_ref[...] = exact_dot(inverse_ref[...] * row_scale, rows, NN)


def sum_peers(parts_ref, index):
    part = parts_ref[0, index]
    for peer in range(1, parts_ref.shape[0]):
        part = part + parts_ref[peer, index]
    return part


def image_kernel(
    col_parts_ref,
    row_parts_ref,
    basis_ref,
    residual_ref,
    far_basis_ref,
    far_residual_ref,
    image_ref,
    to_far_ref,
    slots_ref,
):
    x_hi = lax.rem(lax.axis_index("row"), 2)
    blocks = image_ref.shape[1] // LANES
    for index in range(blocks):
        lanes = slice(index * LANES, (index + 1) * LANES)
        image_ref[:, lanes] = sum_peers(col_parts_ref, index) + sum_peers(
            row_parts_ref, x_hi * blocks + index
        )
        to_far_ref[:, lanes] = sum_peers(row_parts_ref, (1 - x_hi) * blocks + index)
    basis = jnp.concatenate([basis_ref[0], residual_ref[...], basis_ref[1]], axis=0)
    late = exact_dot(image_ref[...], basis, NT)
    basis = jnp.concatenate([far_basis_ref[0], far_residual_ref[...], far_basis_ref[1]], axis=0)
    late = late + exact_dot(to_far_ref[...], basis, NT)
    half = late.shape[0] // 2
    pad = jnp.zeros((half, LANES // 2 - late.shape[1]), jnp.float32)
    packed = jnp.concatenate([late[:half], pad, late[half:], pad], axis=1)
    slots_ref[...] = jnp.broadcast_to(packed[None], slots_ref.shape)


def projected_kernel(received_ref, inverse_ref, early_ref, projected_ref):
    packed = jnp.sum(received_ref[...], axis=0)
    early = early_ref[...]
    members = early.shape[0] // 2
    wide = early.shape[1]
    half = LANES // 2
    late = jnp.concatenate([packed[:, :wide], packed[:, half : half + wide]], axis=0)
    mixed_t = jnp.concatenate([early[:members], late, early[members:]], axis=0)
    inverse = inverse_ref[...]
    half_done = exact_dot(inverse, mixed_t, NT)
    projected_ref[...] = exact_dot(half_done, inverse, NT)


def split_blocks(x_ref, split_ref, start, per_peer):
    def split(peer, carry):
        for index in range(per_peer):
            value = x_ref[peer, index]
            high = value.astype(jnp.bfloat16)
            low = (value - high.astype(jnp.float32)).astype(jnp.bfloat16)
            split_ref[start + peer * per_peer + index] = jnp.concatenate([high, low], axis=0)
        return carry

    lax.fori_loop(0, x_ref.shape[0], split, 0)


def group_size(slots):
    return math.gcd(slots, 24)


def group_count(count_ref, slots):
    return (jnp.minimum(count_ref[0, 0], slots) + group_size(slots) - 1) // group_size(slots)


def group_copy(tiles_hbm, tiles_ref, arrived, counter):
    size = group_size(tiles_ref.shape[0])
    part = pl.ds(counter * size, size)
    return pltpu.make_async_copy(tiles_hbm.at[part], tiles_ref.at[part], arrived.at[counter])


def start_tiles(count_ref, tiles_hbm, tiles_ref, arrived):
    def start(counter, carry):
        group_copy(tiles_hbm, tiles_ref, arrived, counter).start()
        return carry

    lax.fori_loop(0, group_count(count_ref, tiles_ref.shape[0]), start, 0)


def tile_groups(
    count_ref, tiles_hbm, tiles_ref, arrived, split_ref, out_ref, source_of, target_of, dims
):
    slots = tiles_ref.shape[0]
    unroll = group_size(slots)
    live = count_ref[0, 0]
    members = split_ref.shape[1] // 2

    def group(counter, carry):
        group_copy(tiles_hbm, tiles_ref, arrived, counter).wait()
        base = counter * unroll
        products = []
        for offset in range(unroll):
            slot = base + offset
            product = lax.dot_general(
                split_ref[source_of(slot)], tiles_ref[slot], dims, preferred_element_type=jnp.float32
            )
            product = product[:members] + product[members:]
            products.append(jnp.where(slot < live, product, 0.0))
        for offset in range(unroll):
            target = target_of(base + offset)
            out_ref[target] = out_ref[target] + products[offset]
        return carry

    lax.fori_loop(0, group_count(count_ref, slots), group, 0)


def backward_kernel(
    count_ref,
    rows_ref,
    cols_ref,
    tiles_hbm,
    own_ref,
    other_ref,
    out_ref,
    tiles_ref,
    arrived,
    split_ref,
):
    start_tiles(count_ref, tiles_hbm, tiles_ref, arrived)
    peers, width = own_ref.shape[:2]
    per_peer = split_ref.shape[0] // (2 * peers)
    extra = width - per_peer
    pair = 2 * per_peer
    out_ref[...] = jnp.zeros_like(out_ref)
    split_blocks(own_ref, split_ref, 0, per_peer)
    split_blocks(other_ref, split_ref, peers * per_peer, per_peer)
    for index in range(extra):
        part = sum_peers(own_ref, per_peer + index) + sum_peers(other_ref, per_peer + index)
        for start in range(pair, out_ref.shape[0], pair + extra):
            out_ref[start + index] = part
    tile_groups(
        count_ref,
        tiles_hbm,
        tiles_ref,
        arrived,
        split_ref,
        out_ref,
        lambda slot: rows_ref[0, 0, slot],
        lambda slot: cols_ref[0, 0, slot] + extra * (cols_ref[0, 0, slot] // pair),
        NN,
    )


def forward_kernel(
    count_ref,
    rows_ref,
    cols_ref,
    tiles_hbm,
    x_ref,
    own_ref,
    other_ref,
    tiles_ref,
    arrived,
    split_ref,
    totals_ref,
):
    start_tiles(count_ref, tiles_hbm, tiles_ref, arrived)
    totals_ref[...] = jnp.zeros_like(totals_ref)
    split_blocks(x_ref, split_ref, 0, x_ref.shape[1])
    tile_groups(
        count_ref,
        tiles_hbm,
        tiles_ref,
        arrived,
        split_ref,
        totals_ref,
        lambda slot: cols_ref[0, 0, slot],
        lambda slot: rows_ref[0, 0, slot],
        NT,
    )
    half = totals_ref.shape[0] // 2
    own_ref[...] = totals_ref[:half]
    other_ref[...] = totals_ref[half:]


def tile_call(kernel, count, rows, cols, tiles, arrays, out_shapes, scratch, name):
    smem = pl.BlockSpec(memory_space=pltpu.SMEM)
    vmem = pl.BlockSpec(memory_space=pltpu.VMEM)
    return pl.pallas_call(
        kernel,
        out_shape=[jax.ShapeDtypeStruct(shape, jnp.float32) for shape in out_shapes],
        in_specs=[smem] * 3 + [pl.BlockSpec(memory_space=pl.ANY)] + [vmem] * len(arrays),
        out_specs=[vmem] * len(out_shapes),
        scratch_shapes=[
            pltpu.VMEM(tiles.shape, tiles.dtype),
            pltpu.SemaphoreType.DMA((tiles.shape[0] // group_size(tiles.shape[0]),)),
        ]
        + scratch,
        compiler_params=pltpu.CompilerParams(vmem_limit_bytes=FULL_VMEM_BYTES),
        name=name,
    )(count, rows, cols, tiles, *arrays)


def exchange(slots, axes, groups=None):
    return lax.all_to_all(slots, axes, 0, 0, axis_index_groups=groups, tiled=True)


def swap(array, axis, distance):
    return lax.ppermute(array, axis, [(i, i ^ distance) for i in range(lax.axis_size(axis))])


def on_device(
    tile_blocks, tile_rows, tile_cols, tile_count, vectors, hvectors, previous, hprevious
):
    n_row = lax.axis_size("row")
    n_col = lax.axis_size("col")
    everyone = ("row", "col")
    chips = n_col // 2
    lines = n_row // 2
    core_groups = [[2 * chip + core for chip in range(chips)] for core in (0, 1)]
    z_groups = [[2 * line + x for line in range(lines)] for x in (0, 1)]
    members, piece = vectors.shape
    blocks = piece // LANES
    pair = 2 * blocks
    order = 3 * members
    tiles = tile_blocks[0, 0]
    row_scale = math.sqrt(piece * n_row * n_col)
    f32 = jnp.float32

    hbm_spec = pl.BlockSpec(memory_space=pl.ANY)
    vmem_spec = pl.BlockSpec(memory_space=pltpu.VMEM)
    params = pltpu.CompilerParams(vmem_limit_bytes=VMEM_BYTES)
    (sums,) = pl.pallas_call(
        stage_kernel,
        out_shape=[jax.ShapeDtypeStruct((n_row * n_col, LANES), f32)],
        in_specs=[hbm_spec, hbm_spec],
        out_specs=[vmem_spec],
        scratch_shapes=[
            pltpu.VMEM((2, members, piece), f32),
            pltpu.SemaphoreType.DMA((2,)),
        ],
        compiler_params=pltpu.CompilerParams(vmem_limit_bytes=FULL_VMEM_BYTES),
        name="stage",
    )(vectors, hvectors)
    rows, basis, images = pl.pallas_call(
        prepare_kernel,
        out_shape=[
            jax.ShapeDtypeStruct(tile_rows.shape, jnp.int32),
            jax.ShapeDtypeStruct((2, members, piece), f32),
            jax.ShapeDtypeStruct((2, members, piece), f32),
        ],
        in_specs=[vmem_spec] + [hbm_spec] * 4,
        out_specs=[vmem_spec] * 3,
        scratch_shapes=[pltpu.SemaphoreType.DMA((4,))],
        compiler_params=params,
        name="prepare",
    )(tile_rows, vectors, previous, hvectors, hprevious)
    sums = exchange(sums, everyone)
    sums, rows, basis, images = lax.optimization_barrier((sums, rows, basis, images))
    residual, col_slots = call(
        residual_kernel, [(members, piece), (chips, blocks + 2, members, LANES)], "residual"
    )(sums, basis, images)
    far_residual = swap(residual, "row", 1)
    (row_slots,) = call(pair_kernel, [(lines, pair, members, LANES)], "pair")(residual, far_residual)
    own_range = exchange(col_slots, "col", core_groups)
    own_range, row_slots, sent_basis = lax.optimization_barrier((own_range, row_slots, basis))
    far_basis = swap(sent_basis, "row", 1)
    other_range = swap(own_range, "col", 1)
    col_range = exchange(row_slots, "row", z_groups)
    (col_totals,) = tile_call(
        backward_kernel,
        tile_count,
        rows,
        tile_cols,
        tiles,
        (own_range, other_range),
        [(lines * (pair + 2), members, LANES)],
        [pltpu.VMEM((n_col * blocks, 2 * members, LANES), jnp.bfloat16)],
        "backward_tiles",
    )
    col_totals, col_range, far_basis = lax.optimization_barrier((col_totals, col_range, far_basis))
    row_parts = exchange(col_totals.reshape(lines, pair + 2, members, LANES), "row", z_groups)
    half = (chips * blocks, members, LANES)
    own_totals, other_totals = tile_call(
        forward_kernel,
        tile_count,
        rows,
        tile_cols,
        tiles,
        (col_range,),
        [half, half],
        [
            pltpu.VMEM((lines * pair, 2 * members, LANES), jnp.bfloat16),
            pltpu.VMEM((n_col * blocks, members, LANES), f32),
        ],
        "forward_tiles",
    )
    row_parts, own_totals, other_totals = lax.optimization_barrier(
        (row_parts, own_totals, other_totals)
    )
    totals = own_totals + swap(other_totals, "col", 1)
    col_parts = exchange(totals.reshape(chips, blocks, members, LANES), "col", core_groups)
    gram_sums = jnp.sum(row_parts[:, pair:], axis=0)
    gram_far = swap(gram_sums, "row", 1)
    col_parts, gram_far = lax.optimization_barrier((col_parts, gram_far))
    image, to_far, slots = call(
        image_kernel,
        [(members, piece)] * 2 + [(n_row * n_col, members // 2, LANES)],
        "image",
    )(col_parts, row_parts, basis, residual, far_basis, far_residual)
    late = exchange(slots, everyone)
    to_far, gram_sums, gram_far = lax.optimization_barrier((to_far, gram_sums, gram_far))
    from_far = swap(to_far, "row", 1)
    inverse, early = call(factor_kernel, [(order, order), (2 * members, order)], "factor")(
        gram_sums, gram_far
    )
    (orthonormal,) = call(
        functools.partial(orthonormal_kernel, row_scale=row_scale), [(order, piece)], "orthonormal"
    )(inverse, basis, residual)
    (orthonormal_image,) = call(
        functools.partial(orthonormal_image_kernel, row_scale=row_scale),
        [(order, piece)],
        "orthonormal_image",
    )(inverse, images, image, from_far)
    (projected,) = call(projected_kernel, [(order, order)], "projected")(late, inverse, early)
    return (orthonormal, orthonormal_image, projected)


def solution(mesh):
    in_specs = (
        P("row", "col", None, None, None),
        P("row", "col", None),
        P("row", "col", None),
        P("row", "col"),
        P(None, ("row", "col")),
        P(None, ("row", "col")),
        P(None, ("row", "col")),
        P(None, ("row", "col")),
    )
    out_specs = (P(None, ("row", "col")), P(None, ("row", "col")), P())
    return jax.shard_map(
        on_device, mesh=mesh, in_specs=in_specs, out_specs=out_specs, check_vma=False
    )
```

```python
import functools
import math

import jax
import jax.numpy as jnp
from jax import lax
from jax.experimental import pallas as pl
from jax.experimental.pallas import tpu as pltpu
from jax.sharding import PartitionSpec as P

EPSILON = 1e-06
HIGHEST_PRECISION = lax.Precision.HIGHEST
LANES = 128
VMEM_BYTES = 32 << 20
FULL_VMEM_BYTES = 60 << 20
TILE_VMEM_BYTES = 54 << 20
NT = (((1,), (1,)), ((), ()))
NN = (((1,), (0,)), ((), ()))


def exact_dot(first, second, dims):
    return lax.dot_general(
        first, second, dims, precision=HIGHEST_PRECISION, preferred_element_type=jnp.float32
    )


def call(kernel, out_shapes, name):
    return pl.pallas_call(
        kernel,
        out_shape=[jax.ShapeDtypeStruct(shape, jnp.float32) for shape in out_shapes],
        compiler_params=pltpu.CompilerParams(vmem_limit_bytes=VMEM_BYTES),
        name=name,
    )


def block(array, index):
    return array[:, index * LANES : (index + 1) * LANES]


def stage_kernel(vectors_hbm, hvectors_hbm, slots_ref, stack_ref, arrived):
    copies = [
        pltpu.make_async_copy(source, stack_ref.at[index], arrived.at[index])
        for index, source in enumerate((vectors_hbm, hvectors_hbm))
    ]
    for copy in copies:
        copy.start()
    for copy in copies:
        copy.wait()
    vectors = stack_ref[0]
    hvectors = stack_ref[1]
    members = vectors.shape[0]
    top = jnp.sum(vectors * hvectors, axis=1, keepdims=True)
    bottom = jnp.sum(vectors * vectors, axis=1, keepdims=True)
    lane = lax.broadcasted_iota(jnp.int32, (members, LANES), 1)
    line = lax.broadcasted_iota(jnp.int32, (members, LANES), 0)
    spread = jnp.where(lane == line, top, 0.0) + jnp.where(lane == line + members, bottom, 0.0)
    sums = jnp.sum(spread, axis=0, keepdims=True)
    slots_ref[...] = jnp.broadcast_to(sums, slots_ref.shape)


def prepare_kernel(
    rows_ref,
    vectors_hbm,
    previous_hbm,
    hvectors_hbm,
    hprevious_hbm,
    rows_out_ref,
    basis_ref,
    images_ref,
    arrived,
):
    copies = [
        pltpu.make_async_copy(source, target.at[place], arrived.at[index])
        for index, (source, target, place) in enumerate(
            (
                (vectors_hbm, basis_ref, 0),
                (previous_hbm, basis_ref, 1),
                (hvectors_hbm, images_ref, 0),
                (hprevious_hbm, images_ref, 1),
            )
        )
    ]
    for copy in copies:
        copy.start()
    rows = rows_ref[...]
    core = lax.rem(lax.axis_index("col"), 2)
    chips = lax.axis_size("col") // 2
    blocks = basis_ref.shape[2] // LANES
    index, peer = rows % blocks, rows // blocks
    other = jnp.where(peer % 2 == core, 0, 1)
    rows_out_ref[...] = (other * chips + peer // 2) * blocks + index
    for copy in copies:
        copy.wait()


def residual_kernel(sums_ref, basis_ref, images_ref, residual_ref, col_slots_ref, row_slots_ref):
    members = basis_ref.shape[1]
    sums = jnp.sum(sums_ref[...], axis=0, keepdims=True)
    lane = lax.broadcasted_iota(jnp.int32, (members, LANES), 1)
    line = lax.broadcasted_iota(jnp.int32, (members, LANES), 0)
    top = jnp.sum(jnp.where(lane == line, sums, 0.0), axis=1, keepdims=True)
    bottom = jnp.sum(jnp.where(lane == line + members, sums, 0.0), axis=1, keepdims=True)
    residual = images_ref[0] - (top / (bottom + EPSILON)) * basis_ref[0]
    residual_ref[...] = residual
    blocks = residual.shape[1] // LANES
    for index in range(blocks):
        for slots_ref in (col_slots_ref, row_slots_ref):
            for slot in range(slots_ref.shape[0]):
                slots_ref[slot, index] = block(residual, index)
    basis = jnp.concatenate([basis_ref[0], residual, basis_ref[1]], axis=0)
    gram = exact_dot(basis, basis, NT)
    early = exact_dot(jnp.concatenate([images_ref[0], images_ref[1]], axis=0), basis, NT)
    extra = [
        gram[:members],
        gram[members : 2 * members],
        gram[2 * members :],
        early[:members],
        early[members:],
    ]
    for index, part in enumerate(pack_rows(extra)):
        for slot in range(col_slots_ref.shape[0]):
            col_slots_ref[slot, blocks + index] = part


def pack_rows(parts):
    first, second, third, fourth, fifth = parts
    members = first.shape[0]
    pieces = [fifth[:, i * members : (i + 1) * members] for i in range(3)]
    zero = jnp.zeros((members, members), jnp.float32)
    return [
        jnp.concatenate([first, second, pieces[0], pieces[1]], axis=1),
        jnp.concatenate([third, fourth, pieces[2], zero], axis=1),
    ]


def unpack_rows(one, two):
    members = one.shape[0]
    wide = 3 * members
    fifth = jnp.concatenate([one[:, 2 * wide :], two[:, 2 * wide : 2 * wide + members]], axis=1)
    return [one[:, :wide], one[:, wide : 2 * wide], two[:, :wide], two[:, wide : 2 * wide], fifth]


def sum_peers(parts_ref, index):
    part = parts_ref[0, index]
    for peer in range(1, parts_ref.shape[0]):
        part = part + parts_ref[peer, index]
    return part


def factor_kernel(parts_ref, inverse_ref, early_ref):
    width = parts_ref.shape[1]
    extras = [sum_peers(parts_ref, width - 2), sum_peers(parts_ref, width - 1)]
    members = extras[0].shape[0]
    order = 3 * members
    first, second, third, fourth, fifth = unpack_rows(*extras)
    early_ref[...] = jnp.concatenate([fourth, fifth], axis=0)
    gram = jnp.concatenate([first, second, third], axis=0)
    line = lax.broadcasted_iota(jnp.int32, (order, order), 0)
    lane = lax.broadcasted_iota(jnp.int32, (order, order), 1)
    work = jnp.concatenate([gram, jnp.where(line == lane, 1.0, 0.0)], axis=1)
    rows = lax.broadcasted_iota(jnp.int32, (order, 1), 0)
    for step in range(order):
        pivot = work[step : step + 1, step : step + 1]
        scale = lax.rsqrt(pivot)
        scale = scale * (1.5 - 0.5 * pivot * scale * scale)
        lead = work[step : step + 1, :] * scale
        column = work[:, step : step + 1] * scale
        work = jnp.where(rows == step, lead, jnp.where(rows > step, work - column * lead, work))
    inverse_ref[...] = work[:, order:]


def orthonormal_kernel(inverse_ref, basis_ref, residual_ref, out_ref, *, row_scale):
    rows = jnp.concatenate([basis_ref[0], residual_ref[...], basis_ref[1]], axis=0)
    out_ref[...] = exact_dot(inverse_ref[...] * row_scale, rows, NN)


def orthonormal_image_kernel(inverse_ref, images_ref, image_ref, out_ref, *, row_scale):
    rows = jnp.concatenate([images_ref[0], image_ref[...], images_ref[1]], axis=0)
    out_ref[...] = exact_dot(inverse_ref[...] * row_scale, rows, NN)


def image_kernel(col_parts_ref, row_parts_ref, basis_ref, residual_ref, image_ref, slots_ref):
    blocks = image_ref.shape[1] // LANES
    for index in range(blocks):
        image_ref[:, index * LANES : (index + 1) * LANES] = sum_peers(
            col_parts_ref, index
        ) + sum_peers(row_parts_ref, index)
    basis = jnp.concatenate([basis_ref[0], residual_ref[...], basis_ref[1]], axis=0)
    late = exact_dot(image_ref[...], basis, NT)
    half = late.shape[0] // 2
    pad = jnp.zeros((half, LANES // 2 - late.shape[1]), jnp.float32)
    packed = jnp.concatenate([late[:half], pad, late[half:], pad], axis=1)
    slots_ref[...] = jnp.broadcast_to(packed[None], slots_ref.shape)


def projected_kernel(received_ref, inverse_ref, early_ref, projected_ref):
    packed = jnp.sum(received_ref[...], axis=0)
    early = early_ref[...]
    members = early.shape[0] // 2
    wide = early.shape[1]
    half = LANES // 2
    late = jnp.concatenate([packed[:, :wide], packed[:, half : half + wide]], axis=0)
    mixed_t = jnp.concatenate([early[:members], late, early[members:]], axis=0)
    inverse = inverse_ref[...]
    half_done = exact_dot(inverse, mixed_t, NT)
    projected_ref[...] = exact_dot(half_done, inverse, NT)


def split_blocks(x_ref, split_ref, start, per_peer):
    def split(peer, carry):
        for index in range(per_peer):
            value = x_ref[peer, index]
            high = value.astype(jnp.bfloat16)
            low = (value - high.astype(jnp.float32)).astype(jnp.bfloat16)
            split_ref[start + peer * per_peer + index] = jnp.concatenate([high, low], axis=0)
        return carry

    lax.fori_loop(0, x_ref.shape[0], split, 0)


def group_size(slots):
    return math.gcd(slots, 24)


def group_count(count_ref, slots):
    return (jnp.minimum(count_ref[0, 0], slots) + group_size(slots) - 1) // group_size(slots)


def group_copy(tiles_hbm, tiles_ref, arrived, counter):
    size = group_size(tiles_ref.shape[0])
    part = pl.ds(counter * size, size)
    return pltpu.make_async_copy(tiles_hbm.at[part], tiles_ref.at[part], arrived.at[counter])


def start_tiles(count_ref, tiles_hbm, tiles_ref, arrived):
    def start(counter, carry):
        group_copy(tiles_hbm, tiles_ref, arrived, counter).start()
        return carry

    lax.fori_loop(0, group_count(count_ref, tiles_ref.shape[0]), start, 0)


def tile_groups(
    count_ref, tiles_hbm, tiles_ref, arrived, split_ref, out_ref, source_of, target_of, dims
):
    slots = tiles_ref.shape[0]
    unroll = group_size(slots)
    live = count_ref[0, 0]
    members = split_ref.shape[1] // 2

    def group(counter, carry):
        group_copy(tiles_hbm, tiles_ref, arrived, counter).wait()
        base = counter * unroll
        products = []
        for offset in range(unroll):
            slot = base + offset
            product = lax.dot_general(
                split_ref[source_of(slot)], tiles_ref[slot], dims, preferred_element_type=jnp.float32
            )
            product = product[:members] + product[members:]
            products.append(jnp.where(slot < live, product, 0.0))
        for offset in range(unroll):
            target = target_of(base + offset)
            out_ref[target] = out_ref[target] + products[offset]
        return carry

    lax.fori_loop(0, group_count(count_ref, slots), group, 0)


def backward_kernel(
    count_ref,
    rows_ref,
    cols_ref,
    tiles_hbm,
    own_ref,
    other_ref,
    out_ref,
    tiles_ref,
    arrived,
    split_ref,
):
    start_tiles(count_ref, tiles_hbm, tiles_ref, arrived)
    peers, width = own_ref.shape[:2]
    per_peer = split_ref.shape[0] // (2 * peers)
    extra = width - per_peer
    out_ref[...] = jnp.zeros_like(out_ref)
    split_blocks(own_ref, split_ref, 0, per_peer)
    split_blocks(other_ref, split_ref, peers * per_peer, per_peer)
    for index in range(extra):
        part = sum_peers(own_ref, per_peer + index) + sum_peers(other_ref, per_peer + index)
        for start in range(per_peer, out_ref.shape[0], width):
            out_ref[start + index] = part
    tile_groups(
        count_ref,
        tiles_hbm,
        tiles_ref,
        arrived,
        split_ref,
        out_ref,
        lambda slot: rows_ref[0, 0, slot],
        lambda slot: cols_ref[0, 0, slot] + extra * (cols_ref[0, 0, slot] // per_peer),
        NN,
    )


def forward_kernel(
    count_ref,
    rows_ref,
    cols_ref,
    tiles_hbm,
    x_ref,
    own_ref,
    other_ref,
    tiles_ref,
    arrived,
    split_ref,
    totals_ref,
):
    start_tiles(count_ref, tiles_hbm, tiles_ref, arrived)
    totals_ref[...] = jnp.zeros_like(totals_ref)
    split_blocks(x_ref, split_ref, 0, x_ref.shape[1])
    tile_groups(
        count_ref,
        tiles_hbm,
        tiles_ref,
        arrived,
        split_ref,
        totals_ref,
        lambda slot: cols_ref[0, 0, slot],
        lambda slot: rows_ref[0, 0, slot],
        NT,
    )
    half = totals_ref.shape[0] // 2
    own_ref[...] = totals_ref[:half]
    other_ref[...] = totals_ref[half:]


def tile_call(kernel, count, rows, cols, tiles, arrays, out_shapes, scratch, name):
    smem = pl.BlockSpec(memory_space=pltpu.SMEM)
    vmem = pl.BlockSpec(memory_space=pltpu.VMEM)
    return pl.pallas_call(
        kernel,
        out_shape=[jax.ShapeDtypeStruct(shape, jnp.float32) for shape in out_shapes],
        in_specs=[smem] * 3 + [pl.BlockSpec(memory_space=pl.ANY)] + [vmem] * len(arrays),
        out_specs=[vmem] * len(out_shapes),
        scratch_shapes=[
            pltpu.VMEM(tiles.shape, tiles.dtype),
            pltpu.SemaphoreType.DMA((tiles.shape[0] // group_size(tiles.shape[0]),)),
        ]
        + scratch,
        compiler_params=pltpu.CompilerParams(vmem_limit_bytes=TILE_VMEM_BYTES),
        name=name,
    )(count, rows, cols, tiles, *arrays)


def exchange(slots, axes, groups=None):
    return lax.all_to_all(slots, axes, 0, 0, axis_index_groups=groups, tiled=True)


def swap(array, axis, distance):
    return lax.ppermute(array, axis, [(i, i ^ distance) for i in range(lax.axis_size(axis))])


def on_device(
    tile_blocks, tile_rows, tile_cols, tile_count, vectors, hvectors, previous, hprevious
):
    n_row = lax.axis_size("row")
    n_col = lax.axis_size("col")
    everyone = ("row", "col")
    chips = n_col // 2
    core_groups = [[2 * chip + core for chip in range(chips)] for core in (0, 1)]
    members, piece = vectors.shape
    blocks = piece // LANES
    order = 3 * members
    tiles = tile_blocks[0, 0]
    row_scale = math.sqrt(piece * n_row * n_col)
    f32 = jnp.float32

    hbm_spec = pl.BlockSpec(memory_space=pl.ANY)
    vmem_spec = pl.BlockSpec(memory_space=pltpu.VMEM)
    params = pltpu.CompilerParams(vmem_limit_bytes=VMEM_BYTES)
    (sums,) = pl.pallas_call(
        stage_kernel,
        out_shape=[jax.ShapeDtypeStruct((n_row * n_col, LANES), f32)],
        in_specs=[hbm_spec, hbm_spec],
        out_specs=[vmem_spec],
        scratch_shapes=[
            pltpu.VMEM((2, members, piece), f32),
            pltpu.SemaphoreType.DMA((2,)),
        ],
        compiler_params=pltpu.CompilerParams(vmem_limit_bytes=FULL_VMEM_BYTES),
        name="stage",
    )(vectors, hvectors)
    rows, basis, images = pl.pallas_call(
        prepare_kernel,
        out_shape=[
            jax.ShapeDtypeStruct(tile_rows.shape, jnp.int32),
            jax.ShapeDtypeStruct((2, members, piece), f32),
            jax.ShapeDtypeStruct((2, members, piece), f32),
        ],
        in_specs=[vmem_spec] + [hbm_spec] * 4,
        out_specs=[vmem_spec] * 3,
        scratch_shapes=[pltpu.SemaphoreType.DMA((4,))],
        compiler_params=params,
        name="prepare",
    )(tile_rows, vectors, previous, hvectors, hprevious)
    sums = exchange(sums, everyone)
    sums, rows, basis, images = lax.optimization_barrier((sums, rows, basis, images))
    residual, col_slots, row_slots = call(
        residual_kernel,
        [
            (members, piece),
            (chips, blocks + 2, members, LANES),
            (n_row, blocks, members, LANES),
        ],
        "residual",
    )(sums, basis, images)
    own_range = exchange(col_slots, "col", core_groups)
    own_range, row_slots = lax.optimization_barrier((own_range, row_slots))
    other_range = swap(own_range, "col", 1)
    col_range = exchange(row_slots, "row")
    (col_totals,) = tile_call(
        backward_kernel,
        tile_count,
        rows,
        tile_cols,
        tiles,
        (own_range, other_range),
        [(n_row * (blocks + 2), members, LANES)],
        [pltpu.VMEM((n_col * blocks, 2 * members, LANES), jnp.bfloat16)],
        "backward_tiles",
    )
    col_totals, col_range = lax.optimization_barrier((col_totals, col_range))
    row_parts = exchange(col_totals.reshape(n_row, blocks + 2, members, LANES), "row")
    half = (chips * blocks, members, LANES)
    own_totals, other_totals = tile_call(
        forward_kernel,
        tile_count,
        rows,
        tile_cols,
        tiles,
        (col_range,),
        [half, half],
        [
            pltpu.VMEM((n_row * blocks, 2 * members, LANES), jnp.bfloat16),
            pltpu.VMEM((n_col * blocks, members, LANES), f32),
        ],
        "forward_tiles",
    )
    row_parts, own_totals, other_totals = lax.optimization_barrier(
        (row_parts, own_totals, other_totals)
    )
    totals = own_totals + swap(other_totals, "col", 1)
    col_parts = exchange(totals.reshape(chips, blocks, members, LANES), "col", core_groups)
    inverse, early = call(factor_kernel, [(order, order), (2 * members, order)], "factor")(row_parts)
    (orthonormal,) = call(
        functools.partial(orthonormal_kernel, row_scale=row_scale), [(order, piece)], "orthonormal"
    )(inverse, basis, residual)
    col_parts, inverse, orthonormal = lax.optimization_barrier((col_parts, inverse, orthonormal))
    image, slots = call(
        image_kernel, [(members, piece), (n_row * n_col, members // 2, LANES)], "image"
    )(col_parts, row_parts, basis, residual)
    late = exchange(slots, everyone)
    (orthonormal_image,) = call(
        functools.partial(orthonormal_image_kernel, row_scale=row_scale),
        [(order, piece)],
        "orthonormal_image",
    )(inverse, images, image)
    (projected,) = call(projected_kernel, [(order, order)], "projected")(late, inverse, early)
    return (orthonormal, orthonormal_image, projected)


def solution(mesh):
    in_specs = (
        P("row", "col", None, None, None),
        P("row", "col", None),
        P("row", "col", None),
        P("row", "col"),
        P(None, ("row", "col")),
        P(None, ("row", "col")),
        P(None, ("row", "col")),
        P(None, ("row", "col")),
    )
    out_specs = (P(None, ("row", "col")), P(None, ("row", "col")), P())
    return jax.shard_map(
        on_device, mesh=mesh, in_specs=in_specs, out_specs=out_specs, check_vma=False
    )
```

```python
import functools
import math

import jax
import jax.numpy as jnp
from jax import lax
from jax.experimental import pallas as pl
from jax.experimental.pallas import tpu as pltpu
from jax.sharding import PartitionSpec as P

EPSILON = 1e-06
HIGHEST_PRECISION = lax.Precision.HIGHEST
LANES = 128
VMEM_BYTES = 32 << 20
FULL_VMEM_BYTES = 60 << 20
TILE_VMEM_BYTES = 54 << 20
NT = (((1,), (1,)), ((), ()))
NN = (((1,), (0,)), ((), ()))


def exact_dot(first, second, dims):
    return lax.dot_general(
        first, second, dims, precision=HIGHEST_PRECISION, preferred_element_type=jnp.float32
    )


def call(kernel, out_shapes, name):
    return pl.pallas_call(
        kernel,
        out_shape=[jax.ShapeDtypeStruct(shape, jnp.float32) for shape in out_shapes],
        compiler_params=pltpu.CompilerParams(vmem_limit_bytes=VMEM_BYTES),
        name=name,
    )


def block(array, index):
    return array[:, index * LANES : (index + 1) * LANES]


def stage_kernel(vectors_hbm, hvectors_hbm, slots_ref, stack_ref, arrived):
    copies = [
        pltpu.make_async_copy(source, stack_ref.at[index], arrived.at[index])
        for index, source in enumerate((vectors_hbm, hvectors_hbm))
    ]
    for copy in copies:
        copy.start()
    for copy in copies:
        copy.wait()
    vectors = stack_ref[0]
    hvectors = stack_ref[1]
    members = vectors.shape[0]
    top = jnp.sum(vectors * hvectors, axis=1, keepdims=True)
    bottom = jnp.sum(vectors * vectors, axis=1, keepdims=True)
    lane = lax.broadcasted_iota(jnp.int32, (members, LANES), 1)
    line = lax.broadcasted_iota(jnp.int32, (members, LANES), 0)
    spread = jnp.where(lane == line, top, 0.0) + jnp.where(lane == line + members, bottom, 0.0)
    sums = jnp.sum(spread, axis=0, keepdims=True)
    slots_ref[...] = jnp.broadcast_to(sums, slots_ref.shape)


def prepare_kernel(
    rows_ref,
    cols_ref,
    vectors_hbm,
    previous_hbm,
    hvectors_hbm,
    hprevious_hbm,
    rows_out_ref,
    cols_out_ref,
    basis_ref,
    images_ref,
    arrived,
):
    copies = [
        pltpu.make_async_copy(source, target.at[place], arrived.at[index])
        for index, (source, target, place) in enumerate(
            (
                (vectors_hbm, basis_ref, 0),
                (previous_hbm, basis_ref, 1),
                (hvectors_hbm, images_ref, 0),
                (hprevious_hbm, images_ref, 1),
            )
        )
    ]
    for copy in copies:
        copy.start()
    rows = rows_ref[...]
    core = lax.rem(lax.axis_index("col"), 2)
    chips = lax.axis_size("col") // 2
    blocks = basis_ref.shape[2] // LANES
    index, peer = rows % blocks, rows // blocks
    other = jnp.where(peer % 2 == core, 0, 1)
    rows_out_ref[...] = (other * chips + peer // 2) * blocks + index
    cols = cols_ref[...]
    half = lax.rem(lax.axis_index("row"), 2)
    lines = lax.axis_size("row") // 2
    index, peer = cols % blocks, cols // blocks
    other = jnp.where(peer % 2 == half, 0, 1)
    cols_out_ref[...] = (other * lines + peer // 2) * blocks + index
    for copy in copies:
        copy.wait()


def residual_kernel(sums_ref, basis_ref, images_ref, residual_ref, slots_ref):
    members = basis_ref.shape[1]
    sums = jnp.sum(sums_ref[...], axis=0, keepdims=True)
    lane = lax.broadcasted_iota(jnp.int32, (members, LANES), 1)
    line = lax.broadcasted_iota(jnp.int32, (members, LANES), 0)
    top = jnp.sum(jnp.where(lane == line, sums, 0.0), axis=1, keepdims=True)
    bottom = jnp.sum(jnp.where(lane == line + members, sums, 0.0), axis=1, keepdims=True)
    residual = images_ref[0] - (top / (bottom + EPSILON)) * basis_ref[0]
    residual_ref[...] = residual
    blocks = residual.shape[1] // LANES
    for index in range(blocks):
        for slot in range(slots_ref.shape[0]):
            slots_ref[slot, index] = block(residual, index)
    basis = jnp.concatenate([basis_ref[0], residual, basis_ref[1]], axis=0)
    gram = exact_dot(basis, basis, NT)
    early = exact_dot(jnp.concatenate([images_ref[0], images_ref[1]], axis=0), basis, NT)
    extra = [
        gram[:members],
        gram[members : 2 * members],
        gram[2 * members :],
        early[:members],
        early[members:],
    ]
    for index, part in enumerate(pack_rows(extra)):
        for slot in range(slots_ref.shape[0]):
            slots_ref[slot, blocks + index] = part


def line_kernel(first_ref, second_ref, third_ref, fourth_ref, line_ref):
    lines, blocks = line_ref.shape[:2]
    here = lax.axis_index("row") // 2
    for shift, piece_ref in enumerate((first_ref, second_ref, third_ref, fourth_ref)):
        place = lax.rem(here + lines - shift, lines)
        for index in range(blocks):
            line_ref[place, index] = piece_ref[:, index * LANES : (index + 1) * LANES]


def halves_kernel(own_ref, received_ref, first_ref, second_ref, third_ref, fourth_ref):
    here = lax.axis_index("row") // 2
    outputs = (first_ref, second_ref, third_ref, fourth_ref)
    lines = len(outputs)
    blocks = (own_ref.shape[0] - first_ref.shape[0]) // (lines - 1)
    for shift, out_ref in enumerate(outputs):
        start = lax.rem(here + shift, lines) * blocks
        for index in range(blocks):
            out_ref[index] = own_ref[start + index] + received_ref[start + index]
        for index in range(out_ref.shape[0] - blocks):
            tail = lines * blocks + index
            out_ref[blocks + index] = own_ref[tail] + received_ref[tail]


def pack_rows(parts):
    first, second, third, fourth, fifth = parts
    members = first.shape[0]
    pieces = [fifth[:, i * members : (i + 1) * members] for i in range(3)]
    zero = jnp.zeros((members, members), jnp.float32)
    return [
        jnp.concatenate([first, second, pieces[0], pieces[1]], axis=1),
        jnp.concatenate([third, fourth, pieces[2], zero], axis=1),
    ]


def unpack_rows(one, two):
    members = one.shape[0]
    wide = 3 * members
    fifth = jnp.concatenate([one[:, 2 * wide :], two[:, 2 * wide : 2 * wide + members]], axis=1)
    return [one[:, :wide], one[:, wide : 2 * wide], two[:, :wide], two[:, wide : 2 * wide], fifth]


def sum_peers(parts_ref, index):
    part = parts_ref[0, index]
    for peer in range(1, parts_ref.shape[0]):
        part = part + parts_ref[peer, index]
    return part


def factor_kernel(first_ref, second_ref, third_ref, fourth_ref, inverse_ref, early_ref):
    parts = [part_ref[first_ref.shape[0] - 2 :] for part_ref in (first_ref, second_ref, third_ref, fourth_ref)]
    sums = parts[0] + parts[1] + parts[2] + parts[3]
    extras = [sums[0], sums[1]]
    members = extras[0].shape[0]
    order = 3 * members
    first, second, third, fourth, fifth = unpack_rows(*extras)
    early_ref[...] = jnp.concatenate([fourth, fifth], axis=0)
    gram = jnp.concatenate([first, second, third], axis=0)
    line = lax.broadcasted_iota(jnp.int32, (order, order), 0)
    lane = lax.broadcasted_iota(jnp.int32, (order, order), 1)
    work = jnp.concatenate([gram, jnp.where(line == lane, 1.0, 0.0)], axis=1)
    rows = lax.broadcasted_iota(jnp.int32, (order, 1), 0)
    for step in range(order):
        pivot = work[step : step + 1, step : step + 1]
        scale = lax.rsqrt(pivot)
        scale = scale * (1.5 - 0.5 * pivot * scale * scale)
        lead = work[step : step + 1, :] * scale
        column = work[:, step : step + 1] * scale
        work = jnp.where(rows == step, lead, jnp.where(rows > step, work - column * lead, work))
    inverse_ref[...] = work[:, order:]


def orthonormal_kernel(inverse_ref, basis_ref, residual_ref, out_ref, *, row_scale):
    rows = jnp.concatenate([basis_ref[0], residual_ref[...], basis_ref[1]], axis=0)
    out_ref[...] = exact_dot(inverse_ref[...] * row_scale, rows, NN)


def orthonormal_image_kernel(inverse_ref, images_ref, image_ref, out_ref, *, row_scale):
    rows = jnp.concatenate([images_ref[0], image_ref[...], images_ref[1]], axis=0)
    out_ref[...] = exact_dot(inverse_ref[...] * row_scale, rows, NN)


def image_kernel(
    col_parts_ref,
    first_ref,
    second_ref,
    third_ref,
    fourth_ref,
    basis_ref,
    residual_ref,
    image_ref,
    slots_ref,
):
    blocks = image_ref.shape[1] // LANES
    for index in range(blocks):
        part = first_ref[index] + second_ref[index] + third_ref[index] + fourth_ref[index]
        image_ref[:, index * LANES : (index + 1) * LANES] = sum_peers(col_parts_ref, index) + part
    basis = jnp.concatenate([basis_ref[0], residual_ref[...], basis_ref[1]], axis=0)
    late = exact_dot(image_ref[...], basis, NT)
    half = late.shape[0] // 2
    pad = jnp.zeros((half, LANES // 2 - late.shape[1]), jnp.float32)
    packed = jnp.concatenate([late[:half], pad, late[half:], pad], axis=1)
    slots_ref[...] = jnp.broadcast_to(packed[None], slots_ref.shape)


def projected_kernel(received_ref, inverse_ref, early_ref, projected_ref):
    packed = jnp.sum(received_ref[...], axis=0)
    early = early_ref[...]
    members = early.shape[0] // 2
    wide = early.shape[1]
    half = LANES // 2
    late = jnp.concatenate([packed[:, :wide], packed[:, half : half + wide]], axis=0)
    mixed_t = jnp.concatenate([early[:members], late, early[members:]], axis=0)
    inverse = inverse_ref[...]
    half_done = exact_dot(inverse, mixed_t, NT)
    projected_ref[...] = exact_dot(half_done, inverse, NT)


def split_blocks(x_ref, split_ref, start, per_peer):
    def split(peer, carry):
        for index in range(per_peer):
            value = x_ref[peer, index]
            high = value.astype(jnp.bfloat16)
            low = (value - high.astype(jnp.float32)).astype(jnp.bfloat16)
            split_ref[start + peer * per_peer + index] = jnp.concatenate([high, low], axis=0)
        return carry

    lax.fori_loop(0, x_ref.shape[0], split, 0)


def group_size(slots):
    return math.gcd(slots, 24)


def group_count(count_ref, slots):
    return (jnp.minimum(count_ref[0, 0], slots) + group_size(slots) - 1) // group_size(slots)


def group_copy(tiles_hbm, tiles_ref, arrived, counter):
    size = group_size(tiles_ref.shape[0])
    part = pl.ds(counter * size, size)
    return pltpu.make_async_copy(tiles_hbm.at[part], tiles_ref.at[part], arrived.at[counter])


def start_tiles(count_ref, tiles_hbm, tiles_ref, arrived):
    def start(counter, carry):
        group_copy(tiles_hbm, tiles_ref, arrived, counter).start()
        return carry

    lax.fori_loop(0, group_count(count_ref, tiles_ref.shape[0]), start, 0)


def tile_groups(
    count_ref, tiles_hbm, tiles_ref, arrived, split_ref, out_ref, source_of, target_of, dims
):
    slots = tiles_ref.shape[0]
    unroll = group_size(slots)
    live = count_ref[0, 0]
    members = split_ref.shape[1] // 2

    def group(counter, carry):
        group_copy(tiles_hbm, tiles_ref, arrived, counter).wait()
        base = counter * unroll
        products = []
        for offset in range(unroll):
            slot = base + offset
            product = lax.dot_general(
                split_ref[source_of(slot)], tiles_ref[slot], dims, preferred_element_type=jnp.float32
            )
            product = product[:members] + product[members:]
            products.append(jnp.where(slot < live, product, 0.0))
        for offset in range(unroll):
            target = target_of(base + offset)
            out_ref[target] = out_ref[target] + products[offset]
        return carry

    lax.fori_loop(0, group_count(count_ref, slots), group, 0)


def backward_kernel(
    count_ref,
    rows_ref,
    cols_ref,
    tiles_hbm,
    own_ref,
    other_ref,
    own_out_ref,
    other_out_ref,
    tiles_ref,
    arrived,
    split_ref,
    totals_ref,
):
    start_tiles(count_ref, tiles_hbm, tiles_ref, arrived)
    peers, width = own_ref.shape[:2]
    per_peer = split_ref.shape[0] // (2 * peers)
    half = totals_ref.shape[0] // 2
    totals_ref[...] = jnp.zeros_like(totals_ref)
    split_blocks(own_ref, split_ref, 0, per_peer)
    split_blocks(other_ref, split_ref, peers * per_peer, per_peer)
    for index in range(width - per_peer):
        part = sum_peers(own_ref, per_peer + index) + sum_peers(other_ref, per_peer + index)
        own_out_ref[half + index] = part
        other_out_ref[half + index] = part
    tile_groups(
        count_ref,
        tiles_hbm,
        tiles_ref,
        arrived,
        split_ref,
        totals_ref,
        lambda slot: rows_ref[0, 0, slot],
        lambda slot: cols_ref[0, 0, slot],
        NN,
    )
    own_out_ref[:half] = totals_ref[:half]
    other_out_ref[:half] = totals_ref[half:]


def forward_kernel(
    count_ref,
    rows_ref,
    cols_ref,
    tiles_hbm,
    line_ref,
    far_line_ref,
    own_ref,
    other_ref,
    tiles_ref,
    arrived,
    split_ref,
    totals_ref,
):
    start_tiles(count_ref, tiles_hbm, tiles_ref, arrived)
    totals_ref[...] = jnp.zeros_like(totals_ref)
    lines, blocks = line_ref.shape[:2]
    split_blocks(line_ref, split_ref, 0, blocks)
    split_blocks(far_line_ref, split_ref, lines * blocks, blocks)
    tile_groups(
        count_ref,
        tiles_hbm,
        tiles_ref,
        arrived,
        split_ref,
        totals_ref,
        lambda slot: cols_ref[0, 0, slot],
        lambda slot: rows_ref[0, 0, slot],
        NT,
    )
    half = totals_ref.shape[0] // 2
    own_ref[...] = totals_ref[:half]
    other_ref[...] = totals_ref[half:]


def tile_call(kernel, count, rows, cols, tiles, arrays, out_shapes, scratch, name):
    smem = pl.BlockSpec(memory_space=pltpu.SMEM)
    vmem = pl.BlockSpec(memory_space=pltpu.VMEM)
    return pl.pallas_call(
        kernel,
        out_shape=[jax.ShapeDtypeStruct(shape, jnp.float32) for shape in out_shapes],
        in_specs=[smem] * 3 + [pl.BlockSpec(memory_space=pl.ANY)] + [vmem] * len(arrays),
        out_specs=[vmem] * len(out_shapes),
        scratch_shapes=[
            pltpu.VMEM(tiles.shape, tiles.dtype),
            pltpu.SemaphoreType.DMA((tiles.shape[0] // group_size(tiles.shape[0]),)),
        ]
        + scratch,
        compiler_params=pltpu.CompilerParams(vmem_limit_bytes=TILE_VMEM_BYTES),
        name=name,
    )(count, rows, cols, tiles, *arrays)


def exchange(slots, axes, groups=None):
    return lax.all_to_all(slots, axes, 0, 0, axis_index_groups=groups, tiled=True)


def swap(array, axis, distance):
    return lax.ppermute(array, axis, [(i, i ^ distance) for i in range(lax.axis_size(axis))])


def shift_lines(array, shift):
    size = lax.axis_size("row")
    return lax.ppermute(array, "row", [(i, (i + 2 * shift) % size) for i in range(size)])


def on_device(
    tile_blocks, tile_rows, tile_cols, tile_count, vectors, hvectors, previous, hprevious
):
    n_row = lax.axis_size("row")
    n_col = lax.axis_size("col")
    everyone = ("row", "col")
    chips = n_col // 2
    core_groups = [[2 * chip + core for chip in range(chips)] for core in (0, 1)]
    members, piece = vectors.shape
    blocks = piece // LANES
    lines = n_row // 2
    order = 3 * members
    tiles = tile_blocks[0, 0]
    row_scale = math.sqrt(piece * n_row * n_col)
    f32 = jnp.float32

    hbm_spec = pl.BlockSpec(memory_space=pl.ANY)
    vmem_spec = pl.BlockSpec(memory_space=pltpu.VMEM)
    params = pltpu.CompilerParams(vmem_limit_bytes=VMEM_BYTES)
    (sums,) = pl.pallas_call(
        stage_kernel,
        out_shape=[jax.ShapeDtypeStruct((n_row * n_col, LANES), f32)],
        in_specs=[hbm_spec, hbm_spec],
        out_specs=[vmem_spec],
        scratch_shapes=[
            pltpu.VMEM((2, members, piece), f32),
            pltpu.SemaphoreType.DMA((2,)),
        ],
        compiler_params=pltpu.CompilerParams(vmem_limit_bytes=FULL_VMEM_BYTES),
        name="stage",
    )(vectors, hvectors)
    rows, cols, basis, images = pl.pallas_call(
        prepare_kernel,
        out_shape=[
            jax.ShapeDtypeStruct(tile_rows.shape, jnp.int32),
            jax.ShapeDtypeStruct(tile_cols.shape, jnp.int32),
            jax.ShapeDtypeStruct((2, members, piece), f32),
            jax.ShapeDtypeStruct((2, members, piece), f32),
        ],
        in_specs=[vmem_spec] * 2 + [hbm_spec] * 4,
        out_specs=[vmem_spec] * 4,
        scratch_shapes=[pltpu.SemaphoreType.DMA((4,))],
        compiler_params=params,
        name="prepare",
    )(tile_rows, tile_cols, vectors, previous, hvectors, hprevious)
    sums = exchange(sums, everyone)
    sums, rows, cols, basis, images = lax.optimization_barrier((sums, rows, cols, basis, images))
    residual, slots = call(
        residual_kernel, [(members, piece), (chips, blocks + 2, members, LANES)], "residual"
    )(sums, basis, images)
    pieces = [residual] + [shift_lines(residual, shift) for shift in range(1, lines)]
    (line,) = call(line_kernel, [(lines, blocks, members, LANES)], "line")(*pieces)
    own_range = exchange(slots, "col", core_groups)
    own_range, line = lax.optimization_barrier((own_range, line))
    far_line = swap(line, "row", 1)
    other_range = swap(own_range, "col", 1)
    half = (lines * blocks + 2, members, LANES)
    col_own, col_other = tile_call(
        backward_kernel,
        tile_count,
        rows,
        cols,
        tiles,
        (own_range, other_range),
        [half, half],
        [
            pltpu.VMEM((n_col * blocks, 2 * members, LANES), jnp.bfloat16),
            pltpu.VMEM((n_row * blocks, members, LANES), f32),
        ],
        "backward_tiles",
    )
    col_own, col_other, far_line = lax.optimization_barrier((col_own, col_other, far_line))
    col_received = swap(col_other, "row", 1)
    half = (chips * blocks, members, LANES)
    own_totals, other_totals = tile_call(
        forward_kernel,
        tile_count,
        rows,
        cols,
        tiles,
        (line, far_line),
        [half, half],
        [
            pltpu.VMEM((n_row * blocks, 2 * members, LANES), jnp.bfloat16),
            pltpu.VMEM((n_col * blocks, members, LANES), f32),
        ],
        "forward_tiles",
    )
    col_received, own_totals, other_totals = lax.optimization_barrier(
        (col_received, own_totals, other_totals)
    )
    totals = own_totals + swap(other_totals, "col", 1)
    col_parts = exchange(totals.reshape(chips, blocks, members, LANES), "col", core_groups)
    outs = call(halves_kernel, [(blocks + 2, members, LANES)] * lines, "halves")(
        col_own, col_received
    )
    row_parts = [outs[0]] + [shift_lines(outs[shift], shift) for shift in range(1, lines)]
    col_parts, *row_parts = lax.optimization_barrier((col_parts, *row_parts))
    image, slots = call(
        image_kernel, [(members, piece), (n_row * n_col, members // 2, LANES)], "image"
    )(col_parts, *row_parts, basis, residual)
    late = exchange(slots, everyone)
    image, *row_parts = lax.optimization_barrier((image, *row_parts))
    inverse, early = call(factor_kernel, [(order, order), (2 * members, order)], "factor")(*row_parts)
    (orthonormal,) = call(
        functools.partial(orthonormal_kernel, row_scale=row_scale), [(order, piece)], "orthonormal"
    )(inverse, basis, residual)
    (orthonormal_image,) = call(
        functools.partial(orthonormal_image_kernel, row_scale=row_scale),
        [(order, piece)],
        "orthonormal_image",
    )(inverse, images, image)
    (projected,) = call(projected_kernel, [(order, order)], "projected")(late, inverse, early)
    return (orthonormal, orthonormal_image, projected)


def solution(mesh):
    in_specs = (
        P("row", "col", None, None, None),
        P("row", "col", None),
        P("row", "col", None),
        P("row", "col"),
        P(None, ("row", "col")),
        P(None, ("row", "col")),
        P(None, ("row", "col")),
        P(None, ("row", "col")),
    )
    out_specs = (P(None, ("row", "col")), P(None, ("row", "col")), P())
    return jax.shard_map(
        on_device, mesh=mesh, in_specs=in_specs, out_specs=out_specs, check_vma=False
    )
```

```python
import functools
import math

import jax
import jax.numpy as jnp
from jax import lax
from jax.experimental import pallas as pl
from jax.experimental.pallas import tpu as pltpu
from jax.sharding import PartitionSpec as P

EPSILON = 1e-06
HIGHEST_PRECISION = lax.Precision.HIGHEST
LANES = 128
VMEM_BYTES = 32 << 20
FULL_VMEM_BYTES = 60 << 20
TILE_VMEM_BYTES = 48<<20
GROUP = 64
NT = (((1,), (1,)), ((), ()))
NN = (((1,), (0,)), ((), ()))


def exact_dot(first, second, dims):
    return lax.dot_general(
        first, second, dims, precision=HIGHEST_PRECISION, preferred_element_type=jnp.float32
    )


def call(kernel, out_shapes, name):
    return pl.pallas_call(
        kernel,
        out_shape=[jax.ShapeDtypeStruct(shape, jnp.float32) for shape in out_shapes],
        compiler_params=pltpu.CompilerParams(vmem_limit_bytes=VMEM_BYTES),
        name=name,
    )


def block(array, index):
    return array[:, index * LANES : (index + 1) * LANES]


def stage_kernel(vectors_hbm, hvectors_hbm, slots_ref, stack_ref, arrived):
    copies = [
        pltpu.make_async_copy(source, stack_ref.at[index], arrived.at[index])
        for index, source in enumerate((vectors_hbm, hvectors_hbm))
    ]
    for copy in copies:
        copy.start()
    for copy in copies:
        copy.wait()
    vectors = stack_ref[0]
    hvectors = stack_ref[1]
    members = vectors.shape[0]
    top = jnp.sum(vectors * hvectors, axis=1, keepdims=True)
    bottom = jnp.sum(vectors * vectors, axis=1, keepdims=True)
    lane = lax.broadcasted_iota(jnp.int32, (members, LANES), 1)
    line = lax.broadcasted_iota(jnp.int32, (members, LANES), 0)
    spread = jnp.where(lane == line, top, 0.0) + jnp.where(lane == line + members, bottom, 0.0)
    sums = jnp.sum(spread, axis=0, keepdims=True)
    slots_ref[...] = jnp.broadcast_to(sums, slots_ref.shape)


def prepare_kernel(
    vectors_hbm, previous_hbm, hvectors_hbm, hprevious_hbm, basis_ref, images_ref, arrived
):
    copies = [
        pltpu.make_async_copy(source, target.at[place], arrived.at[index])
        for index, (source, target, place) in enumerate(
            (
                (vectors_hbm, basis_ref, 0),
                (previous_hbm, basis_ref, 1),
                (hvectors_hbm, images_ref, 0),
                (hprevious_hbm, images_ref, 1),
            )
        )
    ]
    for copy in copies:
        copy.start()
    for copy in copies:
        copy.wait()


def places_kernel(rows_ref, cols_ref, rows_out_ref, cols_out_ref, *, blocks, gap):
    chips = lax.axis_size("col") // 2
    lines = lax.axis_size("row") // 2
    core = lax.rem(lax.axis_index("col"), 2)
    rows = rows_ref[...]
    index, peer = rows % blocks, rows // blocks
    other = jnp.where(peer % 2 == core, 0, 1)
    rows_out_ref[...] = (other * chips + peer // 2) * blocks + index
    half = lax.rem(lax.axis_index("row"), 2)
    cols = cols_ref[...]
    index, peer = cols % blocks, cols // blocks
    other = jnp.where(peer % 2 == half, 0, 1)
    cols_out_ref[...] = (other * lines + peer // 2) * blocks + index + other * gap


def residual_kernel(sums_ref, basis_ref, images_ref, residual_ref, slots_ref):
    members = basis_ref.shape[1]
    sums = jnp.sum(sums_ref[...], axis=0, keepdims=True)
    lane = lax.broadcasted_iota(jnp.int32, (members, LANES), 1)
    line = lax.broadcasted_iota(jnp.int32, (members, LANES), 0)
    top = jnp.sum(jnp.where(lane == line, sums, 0.0), axis=1, keepdims=True)
    bottom = jnp.sum(jnp.where(lane == line + members, sums, 0.0), axis=1, keepdims=True)
    residual = images_ref[0] - (top / (bottom + EPSILON)) * basis_ref[0]
    residual_ref[...] = residual
    blocks = residual.shape[1] // LANES
    for index in range(blocks):
        for slot in range(slots_ref.shape[0]):
            slots_ref[slot, index] = block(residual, index)
    basis = jnp.concatenate([basis_ref[0], residual, basis_ref[1]], axis=0)
    gram = exact_dot(basis, basis, NT)
    early = exact_dot(jnp.concatenate([images_ref[0], images_ref[1]], axis=0), basis, NT)
    extra = [
        gram[:members],
        gram[members : 2 * members],
        gram[2 * members :],
        early[:members],
        early[members:],
    ]
    for index, part in enumerate(pack_rows(extra)):
        for slot in range(slots_ref.shape[0]):
            slots_ref[slot, blocks + index] = part


def line_kernel(first_ref, second_ref, third_ref, fourth_ref, line_ref):
    lines, blocks = line_ref.shape[:2]
    here = lax.axis_index("row") // 2
    for shift, piece_ref in enumerate((first_ref, second_ref, third_ref, fourth_ref)):
        place = lax.rem(here + lines - shift, lines)
        for index in range(blocks):
            line_ref[place, index] = piece_ref[:, index * LANES : (index + 1) * LANES]


def halves_kernel(own_ref, received_ref, first_ref, second_ref, third_ref, fourth_ref):
    here = lax.axis_index("row") // 2
    outputs = (first_ref, second_ref, third_ref, fourth_ref)
    lines = len(outputs)
    blocks = (own_ref.shape[0] - first_ref.shape[0]) // (lines - 1)
    for shift, out_ref in enumerate(outputs):
        start = lax.rem(here + shift, lines) * blocks
        for index in range(blocks):
            out_ref[index] = own_ref[start + index] + received_ref[start + index]
        for index in range(out_ref.shape[0] - blocks):
            tail = lines * blocks + index
            out_ref[blocks + index] = own_ref[tail] + received_ref[tail]


def pack_rows(parts):
    first, second, third, fourth, fifth = parts
    members = first.shape[0]
    pieces = [fifth[:, i * members : (i + 1) * members] for i in range(3)]
    zero = jnp.zeros((members, members), jnp.float32)
    return [
        jnp.concatenate([first, second, pieces[0], pieces[1]], axis=1),
        jnp.concatenate([third, fourth, pieces[2], zero], axis=1),
    ]


def unpack_rows(one, two):
    members = one.shape[0]
    wide = 3 * members
    fifth = jnp.concatenate([one[:, 2 * wide :], two[:, 2 * wide : 2 * wide + members]], axis=1)
    return [one[:, :wide], one[:, wide : 2 * wide], two[:, :wide], two[:, wide : 2 * wide], fifth]


def sum_peers(parts_ref, index):
    part = parts_ref[0, index]
    for peer in range(1, parts_ref.shape[0]):
        part = part + parts_ref[peer, index]
    return part


def factor_kernel(first_ref, second_ref, third_ref, fourth_ref, inverse_ref, early_ref):
    parts = [part_ref[first_ref.shape[0] - 2 :] for part_ref in (first_ref, second_ref, third_ref, fourth_ref)]
    sums = parts[0] + parts[1] + parts[2] + parts[3]
    extras = [sums[0], sums[1]]
    members = extras[0].shape[0]
    order = 3 * members
    first, second, third, fourth, fifth = unpack_rows(*extras)
    early_ref[...] = jnp.concatenate([fourth, fifth], axis=0)
    gram = jnp.concatenate([first, second, third], axis=0)
    line = lax.broadcasted_iota(jnp.int32, (order, order), 0)
    lane = lax.broadcasted_iota(jnp.int32, (order, order), 1)
    work = jnp.concatenate([gram, jnp.where(line == lane, 1.0, 0.0)], axis=1)
    rows = lax.broadcasted_iota(jnp.int32, (order, 1), 0)
    for step in range(order):
        pivot = work[step : step + 1, step : step + 1]
        scale = lax.rsqrt(pivot)
        scale = scale * (1.5 - 0.5 * pivot * scale * scale)
        lead = work[step : step + 1, :] * scale
        column = work[:, step : step + 1] * scale
        work = jnp.where(rows == step, lead, jnp.where(rows > step, work - column * lead, work))
    inverse_ref[...] = work[:, order:]


def orthonormal_kernel(inverse_ref, basis_ref, residual_ref, out_ref, *, row_scale):
    rows = jnp.concatenate([basis_ref[0], residual_ref[...], basis_ref[1]], axis=0)
    out_ref[...] = exact_dot(inverse_ref[...] * row_scale, rows, NN)


def orthonormal_image_kernel(inverse_ref, images_ref, image_ref, out_ref, *, row_scale):
    rows = jnp.concatenate([images_ref[0], image_ref[...], images_ref[1]], axis=0)
    out_ref[...] = exact_dot(inverse_ref[...] * row_scale, rows, NN)


def image_kernel(
    col_parts_ref,
    first_ref,
    second_ref,
    third_ref,
    fourth_ref,
    basis_ref,
    residual_ref,
    image_ref,
    slots_ref,
):
    blocks = image_ref.shape[1] // LANES
    for index in range(blocks):
        part = first_ref[index] + second_ref[index] + third_ref[index] + fourth_ref[index]
        image_ref[:, index * LANES : (index + 1) * LANES] = sum_peers(col_parts_ref, index) + part
    basis = jnp.concatenate([basis_ref[0], residual_ref[...], basis_ref[1]], axis=0)
    late = exact_dot(image_ref[...], basis, NT)
    half = late.shape[0] // 2
    pad = jnp.zeros((half, LANES // 2 - late.shape[1]), jnp.float32)
    packed = jnp.concatenate([late[:half], pad, late[half:], pad], axis=1)
    slots_ref[...] = jnp.broadcast_to(packed[None], slots_ref.shape)


def projected_kernel(received_ref, inverse_ref, early_ref, projected_ref):
    packed = jnp.sum(received_ref[...], axis=0)
    early = early_ref[...]
    members = early.shape[0] // 2
    wide = early.shape[1]
    half = LANES // 2
    late = jnp.concatenate([packed[:, :wide], packed[:, half : half + wide]], axis=0)
    mixed_t = jnp.concatenate([early[:members], late, early[members:]], axis=0)
    inverse = inverse_ref[...]
    half_done = exact_dot(inverse, mixed_t, NT)
    projected_ref[...] = exact_dot(half_done, inverse, NT)


def split_blocks(x_ref, split_ref, start, per_peer):
    def split(peer, carry):
        for index in range(per_peer):
            value = x_ref[peer, index]
            high = value.astype(jnp.bfloat16)
            low = (value - high.astype(jnp.float32)).astype(jnp.bfloat16)
            split_ref[start + peer * per_peer + index] = jnp.concatenate([high, low], axis=0)
        return carry

    lax.fori_loop(0, x_ref.shape[0], split, 0)


def group_size(slots):
    return math.gcd(slots, GROUP)


def group_count(live, slots):
    return (jnp.minimum(live, slots) + group_size(slots) - 1) // group_size(slots)


def group_copy(tiles_hbm, tiles_ref, arrived, counter):
    size = group_size(tiles_ref.shape[0])
    part = pl.ds(counter * size, size)
    return pltpu.make_async_copy(tiles_hbm.at[part], tiles_ref.at[part], arrived.at[counter])


def tile_kernel(
    count_ref,
    rows_hbm,
    cols_hbm,
    tiles_hbm,
    own_ref,
    other_ref,
    own_out_hbm,
    other_out_hbm,
    rows_ref,
    cols_ref,
    tiles_ref,
    split_ref,
    totals_ref,
    arrived,
    moved,
    *,
    forward,
):
    slots = tiles_ref.shape[0]
    live = count_ref[0, 0]
    rows_copy = pltpu.make_async_copy(rows_hbm, rows_ref, moved.at[2])
    cols_copy = pltpu.make_async_copy(cols_hbm, cols_ref, moved.at[3])
    for copy in (rows_copy, cols_copy):
        copy.start()

    def start(counter, carry):
        group_copy(tiles_hbm, tiles_ref, arrived, counter).start()
        return carry

    lax.fori_loop(0, group_count(live, slots), start, 0)
    totals_ref[...] = jnp.zeros_like(totals_ref)
    peers = own_ref.shape[0]
    split_half = split_ref.shape[0] // 2
    blocks = split_half // peers if forward else own_ref.shape[1] - 2
    half = totals_ref.shape[0] // 2
    split_blocks(own_ref, split_ref, 0, blocks)
    split_blocks(other_ref, split_ref, split_half, blocks)
    if not forward:
        extra = own_ref.shape[1] - blocks
        for index in range(extra):
            part = sum_peers(own_ref, blocks + index) + sum_peers(other_ref, blocks + index)
            totals_ref[half - extra + index] = part
            totals_ref[2 * half - extra + index] = part
    rows_copy.wait()
    cols_copy.wait()
    unroll = group_size(slots)
    members = split_ref.shape[1] // 2
    source_ref, target_ref = (cols_ref, rows_ref) if forward else (rows_ref, cols_ref)

    def group(counter, carry):
        group_copy(tiles_hbm, tiles_ref, arrived, counter).wait()
        base = counter * unroll
        products = []
        for offset in range(unroll):
            slot = base + offset
            product = lax.dot_general(
                split_ref[source_ref[0, 0, slot]],
                tiles_ref[slot],
                NT if forward else NN,
                preferred_element_type=jnp.float32,
            )
            product = product[:members] + product[members:]
            products.append(jnp.where(slot < live, product, 0.0))
        for offset in range(unroll):
            target = target_ref[0, 0, base + offset]
            totals_ref[target] = totals_ref[target] + products[offset]
        return carry

    lax.fori_loop(0, group_count(live, slots), group, 0)
    outs = [
        pltpu.make_async_copy(totals_ref.at[pl.ds(start, half)], out, moved.at[index])
        for index, (start, out) in enumerate(((0, own_out_hbm), (half, other_out_hbm)))
    ]
    for copy in outs:
        copy.start()
    for copy in outs:
        copy.wait()


def tile_call(count, rows, cols, tiles, own, other, split_places, out_places, forward):
    smem = pl.BlockSpec(memory_space=pltpu.SMEM)
    anywhere = pl.BlockSpec(memory_space=pl.ANY)
    members = own.shape[2]
    slots = tiles.shape[0]
    out = jax.ShapeDtypeStruct((out_places, members, LANES), jnp.float32)
    return pl.pallas_call(
        functools.partial(tile_kernel, forward=forward),
        out_shape=[out, out],
        in_specs=[smem] + [anywhere] * 3 + [pl.BlockSpec(memory_space=pltpu.VMEM)] * 2,
        out_specs=[anywhere] * 2,
        scratch_shapes=[
            pltpu.SMEM(rows.shape, jnp.int32),
            pltpu.SMEM(cols.shape, jnp.int32),
            pltpu.VMEM(tiles.shape, tiles.dtype),
            pltpu.VMEM((2 * split_places, 2 * members, LANES), jnp.bfloat16),
            pltpu.VMEM((2 * out_places, members, LANES), jnp.float32),
            pltpu.SemaphoreType.DMA((slots // group_size(slots),)),
            pltpu.SemaphoreType.DMA((4,)),
        ],
        compiler_params=pltpu.CompilerParams(vmem_limit_bytes=TILE_VMEM_BYTES),
        name="forward_tiles" if forward else "backward_tiles",
    )(count, rows, cols, tiles, own, other)


def join_kernel(own_ref, other_ref, out_ref):
    out_ref[...] = own_ref[...] + other_ref[...]


def exchange(slots, axes, groups=None):
    return lax.all_to_all(slots, axes, 0, 0, axis_index_groups=groups, tiled=True)


def swap(array, axis, distance):
    return lax.ppermute(array, axis, [(i, i ^ distance) for i in range(lax.axis_size(axis))])


def shift_lines(array, shift):
    size = lax.axis_size("row")
    return lax.ppermute(array, "row", [(i, (i + 2 * shift) % size) for i in range(size)])


def on_device(
    tile_blocks, tile_rows, tile_cols, tile_count, vectors, hvectors, previous, hprevious
):
    n_row = lax.axis_size("row")
    n_col = lax.axis_size("col")
    everyone = ("row", "col")
    chips = n_col // 2
    core_groups = [[2 * chip + core for chip in range(chips)] for core in (0, 1)]
    members, piece = vectors.shape
    blocks = piece // LANES
    lines = n_row // 2
    order = 3 * members
    tiles = tile_blocks[0, 0]
    row_scale = math.sqrt(piece * n_row * n_col)
    f32 = jnp.float32

    hbm_spec = pl.BlockSpec(memory_space=pl.ANY)
    vmem_spec = pl.BlockSpec(memory_space=pltpu.VMEM)
    params = pltpu.CompilerParams(vmem_limit_bytes=VMEM_BYTES)
    (sums,) = pl.pallas_call(
        stage_kernel,
        out_shape=[jax.ShapeDtypeStruct((n_row * n_col, LANES), f32)],
        in_specs=[hbm_spec, hbm_spec],
        out_specs=[vmem_spec],
        scratch_shapes=[
            pltpu.VMEM((2, members, piece), f32),
            pltpu.SemaphoreType.DMA((2,)),
        ],
        compiler_params=pltpu.CompilerParams(vmem_limit_bytes=FULL_VMEM_BYTES),
        name="stage",
    )(vectors, hvectors)
    basis, images = pl.pallas_call(
        prepare_kernel,
        out_shape=[jax.ShapeDtypeStruct((2, members, piece), f32)] * 2,
        in_specs=[hbm_spec] * 4,
        out_specs=[vmem_spec] * 2,
        scratch_shapes=[pltpu.SemaphoreType.DMA((4,))],
        compiler_params=params,
        name="prepare",
    )(vectors, previous, hvectors, hprevious)
    sums = exchange(sums, everyone)
    sums, basis, images = lax.optimization_barrier((sums, basis, images))
    residual, slots = call(
        residual_kernel, [(members, piece), (chips, blocks + 2, members, LANES)], "residual"
    )(sums, basis, images)
    pieces = [residual] + [shift_lines(residual, shift) for shift in range(1, lines)]
    (line,) = call(line_kernel, [(lines, blocks, members, LANES)], "line")(*pieces)
    own_range = exchange(slots, "col", core_groups)
    residual, tile_rows, tile_cols = lax.optimization_barrier((residual, tile_rows, tile_cols))
    rows, cols = pl.pallas_call(
        functools.partial(places_kernel, blocks=blocks, gap=2),
        out_shape=[jax.ShapeDtypeStruct(tile_rows.shape, jnp.int32)] * 2,
        compiler_params=params,
        name="places",
    )(tile_rows, tile_cols)
    own_range, line, rows, cols = lax.optimization_barrier((own_range, line, rows, cols))
    far_line = swap(line, "row", 1)
    other_range = swap(own_range, "col", 1)
    col_own, col_other = tile_call(
        tile_count,
        rows,
        cols,
        tiles,
        own_range,
        other_range,
        chips * blocks,
        lines * blocks + 2,
        False,
    )
    col_own, col_other, far_line = lax.optimization_barrier((col_own, col_other, far_line))
    col_received = swap(col_other, "row", 1)
    own_totals, other_totals = tile_call(
        tile_count,
        rows,
        cols,
        tiles,
        line,
        far_line,
        lines * blocks + 2,
        chips * blocks,
        True,
    )
    col_received, own_totals, other_totals = lax.optimization_barrier(
        (col_received, own_totals, other_totals)
    )
    (totals,) = pl.pallas_call(
        join_kernel,
        out_shape=[jax.ShapeDtypeStruct(own_totals.shape, f32)],
        compiler_params=pltpu.CompilerParams(vmem_limit_bytes=TILE_VMEM_BYTES),
        name="join",
    )(own_totals, swap(other_totals, "col", 1))
    col_parts = exchange(totals.reshape(chips, blocks, members, LANES), "col", core_groups)
    outs = call(halves_kernel, [(blocks + 2, members, LANES)] * lines, "halves")(
        col_own, col_received
    )
    row_parts = [outs[0]] + [shift_lines(outs[shift], shift) for shift in range(1, lines)]
    col_parts, *row_parts = lax.optimization_barrier((col_parts, *row_parts))
    image, slots = call(
        image_kernel, [(members, piece), (n_row * n_col, members // 2, LANES)], "image"
    )(col_parts, *row_parts, basis, residual)
    late = exchange(slots, everyone)
    image, *row_parts = lax.optimization_barrier((image, *row_parts))
    inverse, early = call(factor_kernel, [(order, order), (2 * members, order)], "factor")(*row_parts)
    (orthonormal,) = call(
        functools.partial(orthonormal_kernel, row_scale=row_scale), [(order, piece)], "orthonormal"
    )(inverse, basis, residual)
    (orthonormal_image,) = call(
        functools.partial(orthonormal_image_kernel, row_scale=row_scale),
        [(order, piece)],
        "orthonormal_image",
    )(inverse, images, image)
    (projected,) = call(projected_kernel, [(order, order)], "projected")(late, inverse, early)
    return (orthonormal, orthonormal_image, projected)


def solution(mesh):
    in_specs = (
        P("row", "col", None, None, None),
        P("row", "col", None),
        P("row", "col", None),
        P("row", "col"),
        P(None, ("row", "col")),
        P(None, ("row", "col")),
        P(None, ("row", "col")),
        P(None, ("row", "col")),
    )
    out_specs = (P(None, ("row", "col")), P(None, ("row", "col")), P())
    return jax.shard_map(
        on_device, mesh=mesh, in_specs=in_specs, out_specs=out_specs, check_vma=False
    )
```

```python
import functools
import math

import jax
import jax.numpy as jnp
from jax import lax
from jax.experimental import pallas as pl
from jax.experimental.pallas import tpu as pltpu
from jax.sharding import PartitionSpec as P

EPSILON = 1e-06
HIGHEST_PRECISION = lax.Precision.HIGHEST
LANES = 128
VMEM_BYTES = 32 << 20
FULL_VMEM_BYTES = 60 << 20
TILE_VMEM_BYTES = 48<<20
GROUP = 64
NT = (((1,), (1,)), ((), ()))
NN = (((1,), (0,)), ((), ()))


def exact_dot(first, second, dims):
    return lax.dot_general(
        first, second, dims, precision=HIGHEST_PRECISION, preferred_element_type=jnp.float32
    )


def call(kernel, out_shapes, name):
    return pl.pallas_call(
        kernel,
        out_shape=[jax.ShapeDtypeStruct(shape, jnp.float32) for shape in out_shapes],
        compiler_params=pltpu.CompilerParams(vmem_limit_bytes=VMEM_BYTES),
        name=name,
    )


def block(array, index):
    return array[:, index * LANES : (index + 1) * LANES]


def stage_kernel(vectors_hbm, hvectors_hbm, slots_ref, stack_ref, arrived):
    copies = [
        pltpu.make_async_copy(source, stack_ref.at[index], arrived.at[index])
        for index, source in enumerate((vectors_hbm, hvectors_hbm))
    ]
    for copy in copies:
        copy.start()
    for copy in copies:
        copy.wait()
    vectors = stack_ref[0]
    hvectors = stack_ref[1]
    members = vectors.shape[0]
    top = jnp.sum(vectors * hvectors, axis=1, keepdims=True)
    bottom = jnp.sum(vectors * vectors, axis=1, keepdims=True)
    lane = lax.broadcasted_iota(jnp.int32, (members, LANES), 1)
    line = lax.broadcasted_iota(jnp.int32, (members, LANES), 0)
    spread = jnp.where(lane == line, top, 0.0) + jnp.where(lane == line + members, bottom, 0.0)
    sums = jnp.sum(spread, axis=0, keepdims=True)
    slots_ref[...] = jnp.broadcast_to(sums, slots_ref.shape)


def prepare_kernel(
    vectors_hbm, previous_hbm, hvectors_hbm, hprevious_hbm, basis_ref, images_ref, arrived
):
    copies = [
        pltpu.make_async_copy(source, target.at[place], arrived.at[index])
        for index, (source, target, place) in enumerate(
            (
                (vectors_hbm, basis_ref, 0),
                (previous_hbm, basis_ref, 1),
                (hvectors_hbm, images_ref, 0),
                (hprevious_hbm, images_ref, 1),
            )
        )
    ]
    for copy in copies:
        copy.start()
    for copy in copies:
        copy.wait()


def places_kernel(rows_ref, cols_ref, rows_out_ref, cols_out_ref, *, blocks, gap):
    chips = lax.axis_size("col") // 2
    lines = lax.axis_size("row") // 2
    core = lax.rem(lax.axis_index("col"), 2)
    rows = rows_ref[...]
    index, peer = rows % blocks, rows // blocks
    other = jnp.where(peer % 2 == core, 0, 1)
    rows_out_ref[...] = (other * chips + peer // 2) * blocks + index
    half = lax.rem(lax.axis_index("row"), 2)
    cols = cols_ref[...]
    index, peer = cols % blocks, cols // blocks
    other = jnp.where(peer % 2 == half, 0, 1)
    cols_out_ref[...] = (other * lines + peer // 2) * blocks + index + other * gap


def residual_kernel(sums_ref, basis_ref, images_ref, residual_ref, slots_ref):
    members = basis_ref.shape[1]
    sums = jnp.sum(sums_ref[...], axis=0, keepdims=True)
    lane = lax.broadcasted_iota(jnp.int32, (members, LANES), 1)
    line = lax.broadcasted_iota(jnp.int32, (members, LANES), 0)
    top = jnp.sum(jnp.where(lane == line, sums, 0.0), axis=1, keepdims=True)
    bottom = jnp.sum(jnp.where(lane == line + members, sums, 0.0), axis=1, keepdims=True)
    residual = images_ref[0] - (top / (bottom + EPSILON)) * basis_ref[0]
    residual_ref[...] = residual
    blocks = residual.shape[1] // LANES
    for index in range(blocks):
        for slot in range(slots_ref.shape[0]):
            slots_ref[slot, index] = block(residual, index)
    basis = jnp.concatenate([basis_ref[0], residual, basis_ref[1]], axis=0)
    gram = exact_dot(basis, basis, NT)
    early = exact_dot(jnp.concatenate([images_ref[0], images_ref[1]], axis=0), basis, NT)
    extra = [
        gram[:members],
        gram[members : 2 * members],
        gram[2 * members :],
        early[:members],
        early[members:],
    ]
    for index, part in enumerate(pack_rows(extra)):
        for slot in range(slots_ref.shape[0]):
            slots_ref[slot, blocks + index] = part


def line_kernel(first_ref, second_ref, third_ref, fourth_ref, line_ref):
    lines, blocks = line_ref.shape[:2]
    here = lax.axis_index("row") // 2
    for shift, piece_ref in enumerate((first_ref, second_ref, third_ref, fourth_ref)):
        place = lax.rem(here + lines - shift, lines)
        for index in range(blocks):
            line_ref[place, index] = piece_ref[:, index * LANES : (index + 1) * LANES]


def halves_kernel(own_ref, received_ref, first_ref, second_ref, third_ref, fourth_ref):
    here = lax.axis_index("row") // 2
    outputs = (first_ref, second_ref, third_ref, fourth_ref)
    lines = len(outputs)
    blocks = (own_ref.shape[0] - first_ref.shape[0]) // (lines - 1)
    for shift, out_ref in enumerate(outputs):
        start = lax.rem(here + shift, lines) * blocks
        for index in range(blocks):
            out_ref[index] = own_ref[start + index] + received_ref[start + index]
        for index in range(out_ref.shape[0] - blocks):
            tail = lines * blocks + index
            out_ref[blocks + index] = own_ref[tail] + received_ref[tail]


def pack_rows(parts):
    first, second, third, fourth, fifth = parts
    members = first.shape[0]
    pieces = [fifth[:, i * members : (i + 1) * members] for i in range(3)]
    zero = jnp.zeros((members, members), jnp.float32)
    return [
        jnp.concatenate([first, second, pieces[0], pieces[1]], axis=1),
        jnp.concatenate([third, fourth, pieces[2], zero], axis=1),
    ]


def unpack_rows(one, two):
    members = one.shape[0]
    wide = 3 * members
    fifth = jnp.concatenate([one[:, 2 * wide :], two[:, 2 * wide : 2 * wide + members]], axis=1)
    return [one[:, :wide], one[:, wide : 2 * wide], two[:, :wide], two[:, wide : 2 * wide], fifth]


def sum_peers(parts_ref, index):
    part = parts_ref[0, index]
    for peer in range(1, parts_ref.shape[0]):
        part = part + parts_ref[peer, index]
    return part


def factor_kernel(first_ref, second_ref, third_ref, fourth_ref, inverse_ref, early_ref):
    parts = [part_ref[first_ref.shape[0] - 2 :] for part_ref in (first_ref, second_ref, third_ref, fourth_ref)]
    sums = parts[0] + parts[1] + parts[2] + parts[3]
    extras = [sums[0], sums[1]]
    members = extras[0].shape[0]
    order = 3 * members
    first, second, third, fourth, fifth = unpack_rows(*extras)
    early_ref[...] = jnp.concatenate([fourth, fifth], axis=0)
    gram = jnp.concatenate([first, second, third], axis=0)
    line = lax.broadcasted_iota(jnp.int32, (order, order), 0)
    lane = lax.broadcasted_iota(jnp.int32, (order, order), 1)
    work = jnp.concatenate([gram, jnp.where(line == lane, 1.0, 0.0)], axis=1)
    rows = lax.broadcasted_iota(jnp.int32, (order, 1), 0)
    for step in range(order):
        pivot = work[step : step + 1, step : step + 1]
        scale = lax.rsqrt(pivot)
        scale = scale * (1.5 - 0.5 * pivot * scale * scale)
        lead = work[step : step + 1, :] * scale
        column = work[:, step : step + 1] * scale
        work = jnp.where(rows == step, lead, jnp.where(rows > step, work - column * lead, work))
    inverse_ref[...] = work[:, order:]


def orthonormal_kernel(inverse_ref, basis_ref, residual_ref, out_ref, *, row_scale):
    rows = jnp.concatenate([basis_ref[0], residual_ref[...], basis_ref[1]], axis=0)
    out_ref[...] = exact_dot(inverse_ref[...] * row_scale, rows, NN)


def orthonormal_image_kernel(inverse_ref, images_ref, image_ref, out_ref, *, row_scale):
    rows = jnp.concatenate([images_ref[0], image_ref[...], images_ref[1]], axis=0)
    out_ref[...] = exact_dot(inverse_ref[...] * row_scale, rows, NN)


def image_kernel(
    col_parts_ref,
    first_ref,
    second_ref,
    third_ref,
    fourth_ref,
    basis_ref,
    residual_ref,
    image_ref,
    slots_ref,
):
    blocks = image_ref.shape[1] // LANES
    for index in range(blocks):
        part = first_ref[index] + second_ref[index] + third_ref[index] + fourth_ref[index]
        image_ref[:, index * LANES : (index + 1) * LANES] = sum_peers(col_parts_ref, index) + part
    basis = jnp.concatenate([basis_ref[0], residual_ref[...], basis_ref[1]], axis=0)
    late = exact_dot(image_ref[...], basis, NT)
    packed = jnp.concatenate([late[row : row + 1] for row in range(late.shape[0])], axis=1)
    slots_ref[...] = jnp.broadcast_to(packed[None], slots_ref.shape)


def projected_kernel(received_ref, inverse_ref, early_ref, projected_ref):
    packed = jnp.sum(received_ref[...], axis=0)
    early = early_ref[...]
    members = early.shape[0] // 2
    wide = early.shape[1]
    late = jnp.concatenate(
        [packed[:, row * wide : (row + 1) * wide] for row in range(members)], axis=0
    )
    mixed_t = jnp.concatenate([early[:members], late, early[members:]], axis=0)
    inverse = inverse_ref[...]
    half_done = exact_dot(inverse, mixed_t, NT)
    projected_ref[...] = exact_dot(half_done, inverse, NT)


def split_blocks(x_ref, split_ref, start, per_peer):
    def split(peer, carry):
        for index in range(per_peer):
            value = x_ref[peer, index]
            high = value.astype(jnp.bfloat16)
            low = (value - high.astype(jnp.float32)).astype(jnp.bfloat16)
            split_ref[start + peer * per_peer + index] = jnp.concatenate([high, low], axis=0)
        return carry

    lax.fori_loop(0, x_ref.shape[0], split, 0)


def group_size(slots):
    return math.gcd(slots, GROUP)


def group_count(live, slots):
    return (jnp.minimum(live, slots) + group_size(slots) - 1) // group_size(slots)


def group_copy(tiles_hbm, tiles_ref, arrived, counter):
    size = group_size(tiles_ref.shape[0])
    part = pl.ds(counter * size, size)
    return pltpu.make_async_copy(tiles_hbm.at[part], tiles_ref.at[part], arrived.at[counter])


def tile_kernel(
    count_ref,
    rows_hbm,
    cols_hbm,
    tiles_hbm,
    own_ref,
    other_ref,
    own_out_hbm,
    other_out_hbm,
    rows_ref,
    cols_ref,
    tiles_ref,
    split_ref,
    totals_ref,
    arrived,
    moved,
    *,
    forward,
):
    slots = tiles_ref.shape[0]
    live = count_ref[0, 0]
    rows_copy = pltpu.make_async_copy(rows_hbm, rows_ref, moved.at[2])
    cols_copy = pltpu.make_async_copy(cols_hbm, cols_ref, moved.at[3])
    for copy in (rows_copy, cols_copy):
        copy.start()

    def start(counter, carry):
        group_copy(tiles_hbm, tiles_ref, arrived, counter).start()
        return carry

    lax.fori_loop(0, group_count(live, slots), start, 0)
    totals_ref[...] = jnp.zeros_like(totals_ref)
    peers = own_ref.shape[0]
    split_half = split_ref.shape[0] // 2
    blocks = split_half // peers if forward else own_ref.shape[1] - 2
    half = totals_ref.shape[0] // 2
    split_blocks(own_ref, split_ref, 0, blocks)
    split_blocks(other_ref, split_ref, split_half, blocks)
    if not forward:
        extra = own_ref.shape[1] - blocks
        for index in range(extra):
            part = sum_peers(own_ref, blocks + index) + sum_peers(other_ref, blocks + index)
            totals_ref[half - extra + index] = part
            totals_ref[2 * half - extra + index] = part
    rows_copy.wait()
    cols_copy.wait()
    unroll = group_size(slots)
    members = split_ref.shape[1] // 2
    source_ref, target_ref = (cols_ref, rows_ref) if forward else (rows_ref, cols_ref)

    def group(counter, carry):
        group_copy(tiles_hbm, tiles_ref, arrived, counter).wait()
        base = counter * unroll
        products = []
        for offset in range(unroll):
            slot = base + offset
            product = lax.dot_general(
                split_ref[source_ref[0, 0, slot]],
                tiles_ref[slot],
                NT if forward else NN,
                preferred_element_type=jnp.float32,
            )
            product = product[:members] + product[members:]
            products.append(jnp.where(slot < live, product, 0.0))
        for offset in range(unroll):
            target = target_ref[0, 0, base + offset]
            totals_ref[target] = totals_ref[target] + products[offset]
        return carry

    lax.fori_loop(0, group_count(live, slots), group, 0)
    outs = [
        pltpu.make_async_copy(totals_ref.at[pl.ds(start, half)], out, moved.at[index])
        for index, (start, out) in enumerate(((0, own_out_hbm), (half, other_out_hbm)))
    ]
    for copy in outs:
        copy.start()
    for copy in outs:
        copy.wait()


def tile_call(count, rows, cols, tiles, own, other, split_places, out_places, forward):
    smem = pl.BlockSpec(memory_space=pltpu.SMEM)
    anywhere = pl.BlockSpec(memory_space=pl.ANY)
    members = own.shape[2]
    slots = tiles.shape[0]
    out = jax.ShapeDtypeStruct((out_places, members, LANES), jnp.float32)
    return pl.pallas_call(
        functools.partial(tile_kernel, forward=forward),
        out_shape=[out, out],
        in_specs=[smem] + [anywhere] * 3 + [pl.BlockSpec(memory_space=pltpu.VMEM)] * 2,
        out_specs=[anywhere] * 2,
        scratch_shapes=[
            pltpu.SMEM(rows.shape, jnp.int32),
            pltpu.SMEM(cols.shape, jnp.int32),
            pltpu.VMEM(tiles.shape, tiles.dtype),
            pltpu.VMEM((2 * split_places, 2 * members, LANES), jnp.bfloat16),
            pltpu.VMEM((2 * out_places, members, LANES), jnp.float32),
            pltpu.SemaphoreType.DMA((slots // group_size(slots),)),
            pltpu.SemaphoreType.DMA((4,)),
        ],
        compiler_params=pltpu.CompilerParams(vmem_limit_bytes=TILE_VMEM_BYTES),
        name="forward_tiles" if forward else "backward_tiles",
    )(count, rows, cols, tiles, own, other)


def join_kernel(own_ref, other_ref, out_ref):
    out_ref[...] = own_ref[...] + other_ref[...]


def exchange(slots, axes, groups=None):
    return lax.all_to_all(slots, axes, 0, 0, axis_index_groups=groups, tiled=True)


def swap(array, axis, distance):
    return lax.ppermute(array, axis, [(i, i ^ distance) for i in range(lax.axis_size(axis))])


def shift_lines(array, shift):
    size = lax.axis_size("row")
    return lax.ppermute(array, "row", [(i, (i + 2 * shift) % size) for i in range(size)])


def on_device(
    tile_blocks, tile_rows, tile_cols, tile_count, vectors, hvectors, previous, hprevious
):
    n_row = lax.axis_size("row")
    n_col = lax.axis_size("col")
    everyone = ("row", "col")
    chips = n_col // 2
    core_groups = [[2 * chip + core for chip in range(chips)] for core in (0, 1)]
    members, piece = vectors.shape
    blocks = piece // LANES
    lines = n_row // 2
    order = 3 * members
    tiles = tile_blocks[0, 0]
    row_scale = math.sqrt(piece * n_row * n_col)
    f32 = jnp.float32

    hbm_spec = pl.BlockSpec(memory_space=pl.ANY)
    vmem_spec = pl.BlockSpec(memory_space=pltpu.VMEM)
    params = pltpu.CompilerParams(vmem_limit_bytes=VMEM_BYTES)
    (sums,) = pl.pallas_call(
        stage_kernel,
        out_shape=[jax.ShapeDtypeStruct((n_row * n_col, LANES), f32)],
        in_specs=[hbm_spec, hbm_spec],
        out_specs=[vmem_spec],
        scratch_shapes=[
            pltpu.VMEM((2, members, piece), f32),
            pltpu.SemaphoreType.DMA((2,)),
        ],
        compiler_params=pltpu.CompilerParams(vmem_limit_bytes=FULL_VMEM_BYTES),
        name="stage",
    )(vectors, hvectors)
    basis, images = pl.pallas_call(
        prepare_kernel,
        out_shape=[jax.ShapeDtypeStruct((2, members, piece), f32)] * 2,
        in_specs=[hbm_spec] * 4,
        out_specs=[vmem_spec] * 2,
        scratch_shapes=[pltpu.SemaphoreType.DMA((4,))],
        compiler_params=params,
        name="prepare",
    )(vectors, previous, hvectors, hprevious)
    sums = exchange(sums, everyone)
    sums, basis, images = lax.optimization_barrier((sums, basis, images))
    residual, slots = call(
        residual_kernel, [(members, piece), (chips, blocks + 2, members, LANES)], "residual"
    )(sums, basis, images)
    pieces = [residual] + [shift_lines(residual, shift) for shift in range(1, lines)]
    (line,) = call(line_kernel, [(lines, blocks, members, LANES)], "line")(*pieces)
    own_range = exchange(slots, "col", core_groups)
    residual, tile_rows, tile_cols = lax.optimization_barrier((residual, tile_rows, tile_cols))
    rows, cols = pl.pallas_call(
        functools.partial(places_kernel, blocks=blocks, gap=2),
        out_shape=[jax.ShapeDtypeStruct(tile_rows.shape, jnp.int32)] * 2,
        compiler_params=params,
        name="places",
    )(tile_rows, tile_cols)
    own_range, line, rows, cols = lax.optimization_barrier((own_range, line, rows, cols))
    far_line = swap(line, "row", 1)
    other_range = swap(own_range, "col", 1)
    col_own, col_other = tile_call(
        tile_count,
        rows,
        cols,
        tiles,
        own_range,
        other_range,
        chips * blocks,
        lines * blocks + 2,
        False,
    )
    col_own, col_other, far_line = lax.optimization_barrier((col_own, col_other, far_line))
    col_received = swap(col_other, "row", 1)
    own_totals, other_totals = tile_call(
        tile_count,
        rows,
        cols,
        tiles,
        line,
        far_line,
        lines * blocks + 2,
        chips * blocks,
        True,
    )
    col_received, own_totals, other_totals = lax.optimization_barrier(
        (col_received, own_totals, other_totals)
    )
    (totals,) = pl.pallas_call(
        join_kernel,
        out_shape=[jax.ShapeDtypeStruct(own_totals.shape, f32)],
        compiler_params=pltpu.CompilerParams(vmem_limit_bytes=TILE_VMEM_BYTES),
        name="join",
    )(own_totals, swap(other_totals, "col", 1))
    col_parts = exchange(totals.reshape(chips, blocks, members, LANES), "col", core_groups)
    outs = call(halves_kernel, [(blocks + 2, members, LANES)] * lines, "halves")(
        col_own, col_received
    )
    row_parts = [outs[0]] + [shift_lines(outs[shift], shift) for shift in range(1, lines)]
    col_parts, *row_parts = lax.optimization_barrier((col_parts, *row_parts))
    image, slots = call(
        image_kernel, [(members, piece), (n_row * n_col, 1, members * order)], "image"
    )(col_parts, *row_parts, basis, residual)
    late = exchange(slots, everyone)
    image, *row_parts = lax.optimization_barrier((image, *row_parts))
    inverse, early = call(factor_kernel, [(order, order), (2 * members, order)], "factor")(*row_parts)
    (orthonormal,) = call(
        functools.partial(orthonormal_kernel, row_scale=row_scale), [(order, piece)], "orthonormal"
    )(inverse, basis, residual)
    (orthonormal_image,) = call(
        functools.partial(orthonormal_image_kernel, row_scale=row_scale),
        [(order, piece)],
        "orthonormal_image",
    )(inverse, images, image)
    (projected,) = call(projected_kernel, [(order, order)], "projected")(late, inverse, early)
    return (orthonormal, orthonormal_image, projected)


def solution(mesh):
    in_specs = (
        P("row", "col", None, None, None),
        P("row", "col", None),
        P("row", "col", None),
        P("row", "col"),
        P(None, ("row", "col")),
        P(None, ("row", "col")),
        P(None, ("row", "col")),
        P(None, ("row", "col")),
    )
    out_specs = (P(None, ("row", "col")), P(None, ("row", "col")), P())
    return jax.shard_map(
        on_device, mesh=mesh, in_specs=in_specs, out_specs=out_specs, check_vma=False
    )
```

```python
import functools
import math

import jax
import jax.numpy as jnp
from jax import lax
from jax.experimental import pallas as pl
from jax.experimental.pallas import tpu as pltpu
from jax.sharding import PartitionSpec as P

EPSILON = 1e-06
HIGHEST_PRECISION = lax.Precision.HIGHEST
LANES = 128
VMEM_BYTES = 32 << 20
FULL_VMEM_BYTES = 60 << 20
TILE_VMEM_BYTES = 48<<20
GROUP = 64
NT = (((1,), (1,)), ((), ()))
NN = (((1,), (0,)), ((), ()))


def exact_dot(first, second, dims):
    return lax.dot_general(
        first, second, dims, precision=HIGHEST_PRECISION, preferred_element_type=jnp.float32
    )


def call(kernel, out_shapes, name):
    return pl.pallas_call(
        kernel,
        out_shape=[jax.ShapeDtypeStruct(shape, jnp.float32) for shape in out_shapes],
        compiler_params=pltpu.CompilerParams(vmem_limit_bytes=VMEM_BYTES),
        name=name,
    )


def block(array, index):
    return array[:, index * LANES : (index + 1) * LANES]


def stage_kernel(vectors_hbm, hvectors_hbm, slots_ref, stack_ref, arrived):
    copies = [
        pltpu.make_async_copy(source, stack_ref.at[index], arrived.at[index])
        for index, source in enumerate((vectors_hbm, hvectors_hbm))
    ]
    for copy in copies:
        copy.start()
    for copy in copies:
        copy.wait()
    vectors = stack_ref[0]
    hvectors = stack_ref[1]
    members = vectors.shape[0]
    top = jnp.sum(vectors * hvectors, axis=1, keepdims=True)
    bottom = jnp.sum(vectors * vectors, axis=1, keepdims=True)
    lane = lax.broadcasted_iota(jnp.int32, (members, LANES), 1)
    line = lax.broadcasted_iota(jnp.int32, (members, LANES), 0)
    spread = jnp.where(lane == line, top, 0.0) + jnp.where(lane == line + members, bottom, 0.0)
    sums = jnp.sum(spread, axis=0, keepdims=True)
    slots_ref[...] = jnp.broadcast_to(sums, slots_ref.shape)


def prepare_kernel(
    vectors_hbm, previous_hbm, hvectors_hbm, hprevious_hbm, basis_ref, images_ref, arrived
):
    copies = [
        pltpu.make_async_copy(source, target.at[place], arrived.at[index])
        for index, (source, target, place) in enumerate(
            (
                (vectors_hbm, basis_ref, 0),
                (previous_hbm, basis_ref, 1),
                (hvectors_hbm, images_ref, 0),
                (hprevious_hbm, images_ref, 1),
            )
        )
    ]
    for copy in copies:
        copy.start()
    for copy in copies:
        copy.wait()


def places_kernel(rows_ref, cols_ref, rows_out_ref, targets_out_ref, cols_out_ref, *, blocks, gap):
    chips = lax.axis_size("col") // 2
    lines = lax.axis_size("row") // 2
    core = lax.rem(lax.axis_index("col"), 2)
    rows = rows_ref[...]
    index, peer = rows % blocks, rows // blocks
    other = jnp.where(peer % 2 == core, 0, 1)
    chip = peer // 2
    rows_out_ref[...] = (other * chips + chip) * blocks + index
    places = (chip % (chips // 2)) * 2 + chip // (chips // 2)
    targets_out_ref[...] = (other * chips + places) * blocks + index
    half = lax.rem(lax.axis_index("row"), 2)
    cols = cols_ref[...]
    index, peer = cols % blocks, cols // blocks
    other = jnp.where(peer % 2 == half, 0, 1)
    cols_out_ref[...] = (other * lines + peer // 2) * blocks + index + other * gap


def residual_kernel(sums_ref, basis_ref, images_ref, residual_ref, slots_ref):
    members = basis_ref.shape[1]
    sums = jnp.sum(sums_ref[...], axis=0, keepdims=True)
    lane = lax.broadcasted_iota(jnp.int32, (members, LANES), 1)
    line = lax.broadcasted_iota(jnp.int32, (members, LANES), 0)
    top = jnp.sum(jnp.where(lane == line, sums, 0.0), axis=1, keepdims=True)
    bottom = jnp.sum(jnp.where(lane == line + members, sums, 0.0), axis=1, keepdims=True)
    residual = images_ref[0] - (top / (bottom + EPSILON)) * basis_ref[0]
    residual_ref[...] = residual
    blocks = residual.shape[1] // LANES
    for index in range(blocks):
        for slot in range(slots_ref.shape[0]):
            slots_ref[slot, index] = block(residual, index)
    basis = jnp.concatenate([basis_ref[0], residual, basis_ref[1]], axis=0)
    gram = exact_dot(basis, basis, NT)
    early = exact_dot(jnp.concatenate([images_ref[0], images_ref[1]], axis=0), basis, NT)
    extra = [
        gram[:members],
        gram[members : 2 * members],
        gram[2 * members :],
        early[:members],
        early[members:],
    ]
    for index, part in enumerate(pack_rows(extra)):
        for slot in range(slots_ref.shape[0]):
            slots_ref[slot, blocks + index] = part


def line_kernel(first_ref, second_ref, third_ref, fourth_ref, line_ref):
    lines, blocks = line_ref.shape[:2]
    here = lax.axis_index("row") // 2
    for shift, piece_ref in enumerate((first_ref, second_ref, third_ref, fourth_ref)):
        place = lax.rem(here + lines - shift, lines)
        for index in range(blocks):
            line_ref[place, index] = piece_ref[:, index * LANES : (index + 1) * LANES]


def halves_kernel(own_ref, received_ref, first_ref, second_ref, third_ref, fourth_ref):
    here = lax.axis_index("row") // 2
    outputs = (first_ref, second_ref, third_ref, fourth_ref)
    lines = len(outputs)
    blocks = (own_ref.shape[0] - first_ref.shape[0]) // (lines - 1)
    for shift, out_ref in enumerate(outputs):
        start = lax.rem(here + shift, lines) * blocks
        for index in range(blocks):
            out_ref[index] = own_ref[start + index] + received_ref[start + index]
        for index in range(out_ref.shape[0] - blocks):
            tail = lines * blocks + index
            out_ref[blocks + index] = own_ref[tail] + received_ref[tail]


def pack_rows(parts):
    first, second, third, fourth, fifth = parts
    members = first.shape[0]
    pieces = [fifth[:, i * members : (i + 1) * members] for i in range(3)]
    zero = jnp.zeros((members, members), jnp.float32)
    return [
        jnp.concatenate([first, second, pieces[0], pieces[1]], axis=1),
        jnp.concatenate([third, fourth, pieces[2], zero], axis=1),
    ]


def unpack_rows(one, two):
    members = one.shape[0]
    wide = 3 * members
    fifth = jnp.concatenate([one[:, 2 * wide :], two[:, 2 * wide : 2 * wide + members]], axis=1)
    return [one[:, :wide], one[:, wide : 2 * wide], two[:, :wide], two[:, wide : 2 * wide], fifth]


def sum_peers(parts_ref, index):
    part = parts_ref[0, index]
    for peer in range(1, parts_ref.shape[0]):
        part = part + parts_ref[peer, index]
    return part


def factor_kernel(first_ref, second_ref, third_ref, fourth_ref, inverse_ref, early_ref):
    parts = [part_ref[first_ref.shape[0] - 2 :] for part_ref in (first_ref, second_ref, third_ref, fourth_ref)]
    sums = parts[0] + parts[1] + parts[2] + parts[3]
    extras = [sums[0], sums[1]]
    members = extras[0].shape[0]
    order = 3 * members
    first, second, third, fourth, fifth = unpack_rows(*extras)
    early_ref[...] = jnp.concatenate([fourth, fifth], axis=0)
    gram = jnp.concatenate([first, second, third], axis=0)
    line = lax.broadcasted_iota(jnp.int32, (order, order), 0)
    lane = lax.broadcasted_iota(jnp.int32, (order, order), 1)
    work = jnp.concatenate([gram, jnp.where(line == lane, 1.0, 0.0)], axis=1)
    rows = lax.broadcasted_iota(jnp.int32, (order, 1), 0)
    for step in range(order):
        pivot = work[step : step + 1, step : step + 1]
        scale = lax.rsqrt(pivot)
        scale = scale * (1.5 - 0.5 * pivot * scale * scale)
        lead = work[step : step + 1, :] * scale
        column = work[:, step : step + 1] * scale
        work = jnp.where(rows == step, lead, jnp.where(rows > step, work - column * lead, work))
    inverse_ref[...] = work[:, order:]


def orthonormal_kernel(inverse_ref, basis_ref, residual_ref, out_ref, *, row_scale):
    rows = jnp.concatenate([basis_ref[0], residual_ref[...], basis_ref[1]], axis=0)
    out_ref[...] = exact_dot(inverse_ref[...] * row_scale, rows, NN)


def orthonormal_image_kernel(
    inverse_ref, images_ref, image_ref, from_lo_ref, out_ref, *, row_scale
):
    image = image_ref[...] + from_lo_ref[...]
    rows = jnp.concatenate([images_ref[0], image, images_ref[1]], axis=0)
    out_ref[...] = exact_dot(inverse_ref[...] * row_scale, rows, NN)


def image_kernel(
    col_parts_ref,
    first_ref,
    second_ref,
    third_ref,
    fourth_ref,
    basis_ref,
    residual_ref,
    lo_basis_ref,
    range_ref,
    image_ref,
    to_lo_ref,
    slots_ref,
):
    chips = range_ref.shape[0]
    chip = lax.axis_index("col") // 2
    x_lo = chip // (chips // 2)
    partner = lax.rem(chip + chips // 2, chips)
    blocks = image_ref.shape[1] // LANES
    for index in range(blocks):
        part = first_ref[index] + second_ref[index] + third_ref[index] + fourth_ref[index]
        image_ref[:, index * LANES : (index + 1) * LANES] = (
            sum_peers(col_parts_ref, x_lo * blocks + index) + part
        )
        to_lo_ref[:, index * LANES : (index + 1) * LANES] = sum_peers(
            col_parts_ref, (1 - x_lo) * blocks + index
        )
    basis = jnp.concatenate([basis_ref[0], residual_ref[...], basis_ref[1]], axis=0)
    late = exact_dot(image_ref[...], basis, NT)
    lo_residual = jnp.concatenate([range_ref[partner, index] for index in range(blocks)], axis=1)
    basis = jnp.concatenate([lo_basis_ref[0], lo_residual, lo_basis_ref[1]], axis=0)
    late = late + exact_dot(to_lo_ref[...], basis, NT)
    packed = jnp.concatenate([late[row : row + 1] for row in range(late.shape[0])], axis=1)
    slots_ref[...] = jnp.broadcast_to(packed[None], slots_ref.shape)


def projected_kernel(received_ref, inverse_ref, early_ref, projected_ref):
    packed = jnp.sum(received_ref[...], axis=0)
    early = early_ref[...]
    members = early.shape[0] // 2
    wide = early.shape[1]
    late = jnp.concatenate(
        [packed[:, row * wide : (row + 1) * wide] for row in range(members)], axis=0
    )
    mixed_t = jnp.concatenate([early[:members], late, early[members:]], axis=0)
    inverse = inverse_ref[...]
    half_done = exact_dot(inverse, mixed_t, NT)
    projected_ref[...] = exact_dot(half_done, inverse, NT)


def split_blocks(x_ref, split_ref, start, per_peer):
    def split(peer, carry):
        for index in range(per_peer):
            value = x_ref[peer, index]
            high = value.astype(jnp.bfloat16)
            low = (value - high.astype(jnp.float32)).astype(jnp.bfloat16)
            split_ref[start + peer * per_peer + index] = jnp.concatenate([high, low], axis=0)
        return carry

    lax.fori_loop(0, x_ref.shape[0], split, 0)


def group_size(slots):
    return math.gcd(slots, GROUP)


def group_count(live, slots):
    return (jnp.minimum(live, slots) + group_size(slots) - 1) // group_size(slots)


def group_copy(tiles_hbm, tiles_ref, arrived, counter):
    size = group_size(tiles_ref.shape[0])
    part = pl.ds(counter * size, size)
    return pltpu.make_async_copy(tiles_hbm.at[part], tiles_ref.at[part], arrived.at[counter])


def tile_kernel(
    count_ref,
    rows_hbm,
    cols_hbm,
    tiles_hbm,
    own_ref,
    other_ref,
    own_out_hbm,
    other_out_hbm,
    rows_ref,
    cols_ref,
    tiles_ref,
    split_ref,
    totals_ref,
    arrived,
    moved,
    *,
    forward,
):
    slots = tiles_ref.shape[0]
    live = count_ref[0, 0]
    rows_copy = pltpu.make_async_copy(rows_hbm, rows_ref, moved.at[2])
    cols_copy = pltpu.make_async_copy(cols_hbm, cols_ref, moved.at[3])
    for copy in (rows_copy, cols_copy):
        copy.start()

    def start(counter, carry):
        group_copy(tiles_hbm, tiles_ref, arrived, counter).start()
        return carry

    lax.fori_loop(0, group_count(live, slots), start, 0)
    totals_ref[...] = jnp.zeros_like(totals_ref)
    peers = own_ref.shape[0]
    split_half = split_ref.shape[0] // 2
    blocks = split_half // peers if forward else own_ref.shape[1] - 2
    half = totals_ref.shape[0] // 2
    split_blocks(own_ref, split_ref, 0, blocks)
    split_blocks(other_ref, split_ref, split_half, blocks)
    if not forward:
        extra = own_ref.shape[1] - blocks
        for index in range(extra):
            part = sum_peers(own_ref, blocks + index) + sum_peers(other_ref, blocks + index)
            totals_ref[half - extra + index] = part
            totals_ref[2 * half - extra + index] = part
    rows_copy.wait()
    cols_copy.wait()
    unroll = group_size(slots)
    members = split_ref.shape[1] // 2
    source_ref, target_ref = (cols_ref, rows_ref) if forward else (rows_ref, cols_ref)

    def group(counter, carry):
        group_copy(tiles_hbm, tiles_ref, arrived, counter).wait()
        base = counter * unroll
        products = []
        for offset in range(unroll):
            slot = base + offset
            product = lax.dot_general(
                split_ref[source_ref[0, 0, slot]],
                tiles_ref[slot],
                NT if forward else NN,
                preferred_element_type=jnp.float32,
            )
            product = product[:members] + product[members:]
            products.append(jnp.where(slot < live, product, 0.0))
        for offset in range(unroll):
            target = target_ref[0, 0, base + offset]
            totals_ref[target] = totals_ref[target] + products[offset]
        return carry

    lax.fori_loop(0, group_count(live, slots), group, 0)
    outs = [
        pltpu.make_async_copy(totals_ref.at[pl.ds(start, half)], out, moved.at[index])
        for index, (start, out) in enumerate(((0, own_out_hbm), (half, other_out_hbm)))
    ]
    for copy in outs:
        copy.start()
    for copy in outs:
        copy.wait()


def tile_call(count, rows, cols, tiles, own, other, split_places, out_places, forward):
    smem = pl.BlockSpec(memory_space=pltpu.SMEM)
    anywhere = pl.BlockSpec(memory_space=pl.ANY)
    members = own.shape[2]
    slots = tiles.shape[0]
    out = jax.ShapeDtypeStruct((out_places, members, LANES), jnp.float32)
    return pl.pallas_call(
        functools.partial(tile_kernel, forward=forward),
        out_shape=[out, out],
        in_specs=[smem] + [anywhere] * 3 + [pl.BlockSpec(memory_space=pltpu.VMEM)] * 2,
        out_specs=[anywhere] * 2,
        scratch_shapes=[
            pltpu.SMEM(rows.shape, jnp.int32),
            pltpu.SMEM(cols.shape, jnp.int32),
            pltpu.VMEM(tiles.shape, tiles.dtype),
            pltpu.VMEM((2 * split_places, 2 * members, LANES), jnp.bfloat16),
            pltpu.VMEM((2 * out_places, members, LANES), jnp.float32),
            pltpu.SemaphoreType.DMA((slots // group_size(slots),)),
            pltpu.SemaphoreType.DMA((4,)),
        ],
        compiler_params=pltpu.CompilerParams(vmem_limit_bytes=TILE_VMEM_BYTES),
        name="forward_tiles" if forward else "backward_tiles",
    )(count, rows, cols, tiles, own, other)


def join_kernel(own_ref, other_ref, out_ref):
    out_ref[...] = own_ref[...] + other_ref[...]


def exchange(slots, axes, groups=None):
    return lax.all_to_all(slots, axes, 0, 0, axis_index_groups=groups, tiled=True)


def swap(array, axis, distance):
    return lax.ppermute(array, axis, [(i, i ^ distance) for i in range(lax.axis_size(axis))])


def shift_lines(array, shift):
    size = lax.axis_size("row")
    return lax.ppermute(array, "row", [(i, (i + 2 * shift) % size) for i in range(size)])


def on_device(
    tile_blocks, tile_rows, tile_cols, tile_count, vectors, hvectors, previous, hprevious
):
    n_row = lax.axis_size("row")
    n_col = lax.axis_size("col")
    everyone = ("row", "col")
    chips = n_col // 2
    y_groups = [
        [(half * chips // 2 + line) * 2 + core for line in range(chips // 2)]
        for half in (0, 1)
        for core in (0, 1)
    ]
    core_groups = [[2 * chip + core for chip in range(chips)] for core in (0, 1)]
    members, piece = vectors.shape
    blocks = piece // LANES
    lines = n_row // 2
    order = 3 * members
    tiles = tile_blocks[0, 0]
    row_scale = math.sqrt(piece * n_row * n_col)
    f32 = jnp.float32

    hbm_spec = pl.BlockSpec(memory_space=pl.ANY)
    vmem_spec = pl.BlockSpec(memory_space=pltpu.VMEM)
    params = pltpu.CompilerParams(vmem_limit_bytes=VMEM_BYTES)
    (sums,) = pl.pallas_call(
        stage_kernel,
        out_shape=[jax.ShapeDtypeStruct((n_row * n_col, LANES), f32)],
        in_specs=[hbm_spec, hbm_spec],
        out_specs=[vmem_spec],
        scratch_shapes=[
            pltpu.VMEM((2, members, piece), f32),
            pltpu.SemaphoreType.DMA((2,)),
        ],
        compiler_params=pltpu.CompilerParams(vmem_limit_bytes=FULL_VMEM_BYTES),
        name="stage",
    )(vectors, hvectors)
    basis, images = pl.pallas_call(
        prepare_kernel,
        out_shape=[jax.ShapeDtypeStruct((2, members, piece), f32)] * 2,
        in_specs=[hbm_spec] * 4,
        out_specs=[vmem_spec] * 2,
        scratch_shapes=[pltpu.SemaphoreType.DMA((4,))],
        compiler_params=params,
        name="prepare",
    )(vectors, previous, hvectors, hprevious)
    sums = exchange(sums, everyone)
    sums, basis, images = lax.optimization_barrier((sums, basis, images))
    residual, slots = call(
        residual_kernel, [(members, piece), (chips, blocks + 2, members, LANES)], "residual"
    )(sums, basis, images)
    pieces = [residual] + [shift_lines(residual, shift) for shift in range(1, lines)]
    (line,) = call(line_kernel, [(lines, blocks, members, LANES)], "line")(*pieces)
    own_range = exchange(slots, "col", core_groups)
    residual, tile_rows, tile_cols = lax.optimization_barrier((residual, tile_rows, tile_cols))
    rows, targets, cols = pl.pallas_call(
        functools.partial(places_kernel, blocks=blocks, gap=2),
        out_shape=[jax.ShapeDtypeStruct(tile_rows.shape, jnp.int32)] * 3,
        compiler_params=params,
        name="places",
    )(tile_rows, tile_cols)
    own_range, line, rows, targets, cols = lax.optimization_barrier(
        (own_range, line, rows, targets, cols)
    )
    far_line = swap(line, "row", 1)
    other_range = swap(own_range, "col", 1)
    col_own, col_other = tile_call(
        tile_count,
        rows,
        cols,
        tiles,
        own_range,
        other_range,
        chips * blocks,
        lines * blocks + 2,
        False,
    )
    col_own, col_other, far_line = lax.optimization_barrier((col_own, col_other, far_line))
    col_received = swap(col_other, "row", 1)
    own_totals, other_totals = tile_call(
        tile_count,
        targets,
        cols,
        tiles,
        line,
        far_line,
        lines * blocks + 2,
        chips * blocks,
        True,
    )
    col_received, own_totals, other_totals = lax.optimization_barrier(
        (col_received, own_totals, other_totals)
    )
    outs = call(halves_kernel, [(blocks + 2, members, LANES)] * lines, "halves")(
        col_own, col_received
    )
    other_totals, *outs = lax.optimization_barrier((swap(other_totals, "col", 1), *outs))
    (totals,) = pl.pallas_call(
        join_kernel,
        out_shape=[jax.ShapeDtypeStruct(own_totals.shape, f32)],
        compiler_params=pltpu.CompilerParams(vmem_limit_bytes=TILE_VMEM_BYTES),
        name="join",
    )(own_totals, other_totals)
    col_parts = exchange(totals.reshape(chips // 2, 2 * blocks, members, LANES), "col", y_groups)
    lo_basis = swap(basis, "col", chips)
    row_parts = [outs[0]] + [shift_lines(outs[shift], shift) for shift in range(1, lines)]
    col_parts, lo_basis, *row_parts = lax.optimization_barrier((col_parts, lo_basis, *row_parts))
    image, to_lo, slots = call(
        image_kernel, [(members, piece)] * 2 + [(n_row * n_col, 1, members * order)], "image"
    )(col_parts, *row_parts, basis, residual, lo_basis, own_range)
    from_lo = swap(to_lo, "col", chips)
    late = exchange(slots, everyone)
    image, *row_parts = lax.optimization_barrier((image, *row_parts))
    inverse, early = call(factor_kernel, [(order, order), (2 * members, order)], "factor")(*row_parts)
    (orthonormal,) = call(
        functools.partial(orthonormal_kernel, row_scale=row_scale), [(order, piece)], "orthonormal"
    )(inverse, basis, residual)
    (orthonormal_image,) = call(
        functools.partial(orthonormal_image_kernel, row_scale=row_scale),
        [(order, piece)],
        "orthonormal_image",
    )(inverse, images, image, from_lo)
    (projected,) = call(projected_kernel, [(order, order)], "projected")(late, inverse, early)
    return (orthonormal, orthonormal_image, projected)


def solution(mesh):
    in_specs = (
        P("row", "col", None, None, None),
        P("row", "col", None),
        P("row", "col", None),
        P("row", "col"),
        P(None, ("row", "col")),
        P(None, ("row", "col")),
        P(None, ("row", "col")),
        P(None, ("row", "col")),
    )
    out_specs = (P(None, ("row", "col")), P(None, ("row", "col")), P())
    return jax.shard_map(
        on_device, mesh=mesh, in_specs=in_specs, out_specs=out_specs, check_vma=False
    )
```

```python
import functools
import math

import jax
import jax.numpy as jnp
from jax import lax
from jax.experimental import pallas as pl
from jax.experimental.pallas import tpu as pltpu
from jax.sharding import PartitionSpec as P

EPSILON = 1e-06
HIGHEST_PRECISION = lax.Precision.HIGHEST
LANES = 128
VMEM_BYTES = 32 << 20
FULL_VMEM_BYTES = 60 << 20
TILE_VMEM_BYTES = 48<<20
GROUP = 64
NT = (((1,), (1,)), ((), ()))
NN = (((1,), (0,)), ((), ()))


def exact_dot(first, second, dims):
    return lax.dot_general(
        first, second, dims, precision=HIGHEST_PRECISION, preferred_element_type=jnp.float32
    )


def call(kernel, out_shapes, name):
    return pl.pallas_call(
        kernel,
        out_shape=[jax.ShapeDtypeStruct(shape, jnp.float32) for shape in out_shapes],
        compiler_params=pltpu.CompilerParams(vmem_limit_bytes=VMEM_BYTES),
        name=name,
    )


def block(array, index):
    return array[:, index * LANES : (index + 1) * LANES]


def stage_kernel(vectors_hbm, hvectors_hbm, slots_ref, stack_ref, arrived):
    copies = [
        pltpu.make_async_copy(source, stack_ref.at[index], arrived.at[index])
        for index, source in enumerate((vectors_hbm, hvectors_hbm))
    ]
    for copy in copies:
        copy.start()
    for copy in copies:
        copy.wait()
    vectors = stack_ref[0]
    hvectors = stack_ref[1]
    members = vectors.shape[0]
    top = jnp.sum(vectors * hvectors, axis=1, keepdims=True)
    bottom = jnp.sum(vectors * vectors, axis=1, keepdims=True)
    lane = lax.broadcasted_iota(jnp.int32, (members, LANES), 1)
    line = lax.broadcasted_iota(jnp.int32, (members, LANES), 0)
    spread = jnp.where(lane == line, top, 0.0) + jnp.where(lane == line + members, bottom, 0.0)
    sums = jnp.sum(spread, axis=0, keepdims=True)
    slots_ref[...] = jnp.broadcast_to(sums, slots_ref.shape)


def prepare_kernel(
    vectors_hbm, previous_hbm, hvectors_hbm, hprevious_hbm, basis_ref, images_ref, arrived
):
    copies = [
        pltpu.make_async_copy(source, target.at[place], arrived.at[index])
        for index, (source, target, place) in enumerate(
            (
                (vectors_hbm, basis_ref, 0),
                (previous_hbm, basis_ref, 1),
                (hvectors_hbm, images_ref, 0),
                (hprevious_hbm, images_ref, 1),
            )
        )
    ]
    for copy in copies:
        copy.start()
    for copy in copies:
        copy.wait()


def places_kernel(rows_ref, cols_ref, rows_out_ref, cols_out_ref, *, blocks, gap):
    chips = lax.axis_size("col") // 2
    lines = lax.axis_size("row") // 2
    core = lax.rem(lax.axis_index("col"), 2)
    rows = rows_ref[...]
    index, peer = rows % blocks, rows // blocks
    other = jnp.where(peer % 2 == core, 0, 1)
    rows_out_ref[...] = (other * chips + peer // 2) * blocks + index
    half = lax.rem(lax.axis_index("row"), 2)
    cols = cols_ref[...]
    index, peer = cols % blocks, cols // blocks
    other = jnp.where(peer % 2 == half, 0, 1)
    cols_out_ref[...] = (other * lines + peer // 2) * blocks + index + other * gap


def residual_kernel(
    sums_ref, basis_ref, images_ref, residual_ref, slots_hbm, piece_ref, extra_ref, sent
):
    members = basis_ref.shape[1]
    sums = jnp.sum(sums_ref[...], axis=0, keepdims=True)
    lane = lax.broadcasted_iota(jnp.int32, (members, LANES), 1)
    line = lax.broadcasted_iota(jnp.int32, (members, LANES), 0)
    top = jnp.sum(jnp.where(lane == line, sums, 0.0), axis=1, keepdims=True)
    bottom = jnp.sum(jnp.where(lane == line + members, sums, 0.0), axis=1, keepdims=True)
    residual = images_ref[0] - (top / (bottom + EPSILON)) * basis_ref[0]
    residual_ref[...] = residual
    blocks = residual.shape[1] // LANES
    for index in range(blocks):
        piece_ref[index] = block(residual, index)
    slots = slots_hbm.shape[0]
    copies = [
        pltpu.make_async_copy(piece_ref, slots_hbm.at[slot, pl.ds(0, blocks)], sent.at[slot])
        for slot in range(slots)
    ]
    for copy in copies:
        copy.start()
    basis = jnp.concatenate([basis_ref[0], residual, basis_ref[1]], axis=0)
    rows = jnp.concatenate([basis, images_ref[0], images_ref[1]], axis=0)
    products = exact_dot(rows, basis, NT)
    gram = products[: 3 * members]
    early = products[3 * members :]
    extra = [
        gram[:members],
        gram[members : 2 * members],
        gram[2 * members :],
        early[:members],
        early[members:],
    ]
    for index, part in enumerate(pack_rows(extra)):
        extra_ref[index] = part
    extras = extra_ref.shape[0]
    more = [
        pltpu.make_async_copy(
            extra_ref, slots_hbm.at[slot, pl.ds(blocks, extras)], sent.at[slots + slot]
        )
        for slot in range(slots)
    ]
    for copy in more:
        copy.start()
    for copy in copies + more:
        copy.wait()


def line_kernel(first_ref, second_ref, third_ref, fourth_ref, line_ref):
    lines, blocks = line_ref.shape[:2]
    here = lax.axis_index("row") // 2
    for shift, piece_ref in enumerate((first_ref, second_ref, third_ref, fourth_ref)):
        place = lax.rem(here + lines - shift, lines)
        for index in range(blocks):
            line_ref[place, index] = piece_ref[:, index * LANES : (index + 1) * LANES]


def halves_kernel(own_ref, received_ref, first_ref, second_ref, third_ref, fourth_ref):
    here = lax.axis_index("row") // 2
    outputs = (first_ref, second_ref, third_ref, fourth_ref)
    lines = len(outputs)
    blocks = (own_ref.shape[0] - first_ref.shape[0]) // (lines - 1)
    for shift, out_ref in enumerate(outputs):
        start = lax.rem(here + shift, lines) * blocks
        for index in range(blocks):
            out_ref[index] = own_ref[start + index] + received_ref[start + index]
        for index in range(out_ref.shape[0] - blocks):
            tail = lines * blocks + index
            out_ref[blocks + index] = own_ref[tail] + received_ref[tail]


def pack_rows(parts):
    first, second, third, fourth, fifth = parts
    members = first.shape[0]
    pieces = [fifth[:, i * members : (i + 1) * members] for i in range(3)]
    zero = jnp.zeros((members, members), jnp.float32)
    return [
        jnp.concatenate([first, second, pieces[0], pieces[1]], axis=1),
        jnp.concatenate([third, fourth, pieces[2], zero], axis=1),
    ]


def unpack_rows(one, two):
    members = one.shape[0]
    wide = 3 * members
    fifth = jnp.concatenate([one[:, 2 * wide :], two[:, 2 * wide : 2 * wide + members]], axis=1)
    return [one[:, :wide], one[:, wide : 2 * wide], two[:, :wide], two[:, wide : 2 * wide], fifth]


def sum_peers(parts_ref, index):
    part = parts_ref[0, index]
    for peer in range(1, parts_ref.shape[0]):
        part = part + parts_ref[peer, index]
    return part


def factor_kernel(first_ref, second_ref, third_ref, fourth_ref, inverse_ref, early_ref):
    parts = [part_ref[first_ref.shape[0] - 2 :] for part_ref in (first_ref, second_ref, third_ref, fourth_ref)]
    sums = parts[0] + parts[1] + parts[2] + parts[3]
    extras = [sums[0], sums[1]]
    members = extras[0].shape[0]
    order = 3 * members
    first, second, third, fourth, fifth = unpack_rows(*extras)
    early_ref[...] = jnp.concatenate([fourth, fifth], axis=0)
    gram = jnp.concatenate([first, second, third], axis=0)
    line = lax.broadcasted_iota(jnp.int32, (order, order), 0)
    lane = lax.broadcasted_iota(jnp.int32, (order, order), 1)
    work = jnp.concatenate([gram, jnp.where(line == lane, 1.0, 0.0)], axis=1)
    rows = lax.broadcasted_iota(jnp.int32, (order, 1), 0)
    for step in range(order):
        pivot = work[step : step + 1, step : step + 1]
        scale = lax.rsqrt(pivot)
        scale = scale * (1.5 - 0.5 * pivot * scale * scale)
        lead = work[step : step + 1, :] * scale
        column = work[:, step : step + 1] * scale
        work = jnp.where(rows == step, lead, jnp.where(rows > step, work - column * lead, work))
    inverse_ref[...] = work[:, order:]


def orthonormal_kernel(inverse_ref, basis_ref, residual_ref, out_ref, *, row_scale):
    rows = jnp.concatenate([basis_ref[0], residual_ref[...], basis_ref[1]], axis=0)
    out_ref[...] = exact_dot(inverse_ref[...] * row_scale, rows, NN)


def orthonormal_image_kernel(inverse_ref, images_ref, image_ref, out_ref, *, row_scale):
    rows = jnp.concatenate([images_ref[0], image_ref[...], images_ref[1]], axis=0)
    out_ref[...] = exact_dot(inverse_ref[...] * row_scale, rows, NN)


def image_kernel(
    col_parts_ref,
    first_ref,
    second_ref,
    third_ref,
    fourth_ref,
    basis_ref,
    residual_ref,
    image_ref,
    slots_hbm,
    rows_ref,
    sent,
):
    blocks = image_ref.shape[1] // LANES
    for index in range(blocks):
        part = first_ref[index] + second_ref[index] + third_ref[index] + fourth_ref[index]
        image_ref[:, index * LANES : (index + 1) * LANES] = sum_peers(col_parts_ref, index) + part
    basis = jnp.concatenate([basis_ref[0], residual_ref[...], basis_ref[1]], axis=0)
    late = exact_dot(image_ref[...], basis, NT)
    packed = jnp.concatenate([late[row : row + 1] for row in range(late.shape[0])], axis=1)
    rows_ref[...] = jnp.broadcast_to(packed[None], rows_ref.shape)
    some = rows_ref.shape[0]
    copies = [
        pltpu.make_async_copy(rows_ref, slots_hbm.at[pl.ds(part * some, some)], sent.at[part])
        for part in range(slots_hbm.shape[0] // some)
    ]
    for copy in copies:
        copy.start()
    for copy in copies:
        copy.wait()


def projected_kernel(received_ref, inverse_ref, early_ref, projected_ref):
    packed = jnp.sum(received_ref[...], axis=0)
    early = early_ref[...]
    members = early.shape[0] // 2
    wide = early.shape[1]
    late = jnp.concatenate(
        [packed[:, row * wide : (row + 1) * wide] for row in range(members)], axis=0
    )
    mixed_t = jnp.concatenate([early[:members], late, early[members:]], axis=0)
    inverse = inverse_ref[...]
    half_done = exact_dot(inverse, mixed_t, NT)
    projected_ref[...] = exact_dot(half_done, inverse, NT)


def split_blocks(x_ref, split_ref, start, per_peer):
    def split(peer, carry):
        for index in range(per_peer):
            value = x_ref[peer, index]
            high = value.astype(jnp.bfloat16)
            low = (value - high.astype(jnp.float32)).astype(jnp.bfloat16)
            split_ref[start + peer * per_peer + index] = jnp.concatenate([high, low], axis=0)
        return carry

    lax.fori_loop(0, x_ref.shape[0], split, 0)


def group_size(slots):
    return math.gcd(slots, GROUP)


def group_count(live, slots):
    return (jnp.minimum(live, slots) + group_size(slots) - 1) // group_size(slots)


def group_copy(tiles_hbm, tiles_ref, arrived, counter):
    size = group_size(tiles_ref.shape[0])
    part = pl.ds(counter * size, size)
    return pltpu.make_async_copy(tiles_hbm.at[part], tiles_ref.at[part], arrived.at[counter])


def tile_kernel(
    count_ref,
    rows_hbm,
    cols_hbm,
    tiles_hbm,
    own_ref,
    other_ref,
    own_out_hbm,
    other_out_hbm,
    rows_ref,
    cols_ref,
    tiles_ref,
    split_ref,
    totals_ref,
    arrived,
    moved,
    *,
    forward,
):
    slots = tiles_ref.shape[0]
    live = count_ref[0, 0]
    rows_copy = pltpu.make_async_copy(rows_hbm, rows_ref, moved.at[2])
    cols_copy = pltpu.make_async_copy(cols_hbm, cols_ref, moved.at[3])
    for copy in (rows_copy, cols_copy):
        copy.start()

    def start(counter, carry):
        group_copy(tiles_hbm, tiles_ref, arrived, counter).start()
        return carry

    lax.fori_loop(0, group_count(live, slots), start, 0)
    totals_ref[...] = jnp.zeros_like(totals_ref)
    peers = own_ref.shape[0]
    split_half = split_ref.shape[0] // 2
    blocks = split_half // peers if forward else own_ref.shape[1] - 2
    half = totals_ref.shape[0] // 2
    split_blocks(own_ref, split_ref, 0, blocks)
    split_blocks(other_ref, split_ref, split_half, blocks)
    if not forward:
        extra = own_ref.shape[1] - blocks
        for index in range(extra):
            part = sum_peers(own_ref, blocks + index) + sum_peers(other_ref, blocks + index)
            totals_ref[half - extra + index] = part
            totals_ref[2 * half - extra + index] = part
    rows_copy.wait()
    cols_copy.wait()
    unroll = group_size(slots)
    members = split_ref.shape[1] // 2
    source_ref, target_ref = (cols_ref, rows_ref) if forward else (rows_ref, cols_ref)

    def group(counter, carry):
        group_copy(tiles_hbm, tiles_ref, arrived, counter).wait()
        base = counter * unroll
        products = []
        for offset in range(unroll):
            slot = base + offset
            product = lax.dot_general(
                split_ref[source_ref[0, 0, slot]],
                tiles_ref[slot],
                NT if forward else NN,
                preferred_element_type=jnp.float32,
            )
            product = product[:members] + product[members:]
            products.append(jnp.where(slot < live, product, 0.0))
        for offset in range(unroll):
            target = target_ref[0, 0, base + offset]
            totals_ref[target] = totals_ref[target] + products[offset]
        return carry

    lax.fori_loop(0, group_count(live, slots), group, 0)
    outs = [
        pltpu.make_async_copy(totals_ref.at[pl.ds(start, half)], out, moved.at[index])
        for index, (start, out) in enumerate(((0, own_out_hbm), (half, other_out_hbm)))
    ]
    for copy in outs:
        copy.start()
    for copy in outs:
        copy.wait()


def tile_call(count, rows, cols, tiles, own, other, split_places, out_places, forward):
    smem = pl.BlockSpec(memory_space=pltpu.SMEM)
    anywhere = pl.BlockSpec(memory_space=pl.ANY)
    members = own.shape[2]
    slots = tiles.shape[0]
    out = jax.ShapeDtypeStruct((out_places, members, LANES), jnp.float32)
    return pl.pallas_call(
        functools.partial(tile_kernel, forward=forward),
        out_shape=[out, out],
        in_specs=[smem] + [anywhere] * 3 + [pl.BlockSpec(memory_space=pltpu.VMEM)] * 2,
        out_specs=[anywhere] * 2,
        scratch_shapes=[
            pltpu.SMEM(rows.shape, jnp.int32),
            pltpu.SMEM(cols.shape, jnp.int32),
            pltpu.VMEM(tiles.shape, tiles.dtype),
            pltpu.VMEM((2 * split_places, 2 * members, LANES), jnp.bfloat16),
            pltpu.VMEM((2 * out_places, members, LANES), jnp.float32),
            pltpu.SemaphoreType.DMA((slots // group_size(slots),)),
            pltpu.SemaphoreType.DMA((4,)),
        ],
        compiler_params=pltpu.CompilerParams(vmem_limit_bytes=TILE_VMEM_BYTES),
        name="forward_tiles" if forward else "backward_tiles",
    )(count, rows, cols, tiles, own, other)


def join_kernel(own_ref, other_ref, out_hbm, total_ref, sent):
    parts = sent.shape[0]
    size = own_ref.shape[0] // parts
    copies = []
    for part in range(parts):
        place = slice(part * size, (part + 1) * size)
        total_ref[place] = own_ref[place] + other_ref[place]
        where = pl.ds(part * size, size)
        copy = pltpu.make_async_copy(total_ref.at[where], out_hbm.at[where], sent.at[part])
        copy.start()
        copies.append(copy)
    for copy in copies:
        copy.wait()


def exchange(slots, axes, groups=None):
    return lax.all_to_all(slots, axes, 0, 0, axis_index_groups=groups, tiled=True)


def swap(array, axis, distance):
    return lax.ppermute(array, axis, [(i, i ^ distance) for i in range(lax.axis_size(axis))])


def shift_lines(array, shift):
    size = lax.axis_size("row")
    return lax.ppermute(array, "row", [(i, (i + 2 * shift) % size) for i in range(size)])


def on_device(
    tile_blocks, tile_rows, tile_cols, tile_count, vectors, hvectors, previous, hprevious
):
    n_row = lax.axis_size("row")
    n_col = lax.axis_size("col")
    everyone = ("row", "col")
    chips = n_col // 2
    core_groups = [[2 * chip + core for chip in range(chips)] for core in (0, 1)]
    members, piece = vectors.shape
    blocks = piece // LANES
    lines = n_row // 2
    order = 3 * members
    tiles = tile_blocks[0, 0]
    row_scale = math.sqrt(piece * n_row * n_col)
    f32 = jnp.float32

    hbm_spec = pl.BlockSpec(memory_space=pl.ANY)
    vmem_spec = pl.BlockSpec(memory_space=pltpu.VMEM)
    params = pltpu.CompilerParams(vmem_limit_bytes=VMEM_BYTES)
    (sums,) = pl.pallas_call(
        stage_kernel,
        out_shape=[jax.ShapeDtypeStruct((n_row * n_col, LANES), f32)],
        in_specs=[hbm_spec, hbm_spec],
        out_specs=[vmem_spec],
        scratch_shapes=[
            pltpu.VMEM((2, members, piece), f32),
            pltpu.SemaphoreType.DMA((2,)),
        ],
        compiler_params=pltpu.CompilerParams(vmem_limit_bytes=FULL_VMEM_BYTES),
        name="stage",
    )(vectors, hvectors)
    basis, images = pl.pallas_call(
        prepare_kernel,
        out_shape=[jax.ShapeDtypeStruct((2, members, piece), f32)] * 2,
        in_specs=[hbm_spec] * 4,
        out_specs=[vmem_spec] * 2,
        scratch_shapes=[pltpu.SemaphoreType.DMA((4,))],
        compiler_params=params,
        name="prepare",
    )(vectors, previous, hvectors, hprevious)
    sums = exchange(sums, everyone)
    sums, basis, images = lax.optimization_barrier((sums, basis, images))
    residual, slots = pl.pallas_call(
        residual_kernel,
        out_shape=[
            jax.ShapeDtypeStruct((members, piece), f32),
            jax.ShapeDtypeStruct((chips, blocks + 2, members, LANES), f32),
        ],
        in_specs=[vmem_spec] * 3,
        out_specs=[vmem_spec, hbm_spec],
        scratch_shapes=[
            pltpu.VMEM((blocks, members, LANES), f32),
            pltpu.VMEM((2, members, LANES), f32),
            pltpu.SemaphoreType.DMA((2 * chips,)),
        ],
        compiler_params=params,
        name="residual",
    )(sums, basis, images)
    pieces = [residual] + [shift_lines(residual, shift) for shift in range(1, lines)]
    (line,) = call(line_kernel, [(lines, blocks, members, LANES)], "line")(*pieces)
    own_range = exchange(slots, "col", core_groups)
    residual, tile_rows, tile_cols = lax.optimization_barrier((residual, tile_rows, tile_cols))
    rows, cols = pl.pallas_call(
        functools.partial(places_kernel, blocks=blocks, gap=2),
        out_shape=[jax.ShapeDtypeStruct(tile_rows.shape, jnp.int32)] * 2,
        compiler_params=params,
        name="places",
    )(tile_rows, tile_cols)
    own_range, line, rows, cols = lax.optimization_barrier((own_range, line, rows, cols))
    far_line = swap(line, "row", 1)
    other_range = swap(own_range, "col", 1)
    col_own, col_other = tile_call(
        tile_count,
        rows,
        cols,
        tiles,
        own_range,
        other_range,
        chips * blocks,
        lines * blocks + 2,
        False,
    )
    col_own, col_other, far_line = lax.optimization_barrier((col_own, col_other, far_line))
    col_received = swap(col_other, "row", 1)
    own_totals, other_totals = tile_call(
        tile_count,
        rows,
        cols,
        tiles,
        line,
        far_line,
        lines * blocks + 2,
        chips * blocks,
        True,
    )
    col_received, own_totals, other_totals = lax.optimization_barrier(
        (col_received, own_totals, other_totals)
    )
    outs = call(halves_kernel, [(blocks + 2, members, LANES)] * lines, "halves")(
        col_own, col_received
    )
    other_totals, *outs = lax.optimization_barrier((swap(other_totals, "col", 1), *outs))
    (totals,) = pl.pallas_call(
        join_kernel,
        out_shape=[jax.ShapeDtypeStruct(own_totals.shape, f32)],
        in_specs=[vmem_spec] * 2,
        out_specs=[hbm_spec],
        scratch_shapes=[pltpu.VMEM(own_totals.shape, f32), pltpu.SemaphoreType.DMA((4,))],
        compiler_params=pltpu.CompilerParams(vmem_limit_bytes=TILE_VMEM_BYTES),
        name="join",
    )(own_totals, other_totals)
    col_parts = exchange(totals.reshape(chips, blocks, members, LANES), "col", core_groups)
    row_parts = [outs[0]] + [shift_lines(outs[shift], shift) for shift in range(1, lines)]
    col_parts, *row_parts = lax.optimization_barrier((col_parts, *row_parts))
    image, slots = pl.pallas_call(
        image_kernel,
        out_shape=[
            jax.ShapeDtypeStruct((members, piece), f32),
            jax.ShapeDtypeStruct((n_row * n_col, 1, members * order), f32),
        ],
        in_specs=[vmem_spec] * 7,
        out_specs=[vmem_spec, hbm_spec],
        scratch_shapes=[
            pltpu.VMEM((n_col, 1, members * order), f32),
            pltpu.SemaphoreType.DMA((n_row,)),
        ],
        compiler_params=params,
        name="image",
    )(col_parts, *row_parts, basis, residual)
    late = exchange(slots, everyone)
    image, *row_parts = lax.optimization_barrier((image, *row_parts))
    inverse, early = call(factor_kernel, [(order, order), (2 * members, order)], "factor")(*row_parts)
    (orthonormal,) = call(
        functools.partial(orthonormal_kernel, row_scale=row_scale), [(order, piece)], "orthonormal"
    )(inverse, basis, residual)
    (orthonormal_image,) = call(
        functools.partial(orthonormal_image_kernel, row_scale=row_scale),
        [(order, piece)],
        "orthonormal_image",
    )(inverse, images, image)
    (projected,) = call(projected_kernel, [(order, order)], "projected")(late, inverse, early)
    return (orthonormal, orthonormal_image, projected)


def solution(mesh):
    in_specs = (
        P("row", "col", None, None, None),
        P("row", "col", None),
        P("row", "col", None),
        P("row", "col"),
        P(None, ("row", "col")),
        P(None, ("row", "col")),
        P(None, ("row", "col")),
        P(None, ("row", "col")),
    )
    out_specs = (P(None, ("row", "col")), P(None, ("row", "col")), P())
    return jax.shard_map(
        on_device, mesh=mesh, in_specs=in_specs, out_specs=out_specs, check_vma=False
    )
```

```python
import functools
import math

import jax
import jax.numpy as jnp
from jax import lax
from jax.experimental import pallas as pl
from jax.experimental.pallas import tpu as pltpu
from jax.sharding import PartitionSpec as P

EPSILON = 1e-06
HIGHEST_PRECISION = lax.Precision.HIGHEST
LANES = 128
VMEM_BYTES = 32 << 20
FULL_VMEM_BYTES = 60 << 20
TILE_VMEM_BYTES = 48<<20
GROUP = 64
NT = (((1,), (1,)), ((), ()))
NN = (((1,), (0,)), ((), ()))


def exact_dot(first, second, dims):
    return lax.dot_general(
        first, second, dims, precision=HIGHEST_PRECISION, preferred_element_type=jnp.float32
    )


def call(kernel, out_shapes, name):
    return pl.pallas_call(
        kernel,
        out_shape=[jax.ShapeDtypeStruct(shape, jnp.float32) for shape in out_shapes],
        compiler_params=pltpu.CompilerParams(vmem_limit_bytes=VMEM_BYTES),
        name=name,
    )


def block(array, index):
    return array[:, index * LANES : (index + 1) * LANES]


def stage_kernel(vectors_hbm, hvectors_hbm, slots_ref, stack_ref, arrived):
    copies = [
        pltpu.make_async_copy(source, stack_ref.at[index], arrived.at[index])
        for index, source in enumerate((vectors_hbm, hvectors_hbm))
    ]
    for copy in copies:
        copy.start()
    for copy in copies:
        copy.wait()
    vectors = stack_ref[0]
    hvectors = stack_ref[1]
    members = vectors.shape[0]
    top = jnp.sum(vectors * hvectors, axis=1, keepdims=True)
    bottom = jnp.sum(vectors * vectors, axis=1, keepdims=True)
    lane = lax.broadcasted_iota(jnp.int32, (members, LANES), 1)
    line = lax.broadcasted_iota(jnp.int32, (members, LANES), 0)
    spread = jnp.where(lane == line, top, 0.0) + jnp.where(lane == line + members, bottom, 0.0)
    sums = jnp.sum(spread, axis=0, keepdims=True)
    slots_ref[...] = jnp.broadcast_to(sums, slots_ref.shape)


def prepare_kernel(
    vectors_hbm, previous_hbm, hvectors_hbm, hprevious_hbm, basis_ref, images_ref, arrived
):
    copies = [
        pltpu.make_async_copy(source, target.at[place], arrived.at[index])
        for index, (source, target, place) in enumerate(
            (
                (vectors_hbm, basis_ref, 0),
                (previous_hbm, basis_ref, 1),
                (hvectors_hbm, images_ref, 0),
                (hprevious_hbm, images_ref, 1),
            )
        )
    ]
    for copy in copies:
        copy.start()
    for copy in copies:
        copy.wait()


def places_kernel(rows_ref, cols_ref, rows_out_ref, cols_out_ref, *, blocks, gap):
    chips = lax.axis_size("col") // 2
    lines = lax.axis_size("row") // 2
    core = lax.rem(lax.axis_index("col"), 2)
    rows = rows_ref[...]
    index, peer = rows % blocks, rows // blocks
    other = jnp.where(peer % 2 == core, 0, 1)
    rows_out_ref[...] = (other * chips + peer // 2) * blocks + index
    half = lax.rem(lax.axis_index("row"), 2)
    cols = cols_ref[...]
    index, peer = cols % blocks, cols // blocks
    other = jnp.where(peer % 2 == half, 0, 1)
    cols_out_ref[...] = (other * lines + peer // 2) * blocks + index + other * gap


def residual_kernel(sums_ref, basis_ref, images_ref, residual_ref, slots_ref):
    members = basis_ref.shape[1]
    sums = jnp.sum(sums_ref[...], axis=0, keepdims=True)
    lane = lax.broadcasted_iota(jnp.int32, (members, LANES), 1)
    line = lax.broadcasted_iota(jnp.int32, (members, LANES), 0)
    top = jnp.sum(jnp.where(lane == line, sums, 0.0), axis=1, keepdims=True)
    bottom = jnp.sum(jnp.where(lane == line + members, sums, 0.0), axis=1, keepdims=True)
    residual = images_ref[0] - (top / (bottom + EPSILON)) * basis_ref[0]
    residual_ref[...] = residual
    blocks = residual.shape[1] // LANES
    for index in range(blocks):
        for slot in range(slots_ref.shape[0]):
            slots_ref[slot, index] = block(residual, index)
    basis = jnp.concatenate([basis_ref[0], residual, basis_ref[1]], axis=0)
    rows = jnp.concatenate([basis, images_ref[0], images_ref[1]], axis=0)
    products = exact_dot(rows, basis, NT)
    gram = products[: 3 * members]
    early = products[3 * members :]
    extra = [
        gram[:members],
        gram[members : 2 * members],
        gram[2 * members :],
        early[:members],
        early[members:],
    ]
    for index, part in enumerate(pack_rows(extra)):
        for slot in range(slots_ref.shape[0]):
            slots_ref[slot, blocks + index] = part


def line_kernel(first_ref, second_ref, third_ref, fourth_ref, line_ref):
    lines, blocks = line_ref.shape[:2]
    here = lax.axis_index("row") // 2
    for shift, piece_ref in enumerate((first_ref, second_ref, third_ref, fourth_ref)):
        place = lax.rem(here + lines - shift, lines)
        for index in range(blocks):
            line_ref[place, index] = piece_ref[:, index * LANES : (index + 1) * LANES]


def halves_kernel(own_ref, received_ref, first_ref, second_ref, third_ref, fourth_ref):
    here = lax.axis_index("row") // 2
    outputs = (first_ref, second_ref, third_ref, fourth_ref)
    lines = len(outputs)
    blocks = (own_ref.shape[0] - first_ref.shape[0]) // (lines - 1)
    for shift, out_ref in enumerate(outputs):
        start = lax.rem(here + shift, lines) * blocks
        for index in range(blocks):
            out_ref[index] = own_ref[start + index] + received_ref[start + index]
        for index in range(out_ref.shape[0] - blocks):
            tail = lines * blocks + index
            out_ref[blocks + index] = own_ref[tail] + received_ref[tail]


def pack_rows(parts):
    first, second, third, fourth, fifth = parts
    members = first.shape[0]
    pieces = [fifth[:, i * members : (i + 1) * members] for i in range(3)]
    zero = jnp.zeros((members, members), jnp.float32)
    return [
        jnp.concatenate([first, second, pieces[0], pieces[1]], axis=1),
        jnp.concatenate([third, fourth, pieces[2], zero], axis=1),
    ]


def unpack_rows(one, two):
    members = one.shape[0]
    wide = 3 * members
    fifth = jnp.concatenate([one[:, 2 * wide :], two[:, 2 * wide : 2 * wide + members]], axis=1)
    return [one[:, :wide], one[:, wide : 2 * wide], two[:, :wide], two[:, wide : 2 * wide], fifth]


def sum_peers(parts_ref, index):
    part = parts_ref[0, index]
    for peer in range(1, parts_ref.shape[0]):
        part = part + parts_ref[peer, index]
    return part


def factor_kernel(first_ref, second_ref, third_ref, fourth_ref, inverse_ref, early_ref):
    parts = [part_ref[first_ref.shape[0] - 2 :] for part_ref in (first_ref, second_ref, third_ref, fourth_ref)]
    sums = parts[0] + parts[1] + parts[2] + parts[3]
    extras = [sums[0], sums[1]]
    members = extras[0].shape[0]
    order = 3 * members
    first, second, third, fourth, fifth = unpack_rows(*extras)
    early_ref[...] = jnp.concatenate([fourth, fifth], axis=0)
    gram = jnp.concatenate([first, second, third], axis=0)
    line = lax.broadcasted_iota(jnp.int32, (order, order), 0)
    lane = lax.broadcasted_iota(jnp.int32, (order, order), 1)
    work = jnp.concatenate([gram, jnp.where(line == lane, 1.0, 0.0)], axis=1)
    rows = lax.broadcasted_iota(jnp.int32, (order, 1), 0)
    for step in range(order):
        pivot = work[step : step + 1, step : step + 1]
        scale = lax.rsqrt(pivot)
        scale = scale * (1.5 - 0.5 * pivot * scale * scale)
        lead = work[step : step + 1, :] * scale
        column = work[:, step : step + 1] * scale
        work = jnp.where(rows == step, lead, jnp.where(rows > step, work - column * lead, work))
    inverse_ref[...] = work[:, order:]


def orthonormal_kernel(inverse_ref, basis_ref, residual_ref, out_ref, *, row_scale):
    rows = jnp.concatenate([basis_ref[0], residual_ref[...], basis_ref[1]], axis=0)
    out_ref[...] = exact_dot(inverse_ref[...] * row_scale, rows, NN)


def orthonormal_image_kernel(inverse_ref, images_ref, image_ref, out_ref, *, row_scale):
    rows = jnp.concatenate([images_ref[0], image_ref[...], images_ref[1]], axis=0)
    out_ref[...] = exact_dot(inverse_ref[...] * row_scale, rows, NN)


def image_kernel(
    col_parts_ref,
    first_ref,
    second_ref,
    third_ref,
    fourth_ref,
    basis_ref,
    residual_ref,
    image_ref,
    slots_ref,
):
    blocks = image_ref.shape[1] // LANES
    for index in range(blocks):
        part = first_ref[index] + second_ref[index] + third_ref[index] + fourth_ref[index]
        image_ref[:, index * LANES : (index + 1) * LANES] = sum_peers(col_parts_ref, index) + part
    basis = jnp.concatenate([basis_ref[0], residual_ref[...], basis_ref[1]], axis=0)
    late = exact_dot(image_ref[...], basis, NT)
    packed = jnp.concatenate([late[row : row + 1] for row in range(late.shape[0])], axis=1)
    slots_ref[...] = jnp.broadcast_to(packed[None], slots_ref.shape)


def projected_kernel(received_ref, inverse_ref, early_ref, projected_ref):
    packed = jnp.sum(received_ref[...], axis=0)
    early = early_ref[...]
    members = early.shape[0] // 2
    wide = early.shape[1]
    late = jnp.concatenate(
        [packed[:, row * wide : (row + 1) * wide] for row in range(members)], axis=0
    )
    mixed_t = jnp.concatenate([early[:members], late, early[members:]], axis=0)
    inverse = inverse_ref[...]
    half_done = exact_dot(inverse, mixed_t, NT)
    projected_ref[...] = exact_dot(half_done, inverse, NT)


def split_blocks(x_ref, split_ref, start, per_peer):
    def split(peer, carry):
        for index in range(per_peer):
            value = x_ref[peer, index]
            high = value.astype(jnp.bfloat16)
            low = (value - high.astype(jnp.float32)).astype(jnp.bfloat16)
            split_ref[start + peer * per_peer + index] = jnp.concatenate([high, low], axis=0)
        return carry

    lax.fori_loop(0, x_ref.shape[0], split, 0)


def group_size(slots):
    return math.gcd(slots, GROUP)


def group_count(live, slots):
    return (jnp.minimum(live, slots) + group_size(slots) - 1) // group_size(slots)


def group_copy(tiles_hbm, tiles_ref, arrived, counter):
    size = group_size(tiles_ref.shape[0])
    part = pl.ds(counter * size, size)
    return pltpu.make_async_copy(tiles_hbm.at[part], tiles_ref.at[part], arrived.at[counter])


def tile_kernel(
    count_ref,
    rows_hbm,
    cols_hbm,
    tiles_hbm,
    own_ref,
    other_ref,
    own_out_hbm,
    other_out_hbm,
    rows_ref,
    cols_ref,
    tiles_ref,
    split_ref,
    totals_ref,
    arrived,
    moved,
    *,
    forward,
):
    slots = tiles_ref.shape[0]
    live = count_ref[0, 0]
    rows_copy = pltpu.make_async_copy(rows_hbm, rows_ref, moved.at[2])
    cols_copy = pltpu.make_async_copy(cols_hbm, cols_ref, moved.at[3])
    for copy in (rows_copy, cols_copy):
        copy.start()

    def start(counter, carry):
        group_copy(tiles_hbm, tiles_ref, arrived, counter).start()
        return carry

    lax.fori_loop(0, group_count(live, slots), start, 0)
    totals_ref[...] = jnp.zeros_like(totals_ref)
    peers = own_ref.shape[0]
    split_half = split_ref.shape[0] // 2
    blocks = split_half // peers if forward else own_ref.shape[1] - 2
    half = totals_ref.shape[0] // 2
    split_blocks(own_ref, split_ref, 0, blocks)
    split_blocks(other_ref, split_ref, split_half, blocks)
    if not forward:
        extra = own_ref.shape[1] - blocks
        for index in range(extra):
            part = sum_peers(own_ref, blocks + index) + sum_peers(other_ref, blocks + index)
            totals_ref[half - extra + index] = part
            totals_ref[2 * half - extra + index] = part
    rows_copy.wait()
    cols_copy.wait()
    unroll = group_size(slots)
    members = split_ref.shape[1] // 2
    source_ref, target_ref = (cols_ref, rows_ref) if forward else (rows_ref, cols_ref)

    def group(counter, carry):
        group_copy(tiles_hbm, tiles_ref, arrived, counter).wait()
        base = counter * unroll
        products = []
        for offset in range(unroll):
            slot = base + offset
            product = lax.dot_general(
                split_ref[source_ref[0, 0, slot]],
                tiles_ref[slot],
                NT if forward else NN,
                preferred_element_type=jnp.float32,
            )
            product = product[:members] + product[members:]
            products.append(jnp.where(slot < live, product, 0.0))
        for offset in range(unroll):
            target = target_ref[0, 0, base + offset]
            totals_ref[target] = totals_ref[target] + products[offset]
        return carry

    lax.fori_loop(0, group_count(live, slots), group, 0)
    outs = [
        pltpu.make_async_copy(totals_ref.at[pl.ds(start, half)], out, moved.at[index])
        for index, (start, out) in enumerate(((0, own_out_hbm), (half, other_out_hbm)))
    ]
    for copy in outs:
        copy.start()
    for copy in outs:
        copy.wait()


def tile_call(count, rows, cols, tiles, own, other, split_places, out_places, forward):
    smem = pl.BlockSpec(memory_space=pltpu.SMEM)
    anywhere = pl.BlockSpec(memory_space=pl.ANY)
    members = own.shape[2]
    slots = tiles.shape[0]
    out = jax.ShapeDtypeStruct((out_places, members, LANES), jnp.float32)
    return pl.pallas_call(
        functools.partial(tile_kernel, forward=forward),
        out_shape=[out, out],
        in_specs=[smem] + [anywhere] * 3 + [pl.BlockSpec(memory_space=pltpu.VMEM)] * 2,
        out_specs=[anywhere] * 2,
        scratch_shapes=[
            pltpu.SMEM(rows.shape, jnp.int32),
            pltpu.SMEM(cols.shape, jnp.int32),
            pltpu.VMEM(tiles.shape, tiles.dtype),
            pltpu.VMEM((2 * split_places, 2 * members, LANES), jnp.bfloat16),
            pltpu.VMEM((2 * out_places, members, LANES), jnp.float32),
            pltpu.SemaphoreType.DMA((slots // group_size(slots),)),
            pltpu.SemaphoreType.DMA((4,)),
        ],
        compiler_params=pltpu.CompilerParams(vmem_limit_bytes=TILE_VMEM_BYTES),
        name="forward_tiles" if forward else "backward_tiles",
    )(count, rows, cols, tiles, own, other)


def join_kernel(own_ref, other_ref, out_ref):
    out_ref[...] = own_ref[...] + other_ref[...]


def exchange(slots, axes, groups=None):
    return lax.all_to_all(slots, axes, 0, 0, axis_index_groups=groups, tiled=True)


def swap(array, axis, distance):
    return lax.ppermute(array, axis, [(i, i ^ distance) for i in range(lax.axis_size(axis))])


def shift_lines(array, shift):
    size = lax.axis_size("row")
    return lax.ppermute(array, "row", [(i, (i + 2 * shift) % size) for i in range(size)])


def on_device(
    tile_blocks, tile_rows, tile_cols, tile_count, vectors, hvectors, previous, hprevious
):
    n_row = lax.axis_size("row")
    n_col = lax.axis_size("col")
    everyone = ("row", "col")
    chips = n_col // 2
    core_groups = [[2 * chip + core for chip in range(chips)] for core in (0, 1)]
    members, piece = vectors.shape
    blocks = piece // LANES
    lines = n_row // 2
    order = 3 * members
    tiles = tile_blocks[0, 0]
    row_scale = math.sqrt(piece * n_row * n_col)
    f32 = jnp.float32

    hbm_spec = pl.BlockSpec(memory_space=pl.ANY)
    vmem_spec = pl.BlockSpec(memory_space=pltpu.VMEM)
    params = pltpu.CompilerParams(vmem_limit_bytes=VMEM_BYTES)
    (sums,) = pl.pallas_call(
        stage_kernel,
        out_shape=[jax.ShapeDtypeStruct((n_row * n_col, LANES), f32)],
        in_specs=[hbm_spec, hbm_spec],
        out_specs=[vmem_spec],
        scratch_shapes=[
            pltpu.VMEM((2, members, piece), f32),
            pltpu.SemaphoreType.DMA((2,)),
        ],
        compiler_params=pltpu.CompilerParams(vmem_limit_bytes=FULL_VMEM_BYTES),
        name="stage",
    )(vectors, hvectors)
    basis, images = pl.pallas_call(
        prepare_kernel,
        out_shape=[jax.ShapeDtypeStruct((2, members, piece), f32)] * 2,
        in_specs=[hbm_spec] * 4,
        out_specs=[vmem_spec] * 2,
        scratch_shapes=[pltpu.SemaphoreType.DMA((4,))],
        compiler_params=params,
        name="prepare",
    )(vectors, previous, hvectors, hprevious)
    sums = exchange(sums, everyone)
    sums, basis, images = lax.optimization_barrier((sums, basis, images))
    residual, slots = call(
        residual_kernel, [(members, piece), (chips, blocks + 2, members, LANES)], "residual"
    )(sums, basis, images)
    pieces = [residual] + [shift_lines(residual, shift) for shift in range(1, lines)]
    (line,) = call(line_kernel, [(lines, blocks, members, LANES)], "line")(*pieces)
    own_range = exchange(slots, "col", core_groups)
    residual, tile_rows, tile_cols = lax.optimization_barrier((residual, tile_rows, tile_cols))
    rows, cols = pl.pallas_call(
        functools.partial(places_kernel, blocks=blocks, gap=2),
        out_shape=[jax.ShapeDtypeStruct(tile_rows.shape, jnp.int32)] * 2,
        compiler_params=params,
        name="places",
    )(tile_rows, tile_cols)
    own_range, line, rows, cols = lax.optimization_barrier((own_range, line, rows, cols))
    far_line = swap(line, "row", 1)
    other_range = swap(own_range, "col", 1)
    col_own, col_other = tile_call(
        tile_count,
        rows,
        cols,
        tiles,
        own_range,
        other_range,
        chips * blocks,
        lines * blocks + 2,
        False,
    )
    col_own, col_other, far_line = lax.optimization_barrier((col_own, col_other, far_line))
    col_received = swap(col_other, "row", 1)
    own_totals, other_totals = tile_call(
        tile_count,
        rows,
        cols,
        tiles,
        line,
        far_line,
        lines * blocks + 2,
        chips * blocks,
        True,
    )
    col_received, own_totals, other_totals = lax.optimization_barrier(
        (col_received, own_totals, other_totals)
    )
    outs = call(halves_kernel, [(blocks + 2, members, LANES)] * lines, "halves")(
        col_own, col_received
    )
    other_totals, *outs = lax.optimization_barrier((swap(other_totals, "col", 1), *outs))
    (totals,) = pl.pallas_call(
        join_kernel,
        out_shape=[jax.ShapeDtypeStruct(own_totals.shape, f32)],
        compiler_params=pltpu.CompilerParams(vmem_limit_bytes=TILE_VMEM_BYTES),
        name="join",
    )(own_totals, other_totals)
    col_parts = exchange(totals.reshape(chips, blocks, members, LANES), "col", core_groups)
    row_parts = [outs[0]] + [shift_lines(outs[shift], shift) for shift in range(1, lines)]
    col_parts, *row_parts = lax.optimization_barrier((col_parts, *row_parts))
    image, slots = call(
        image_kernel, [(members, piece), (n_row * n_col, 1, members * order)], "image"
    )(col_parts, *row_parts, basis, residual)
    late = exchange(slots, everyone)
    image, *row_parts = lax.optimization_barrier((image, *row_parts))
    inverse, early = call(factor_kernel, [(order, order), (2 * members, order)], "factor")(*row_parts)
    (orthonormal,) = call(
        functools.partial(orthonormal_kernel, row_scale=row_scale), [(order, piece)], "orthonormal"
    )(inverse, basis, residual)
    (orthonormal_image,) = call(
        functools.partial(orthonormal_image_kernel, row_scale=row_scale),
        [(order, piece)],
        "orthonormal_image",
    )(inverse, images, image)
    (projected,) = call(projected_kernel, [(order, order)], "projected")(late, inverse, early)
    return (orthonormal, orthonormal_image, projected)


def solution(mesh):
    in_specs = (
        P("row", "col", None, None, None),
        P("row", "col", None),
        P("row", "col", None),
        P("row", "col"),
        P(None, ("row", "col")),
        P(None, ("row", "col")),
        P(None, ("row", "col")),
        P(None, ("row", "col")),
    )
    out_specs = (P(None, ("row", "col")), P(None, ("row", "col")), P())
    return jax.shard_map(
        on_device, mesh=mesh, in_specs=in_specs, out_specs=out_specs, check_vma=False
    )
```

```python
import functools
import math

import jax
import jax.numpy as jnp
from jax import lax
from jax.experimental import pallas as pl
from jax.experimental.pallas import tpu as pltpu
from jax.sharding import PartitionSpec as P

EPSILON = 1e-06
HIGHEST_PRECISION = lax.Precision.HIGHEST
LANES = 128
VMEM_BYTES = 32 << 20
FULL_VMEM_BYTES = 60 << 20
TILE_VMEM_BYTES = 48<<20
GROUP = 64
NT = (((1,), (1,)), ((), ()))
NN = (((1,), (0,)), ((), ()))


def exact_dot(first, second, dims):
    return lax.dot_general(
        first, second, dims, precision=HIGHEST_PRECISION, preferred_element_type=jnp.float32
    )


def call(kernel, out_shapes, name):
    return pl.pallas_call(
        kernel,
        out_shape=[jax.ShapeDtypeStruct(shape, jnp.float32) for shape in out_shapes],
        compiler_params=pltpu.CompilerParams(vmem_limit_bytes=VMEM_BYTES),
        name=name,
    )


def block(array, index):
    return array[:, index * LANES : (index + 1) * LANES]


def stage_kernel(vectors_hbm, hvectors_hbm, slots_ref, stack_ref, arrived):
    copies = [
        pltpu.make_async_copy(source, stack_ref.at[index], arrived.at[index])
        for index, source in enumerate((vectors_hbm, hvectors_hbm))
    ]
    for copy in copies:
        copy.start()
    for copy in copies:
        copy.wait()
    vectors = stack_ref[0]
    hvectors = stack_ref[1]
    members = vectors.shape[0]
    top = jnp.sum(vectors * hvectors, axis=1, keepdims=True)
    bottom = jnp.sum(vectors * vectors, axis=1, keepdims=True)
    lane = lax.broadcasted_iota(jnp.int32, (members, LANES), 1)
    line = lax.broadcasted_iota(jnp.int32, (members, LANES), 0)
    spread = jnp.where(lane == line, top, 0.0) + jnp.where(lane == line + members, bottom, 0.0)
    sums = jnp.sum(spread, axis=0, keepdims=True)
    slots_ref[...] = jnp.broadcast_to(sums, slots_ref.shape)


def prepare_kernel(
    vectors_hbm, previous_hbm, hvectors_hbm, hprevious_hbm, basis_ref, images_ref, arrived
):
    copies = [
        pltpu.make_async_copy(source, target.at[place], arrived.at[index])
        for index, (source, target, place) in enumerate(
            (
                (vectors_hbm, basis_ref, 0),
                (previous_hbm, basis_ref, 1),
                (hvectors_hbm, images_ref, 0),
                (hprevious_hbm, images_ref, 1),
            )
        )
    ]
    for copy in copies:
        copy.start()
    for copy in copies:
        copy.wait()


def places_kernel(rows_ref, cols_ref, rows_out_ref, cols_out_ref, *, blocks, gap):
    chips = lax.axis_size("col") // 2
    lines = lax.axis_size("row") // 2
    core = lax.rem(lax.axis_index("col"), 2)
    rows = rows_ref[...]
    index, peer = rows % blocks, rows // blocks
    other = jnp.where(peer % 2 == core, 0, 1)
    rows_out_ref[...] = (other * chips + peer // 2) * blocks + index
    half = lax.rem(lax.axis_index("row"), 2)
    cols = cols_ref[...]
    index, peer = cols % blocks, cols // blocks
    other = jnp.where(peer % 2 == half, 0, 1)
    cols_out_ref[...] = (other * lines + peer // 2) * blocks + index + other * gap


def residual_kernel(sums_ref, basis_ref, images_ref, residual_ref, slots_ref):
    members = basis_ref.shape[1]
    sums = jnp.sum(sums_ref[...], axis=0, keepdims=True)
    lane = lax.broadcasted_iota(jnp.int32, (members, LANES), 1)
    line = lax.broadcasted_iota(jnp.int32, (members, LANES), 0)
    top = jnp.sum(jnp.where(lane == line, sums, 0.0), axis=1, keepdims=True)
    bottom = jnp.sum(jnp.where(lane == line + members, sums, 0.0), axis=1, keepdims=True)
    residual = images_ref[0] - (top / (bottom + EPSILON)) * basis_ref[0]
    residual_ref[...] = residual
    blocks = residual.shape[1] // LANES
    for index in range(blocks):
        for slot in range(slots_ref.shape[0]):
            slots_ref[slot, index] = block(residual, index)
    basis = jnp.concatenate([basis_ref[0], residual, basis_ref[1]], axis=0)
    rows = jnp.concatenate([basis, images_ref[0], images_ref[1]], axis=0)
    products = exact_dot(rows, basis, NT)
    gram = products[: 3 * members]
    early = products[3 * members :]
    extra = [
        gram[:members],
        gram[members : 2 * members],
        gram[2 * members :],
        early[:members],
        early[members:],
    ]
    for index, part in enumerate(pack_rows(extra)):
        for slot in range(slots_ref.shape[0]):
            slots_ref[slot, blocks + index] = part


def line_kernel(first_ref, second_ref, third_ref, fourth_ref, line_ref):
    lines, blocks = line_ref.shape[:2]
    here = lax.axis_index("row") // 2
    for shift, piece_ref in enumerate((first_ref, second_ref, third_ref, fourth_ref)):
        place = lax.rem(here + lines - shift, lines)
        for index in range(blocks):
            line_ref[place, index] = piece_ref[:, index * LANES : (index + 1) * LANES]


def halves_kernel(own_ref, received_ref, first_ref, second_ref, third_ref, fourth_ref):
    here = lax.axis_index("row") // 2
    outputs = (first_ref, second_ref, third_ref, fourth_ref)
    lines = len(outputs)
    blocks = (own_ref.shape[0] - first_ref.shape[0]) // (lines - 1)
    for shift, out_ref in enumerate(outputs):
        start = lax.rem(here + shift, lines) * blocks
        for index in range(blocks):
            out_ref[index] = own_ref[start + index] + received_ref[start + index]
        for index in range(out_ref.shape[0] - blocks):
            tail = lines * blocks + index
            out_ref[blocks + index] = own_ref[tail] + received_ref[tail]


def pack_rows(parts):
    first, second, third, fourth, fifth = parts
    members = first.shape[0]
    pieces = [fifth[:, i * members : (i + 1) * members] for i in range(3)]
    zero = jnp.zeros((members, members), jnp.float32)
    return [
        jnp.concatenate([first, second, pieces[0], pieces[1]], axis=1),
        jnp.concatenate([third, fourth, pieces[2], zero], axis=1),
    ]


def unpack_rows(one, two):
    members = one.shape[0]
    wide = 3 * members
    fifth = jnp.concatenate([one[:, 2 * wide :], two[:, 2 * wide : 2 * wide + members]], axis=1)
    return [one[:, :wide], one[:, wide : 2 * wide], two[:, :wide], two[:, wide : 2 * wide], fifth]


def sum_peers(parts_ref, index):
    part = parts_ref[0, index]
    for peer in range(1, parts_ref.shape[0]):
        part = part + parts_ref[peer, index]
    return part


def factor_kernel(first_ref, second_ref, third_ref, fourth_ref, inverse_ref, early_ref):
    parts = [part_ref[first_ref.shape[0] - 2 :] for part_ref in (first_ref, second_ref, third_ref, fourth_ref)]
    sums = parts[0] + parts[1] + parts[2] + parts[3]
    extras = [sums[0], sums[1]]
    members = extras[0].shape[0]
    order = 3 * members
    first, second, third, fourth, fifth = unpack_rows(*extras)
    early_ref[...] = jnp.concatenate([fourth, fifth], axis=0)
    gram = jnp.concatenate([first, second, third], axis=0)
    line = lax.broadcasted_iota(jnp.int32, (order, order), 0)
    lane = lax.broadcasted_iota(jnp.int32, (order, order), 1)
    work = jnp.concatenate([gram, jnp.where(line == lane, 1.0, 0.0)], axis=1)
    rows = lax.broadcasted_iota(jnp.int32, (order, 1), 0)
    for step in range(order):
        pivot = work[step : step + 1, step : step + 1]
        scale = lax.rsqrt(pivot)
        scale = scale * (1.5 - 0.5 * pivot * scale * scale)
        lead = work[step : step + 1, :] * scale
        column = work[:, step : step + 1] * scale
        work = jnp.where(rows == step, lead, jnp.where(rows > step, work - column * lead, work))
    inverse_ref[...] = work[:, order:]


def orthonormal_kernel(inverse_ref, basis_ref, residual_ref, out_ref, *, row_scale):
    rows = jnp.concatenate([basis_ref[0], residual_ref[...], basis_ref[1]], axis=0)
    out_ref[...] = exact_dot(inverse_ref[...] * row_scale, rows, NN)


def orthonormal_image_kernel(inverse_ref, images_ref, image_ref, out_ref, *, row_scale):
    rows = jnp.concatenate([images_ref[0], image_ref[...], images_ref[1]], axis=0)
    out_ref[...] = exact_dot(inverse_ref[...] * row_scale, rows, NN)


def image_kernel(
    col_parts_ref,
    first_ref,
    second_ref,
    third_ref,
    fourth_ref,
    basis_ref,
    residual_ref,
    image_ref,
    slots_ref,
):
    blocks = image_ref.shape[1] // LANES
    for index in range(blocks):
        part = first_ref[index] + second_ref[index] + third_ref[index] + fourth_ref[index]
        image_ref[:, index * LANES : (index + 1) * LANES] = sum_peers(col_parts_ref, index) + part
    basis = jnp.concatenate([basis_ref[0], residual_ref[...], basis_ref[1]], axis=0)
    late = exact_dot(image_ref[...], basis, NT)
    packed = jnp.concatenate([late[row : row + 1] for row in range(late.shape[0])], axis=1)
    slots_ref[...] = jnp.broadcast_to(packed[None], slots_ref.shape)


def projected_kernel(received_ref, inverse_ref, early_ref, projected_ref):
    packed = jnp.sum(received_ref[...], axis=0)
    early = early_ref[...]
    members = early.shape[0] // 2
    wide = early.shape[1]
    late = jnp.concatenate(
        [packed[:, row * wide : (row + 1) * wide] for row in range(members)], axis=0
    )
    mixed_t = jnp.concatenate([early[:members], late, early[members:]], axis=0)
    inverse = inverse_ref[...]
    half_done = exact_dot(inverse, mixed_t, NT)
    projected_ref[...] = exact_dot(half_done, inverse, NT)


def split_blocks(x_ref, split_ref, start, per_peer):
    def split(peer, carry):
        for index in range(per_peer):
            value = x_ref[peer, index]
            high = value.astype(jnp.bfloat16)
            low = (value - high.astype(jnp.float32)).astype(jnp.bfloat16)
            split_ref[start + peer * per_peer + index] = jnp.concatenate([high, low], axis=0)
        return carry

    lax.fori_loop(0, x_ref.shape[0], split, 0)


def group_size(slots):
    return math.gcd(slots, GROUP)


def group_count(live, slots):
    return (jnp.minimum(live, slots) + group_size(slots) - 1) // group_size(slots)


def group_copy(tiles_hbm, tiles_ref, arrived, counter):
    size = group_size(tiles_ref.shape[0])
    part = pl.ds(counter * size, size)
    return pltpu.make_async_copy(tiles_hbm.at[part], tiles_ref.at[part], arrived.at[counter])


def tile_kernel(
    count_ref,
    rows_hbm,
    cols_hbm,
    tiles_hbm,
    own_ref,
    other_ref,
    own_out_hbm,
    other_out_hbm,
    rows_ref,
    cols_ref,
    tiles_ref,
    split_ref,
    totals_ref,
    arrived,
    moved,
    *,
    forward,
):
    slots = tiles_ref.shape[0]
    live = count_ref[0, 0]
    rows_copy = pltpu.make_async_copy(rows_hbm, rows_ref, moved.at[2])
    cols_copy = pltpu.make_async_copy(cols_hbm, cols_ref, moved.at[3])
    for copy in (rows_copy, cols_copy):
        copy.start()

    def start(counter, carry):
        group_copy(tiles_hbm, tiles_ref, arrived, counter).start()
        return carry

    lax.fori_loop(0, group_count(live, slots), start, 0)
    totals_ref[...] = jnp.zeros_like(totals_ref)
    peers = own_ref.shape[0]
    split_half = split_ref.shape[0] // 2
    blocks = split_half // peers if forward else own_ref.shape[1] - 2
    half = totals_ref.shape[0] // 2
    split_blocks(own_ref, split_ref, 0, blocks)
    split_blocks(other_ref, split_ref, split_half, blocks)
    if not forward:
        extra = own_ref.shape[1] - blocks
        for index in range(extra):
            part = sum_peers(own_ref, blocks + index) + sum_peers(other_ref, blocks + index)
            totals_ref[half - extra + index] = part
            totals_ref[2 * half - extra + index] = part
    rows_copy.wait()
    cols_copy.wait()
    unroll = group_size(slots)
    members = split_ref.shape[1] // 2
    source_ref, target_ref = (cols_ref, rows_ref) if forward else (rows_ref, cols_ref)

    def group(counter, carry):
        group_copy(tiles_hbm, tiles_ref, arrived, counter).wait()
        base = counter * unroll
        products = []
        for offset in range(unroll):
            slot = base + offset
            product = lax.dot_general(
                split_ref[source_ref[0, 0, slot]],
                tiles_ref[slot],
                NT if forward else NN,
                preferred_element_type=jnp.float32,
            )
            product = product[:members] + product[members:]
            products.append(jnp.where(slot < live, product, 0.0))
        for offset in range(unroll):
            target = target_ref[0, 0, base + offset]
            totals_ref[target] = totals_ref[target] + products[offset]
        return carry

    lax.fori_loop(0, group_count(live, slots), group, 0)
    outs = [
        pltpu.make_async_copy(totals_ref.at[pl.ds(start, half)], out, moved.at[index])
        for index, (start, out) in enumerate(((0, own_out_hbm), (half, other_out_hbm)))
    ]
    for copy in outs:
        copy.start()
    for copy in outs:
        copy.wait()


def tile_call(count, rows, cols, tiles, own, other, split_places, out_places, forward):
    smem = pl.BlockSpec(memory_space=pltpu.SMEM)
    anywhere = pl.BlockSpec(memory_space=pl.ANY)
    members = own.shape[2]
    slots = tiles.shape[0]
    out = jax.ShapeDtypeStruct((out_places, members, LANES), jnp.float32)
    return pl.pallas_call(
        functools.partial(tile_kernel, forward=forward),
        out_shape=[out, out],
        in_specs=[smem] + [anywhere] * 3 + [pl.BlockSpec(memory_space=pltpu.VMEM)] * 2,
        out_specs=[anywhere] * 2,
        scratch_shapes=[
            pltpu.SMEM(rows.shape, jnp.int32),
            pltpu.SMEM(cols.shape, jnp.int32),
            pltpu.VMEM(tiles.shape, tiles.dtype),
            pltpu.VMEM((2 * split_places, 2 * members, LANES), jnp.bfloat16),
            pltpu.VMEM((2 * out_places, members, LANES), jnp.float32),
            pltpu.SemaphoreType.DMA((slots // group_size(slots),)),
            pltpu.SemaphoreType.DMA((4,)),
        ],
        compiler_params=pltpu.CompilerParams(vmem_limit_bytes=TILE_VMEM_BYTES),
        name="forward_tiles" if forward else "backward_tiles",
    )(count, rows, cols, tiles, own, other)


def join_kernel(own_ref, other_ref, out_ref):
    out_ref[...] = own_ref[...] + other_ref[...]


def exchange(slots, axes, groups=None):
    return lax.all_to_all(slots, axes, 0, 0, axis_index_groups=groups, tiled=True)


def swap(array, axis, distance):
    return lax.ppermute(array, axis, [(i, i ^ distance) for i in range(lax.axis_size(axis))])


def shift_lines(array, shift):
    size = lax.axis_size("row")
    return lax.ppermute(array, "row", [(i, (i + 2 * shift) % size) for i in range(size)])


def on_device(
    tile_blocks, tile_rows, tile_cols, tile_count, vectors, hvectors, previous, hprevious
):
    n_row = lax.axis_size("row")
    n_col = lax.axis_size("col")
    everyone = ("row", "col")
    chips = n_col // 2
    core_groups = [[2 * chip + core for chip in range(chips)] for core in (0, 1)]
    members, piece = vectors.shape
    blocks = piece // LANES
    lines = n_row // 2
    order = 3 * members
    tiles = tile_blocks[0, 0]
    row_scale = math.sqrt(piece * n_row * n_col)
    f32 = jnp.float32

    hbm_spec = pl.BlockSpec(memory_space=pl.ANY)
    vmem_spec = pl.BlockSpec(memory_space=pltpu.VMEM)
    params = pltpu.CompilerParams(vmem_limit_bytes=VMEM_BYTES)
    (sums,) = pl.pallas_call(
        stage_kernel,
        out_shape=[jax.ShapeDtypeStruct((n_row * n_col, LANES), f32)],
        in_specs=[hbm_spec, hbm_spec],
        out_specs=[vmem_spec],
        scratch_shapes=[
            pltpu.VMEM((2, members, piece), f32),
            pltpu.SemaphoreType.DMA((2,)),
        ],
        compiler_params=pltpu.CompilerParams(vmem_limit_bytes=FULL_VMEM_BYTES),
        name="stage",
    )(vectors, hvectors)
    basis, images = pl.pallas_call(
        prepare_kernel,
        out_shape=[jax.ShapeDtypeStruct((2, members, piece), f32)] * 2,
        in_specs=[hbm_spec] * 4,
        out_specs=[vmem_spec] * 2,
        scratch_shapes=[pltpu.SemaphoreType.DMA((4,))],
        compiler_params=params,
        name="prepare",
    )(vectors, previous, hvectors, hprevious)
    sums = exchange(sums, everyone)
    sums, basis, images = lax.optimization_barrier((sums, basis, images))
    residual, slots = call(
        residual_kernel, [(members, piece), (chips, blocks + 2, members, LANES)], "residual"
    )(sums, basis, images)
    pieces = [residual] + [shift_lines(residual, shift) for shift in range(1, lines)]
    (line,) = call(line_kernel, [(lines, blocks, members, LANES)], "line")(*pieces)
    own_range = exchange(slots, "col", core_groups)
    residual, tile_rows, tile_cols = lax.optimization_barrier((residual, tile_rows, tile_cols))
    rows, cols = pl.pallas_call(
        functools.partial(places_kernel, blocks=blocks, gap=2),
        out_shape=[jax.ShapeDtypeStruct(tile_rows.shape, jnp.int32)] * 2,
        compiler_params=params,
        name="places",
    )(tile_rows, tile_cols)
    own_range, line, rows, cols = lax.optimization_barrier((own_range, line, rows, cols))
    far_line = swap(line, "row", 1)
    other_range = swap(own_range, "col", 1)
    col_own, col_other = tile_call(
        tile_count,
        rows,
        cols,
        tiles,
        own_range,
        other_range,
        chips * blocks,
        lines * blocks + 2,
        False,
    )
    col_own, col_other, far_line = lax.optimization_barrier((col_own, col_other, far_line))
    col_received = swap(col_other, "row", 1)
    own_totals, other_totals = tile_call(
        tile_count,
        rows,
        cols,
        tiles,
        line,
        far_line,
        lines * blocks + 2,
        chips * blocks,
        True,
    )
    col_received, own_totals, other_totals = lax.optimization_barrier(
        (col_received, own_totals, other_totals)
    )
    outs = call(halves_kernel, [(blocks + 2, members, LANES)] * lines, "halves")(
        col_own, col_received
    )
    other_totals, *outs = lax.optimization_barrier((swap(other_totals, "col", 1), *outs))
    (totals,) = pl.pallas_call(
        join_kernel,
        out_shape=[jax.ShapeDtypeStruct(own_totals.shape, f32)],
        compiler_params=pltpu.CompilerParams(vmem_limit_bytes=TILE_VMEM_BYTES),
        name="join",
    )(own_totals, other_totals)
    col_parts = exchange(totals.reshape(chips, blocks, members, LANES), "col", core_groups)
    farthest_first = sorted(range(1, lines), key=lambda shift: -min(shift, lines - shift))
    row_parts = [outs[0]] + [shift_lines(outs[shift], shift) for shift in farthest_first]
    col_parts, *row_parts = lax.optimization_barrier((col_parts, *row_parts))
    image, slots = call(
        image_kernel, [(members, piece), (n_row * n_col, 1, members * order)], "image"
    )(col_parts, *row_parts, basis, residual)
    late = exchange(slots, everyone)
    image, *row_parts = lax.optimization_barrier((image, *row_parts))
    inverse, early = call(factor_kernel, [(order, order), (2 * members, order)], "factor")(*row_parts)
    (orthonormal,) = call(
        functools.partial(orthonormal_kernel, row_scale=row_scale), [(order, piece)], "orthonormal"
    )(inverse, basis, residual)
    (orthonormal_image,) = call(
        functools.partial(orthonormal_image_kernel, row_scale=row_scale),
        [(order, piece)],
        "orthonormal_image",
    )(inverse, images, image)
    (projected,) = call(projected_kernel, [(order, order)], "projected")(late, inverse, early)
    return (orthonormal, orthonormal_image, projected)


def solution(mesh):
    in_specs = (
        P("row", "col", None, None, None),
        P("row", "col", None),
        P("row", "col", None),
        P("row", "col"),
        P(None, ("row", "col")),
        P(None, ("row", "col")),
        P(None, ("row", "col")),
        P(None, ("row", "col")),
    )
    out_specs = (P(None, ("row", "col")), P(None, ("row", "col")), P())
    return jax.shard_map(
        on_device, mesh=mesh, in_specs=in_specs, out_specs=out_specs, check_vma=False
    )
```
